128 devices in a mesh: seq: 32 (over z, y, core), head: 4 (over x).
Axes of the slice: x: 4, y: 4, z: 4, core: 2. Of those that a mesh axis runs over, the one named last changes fastest.
Arguments:
- queries: bfloat16 [16384, 4096], P('seq', 'head'), may hold values from -4 to 4
- key_vectors: bfloat16 [16384, 4096], P('seq', 'head'), may hold values from -6 to 6
- output_grad: bfloat16 [16384, 4096], P('seq', 'head'), may hold values from -6 to 6
- value_weight: bfloat16 [6144, 4096], P('seq', 'head'), may hold values from -0.078125 to 0.078125
- decay_rate: float32 [32], P('head'), may hold values from 1.2207031e-05 to 0.035
- doc_lengths: int32 [4], replicated, may hold values from 1 to 8192, 16384 in all
- owner_block: int32 [16384, 1], P('seq'), may hold values from 0 to 127; in each aligned block of 128 rows (0 to 127, 128 to 255, ...) at most 2 rows name the same one
- row_offset: int32 [16384], P('seq'), may hold values from 0 to 781
Outputs:
- row_grads: bfloat16 [128, 128, 2, 6144], P(('seq', 'head'))
The draws below stay inside these ranges and needn't reach their ends.
Inputs may be any that keep to these rules, and one draw needn't show every extreme that they name: `doc_lengths`: the longest document has exactly 8192 positions. `owner_block`: in each aligned block of 128 positions no owner is named more than 2 times; some block names some owner exactly 2 times.
All inputs are finite; a program needn't handle non-finite values.
Results may differ from the reference program's by a relative error of at most 0.0071.
Values may be sent and summed in bfloat16 or wider, within the bound.
No kernel may reach another device: no remote copies, remote signals or barrier semaphores. Data moves between devices by JAX's collectives and lax.ppermute only.
A program may use at most 128 MiB of HBM per device.

```python
import math
import jax
import jax.numpy as jnp
import numpy as np
from jax import lax

D = 6144
HEADS = 32
HEAD_DIM = 128
DOCS = 4
TOK_DEV = 512
TOKENS = 16384
ROWS_BLK = 128
VROWS = 782
CAP = 2
N_HEAD = 4
DEVICES = 128


def draw_decay_rate(key, part):
    key_pick, key_slow, key_fast = jax.random.split(key, 3)
    slow_rate = jnp.exp(jnp.log(0.2 / TOKENS) + jax.random.uniform(key_slow, (HEADS,), jnp.float32) * jnp.log(10.0))
    fast_rate = jnp.exp(jnp.log(0.02) + jax.random.uniform(key_fast, (HEADS,), jnp.float32) * jnp.log(1.75))
    slow_share = 0.5
    slow_pick = jax.random.uniform(key_pick, (HEADS,), jnp.float32) < slow_share
    return jnp.where(slow_pick, slow_rate, fast_rate).astype(jnp.float32)


def touch_ends(entries, stream_key, least, top_value):
    dims = entries.shape
    spot = [jax.random.randint(jax.random.fold_in(stream_key, axis), (), 0, dims[axis]) for axis in range(len(dims))]
    entries = entries.at[tuple(spot)].set(least)
    longest = dims.index(max(dims))
    spot[longest] = (spot[longest] + 1) % dims[longest]
    return entries.at[tuple(spot)].set(top_value)


def block_levels(rng, shape, cuts, least, largest):
    loudness, own = 1.0, jax.random.fold_in(rng, 6)
    for position, shards_of in cuts:
        steps = jnp.exp(jax.random.uniform(jax.random.fold_in(own, position), (shards_of,), jnp.float32, least / len(cuts), largest / len(cuts)))
        loudness = loudness * jnp.repeat(steps, shape[position] // shards_of).reshape([-1 if axis == position else 1 for axis in range(len(shape))])
    return loudness


def split_up(count, total, reach, lean):
    portions = [(1 << 20) // math.isqrt(grade ** lean) + 1 for grade in range(2, count + 1)]
    spare, counts = total - reach - (count - 1), [1] * (count - 1)
    while spare > 0:
        free = [i for i in range(count - 1) if counts[i] < reach]
        pool, budget = sum([portions[i] for i in free]), spare
        for i in free:
            addition = min(reach - counts[i], max(1, budget * portions[i] // pool), spare)
            counts[i] = counts[i] + addition
            spare = spare - addition
    return np.array([reach] + counts)


def ragged(key, count, total, most, lean):
    if count == 2:
        one = jax.random.randint(key, (), max(1, total - most), min(most, total - 1) + 1)
        return jnp.stack([one, total - one])
    tallies = jnp.asarray(split_up(count, total, most, lean), jnp.int32)
    couples = (count - 1) // 2
    donor, sink = tallies[1:1 + 2 * couples:2], tallies[2:2 + 2 * couples:2]
    slack = jnp.minimum(donor - 1, most - sink)
    moved = jax.random.randint(jax.random.fold_in(key, 1), (couples,), 0, 1 << 20) % (slack + 1)
    tallies = tallies.at[1:1 + 2 * couples:2].set(donor - moved).at[2:2 + 2 * couples:2].set(sink + moved)
    return tallies[jax.random.permutation(jax.random.fold_in(key, 2), count)]


def deal_out(own_key, own, number, rows, number_of, top, limit, lean):
    order = jax.random.permutation(own_key, number_of)
    crowded, common = shares(number_of, rows * top, limit, lean, True), shares(number_of, rows * top, limit, lean, False)
    places = jnp.arange(number_of)

    def named(lengths, turn):
        used = int((lengths > 0).sum())
        fixed = max(1, used // 4)
        moved = fixed + (places - fixed + turn * (used - fixed)) % max(1, number_of - fixed)
        return jnp.zeros((number_of,), jnp.int32).at[order[jnp.where(places < fixed, places, moved)]].set(jnp.asarray(lengths, jnp.int32))

    lengths = jnp.where(number % 4 == 0, named(crowded, number // 4), named(common, number - number // 4 - 1))
    mixed = jax.random.permutation(jax.random.fold_in(own, 3), number_of)
    donor, receiver = mixed[0:number_of // 2 * 2:2], mixed[1:number_of // 2 * 2:2]
    room = jnp.minimum(lengths[donor] - 1, limit - lengths[receiver]) // 2
    room = jnp.where((donor == order[0]) | (receiver == order[0]) | (lengths[receiver] == 0), 0, jnp.maximum(room, 0))
    moved = jax.random.randint(jax.random.fold_in(own, 4), (number_of // 2,), 0, 1 << 20) % (room + 1)
    lengths = lengths.at[donor].add(-moved).at[receiver].add(moved)
    members = jnp.searchsorted(jnp.cumsum(lengths), jnp.arange(rows * top), side="right").astype(jnp.int32)
    table = members.reshape(top, rows).T
    table = table[jax.random.permutation(jax.random.fold_in(own, 1), rows)]
    turn = jax.random.randint(jax.random.fold_in(own, 2), (rows, 1), 0, top)
    return jnp.take_along_axis(table, (jnp.arange(top)[None, :] + turn) % top, axis=1)


def shares(number_of, total, bound, skew, full):
    loads = [(1 << 20) // math.isqrt(rank ** skew) + 1 for rank in range(1, number_of + 1)]
    largest = bound if full else min(bound, max(-(-total // number_of), total * loads[0] // sum(loads)))
    least = 1 if total - largest >= number_of - 1 else 0
    counts, surplus = [largest] + [least] * (number_of - 1), total - largest - least * (number_of - 1)
    while surplus > 0:
        free = [i for i in range(1, number_of) if counts[i] < largest] or [i for i in range(1, number_of) if counts[i] < bound]
        whole, left = sum([loads[i] for i in free]), surplus
        for i in free:
            more = min(bound - counts[i], max(1, left * loads[i] // whole), surplus)
            counts[i] = counts[i] + more
            surplus = surplus - more
    return np.array(counts)


def bell_draw(rng, shape, scale, most, pieces=(), held_as=jnp.bfloat16):
    array = jax.random.normal(rng, shape, jnp.float32) * scale
    if len(pieces) > 0:
        array = block_levels(rng, shape, pieces, -0.22, 0.18) * array
    return jnp.clip(array, min=-most, max=most).astype(held_as)


def setup_inputs(seed: int = 0) -> dict:
    seeds = jax.random.split(jax.random.key(seed), 9)
    queries = bell_draw(seeds[0], (TOKENS, HEADS * HEAD_DIM), 0.25, 4.0, ((0, 32), (1, 4)))
    key_vectors = bell_draw(seeds[1], (TOKENS, HEADS * HEAD_DIM), 1.0, 6.0, ((0, 32), (1, 4)))
    output_grad = bell_draw(seeds[2], (TOKENS, HEADS * HEAD_DIM), 1.0, 6.0, ((0, 32), (1, 4)))
    value_weight = bell_draw(seeds[3], (D, HEADS * HEAD_DIM), D ** -0.5, 0.078125, ((0, 32), (1, 4)))
    decay_rate = draw_decay_rate(jax.random.fold_in(seeds[8], 71), 0)
    doc_lengths = ragged(seeds[5], DOCS, TOKENS, TOKENS // 2, 2).astype(jnp.int32)
    owner_block_keys = jax.random.split(jax.random.fold_in(seeds[6], 1), TOKENS // ROWS_BLK)
    owner_block_turns = jax.random.permutation(jax.random.fold_in(seeds[6], 3), TOKENS // ROWS_BLK)
    owner_block = jax.vmap(lambda own, number: deal_out(jax.random.fold_in(seeds[6], 2), own, number, ROWS_BLK, DEVICES, 1, CAP, 2))(owner_block_keys, owner_block_turns).reshape((TOKENS, 1))
    row_offset = touch_ends(jax.random.randint(seeds[7], (TOKENS,), 0, VROWS), jax.random.fold_in(seeds[7], 1), 0, VROWS - 1).astype(jnp.int32)
    return {"queries": queries, "key_vectors": key_vectors, "output_grad": output_grad, "value_weight": value_weight, "decay_rate": decay_rate, "doc_lengths": doc_lengths, "owner_block": owner_block, "row_offset": row_offset}


def doc_of(positions, doc_ends):
    return jnp.sum((positions[:, None] >= doc_ends[None, :]).astype(jnp.int32), axis=1).astype(jnp.int32)


def intra_terms(query_blk, key_blk, grad_blk, decay_rates, doc_blk, pos_blk):
    scores = jnp.einsum("she,the->hst", key_blk.astype(jnp.float32), query_blk.astype(jnp.float32)) / HEAD_DIM
    distance = pos_blk[None, :] - pos_blk[:, None]
    allowed = (distance >= 0) & (doc_blk[:, None] == doc_blk[None, :])
    spans = jnp.maximum(distance, 0).astype(jnp.float32)
    decayed = jnp.where(allowed[None], jnp.exp(-decay_rates[:, None, None] * spans[None]), 0.0)
    weights = (decayed * scores).astype(jnp.bfloat16)
    return jnp.einsum("hst,thf->shf", weights.astype(jnp.float32), grad_blk.astype(jnp.float32))


def state_terms(query_blk, grad_blk, decay_rates, doc_blk, pos_blk, doc_before, pos_before):
    spans = (pos_blk - pos_before).astype(jnp.float32)
    lead_decay = jnp.where((doc_blk == doc_before)[:, None], jnp.exp(-decay_rates[None, :] * spans[:, None]), 0.0)
    scaled = (query_blk.astype(jnp.float32) * lead_decay[:, :, None]).astype(jnp.bfloat16)
    local_state = jnp.einsum("the,thf->hef", scaled.astype(jnp.float32), grad_blk.astype(jnp.float32))
    whole_span = (pos_blk[-1] - pos_before).astype(jnp.float32)
    link_decay = jnp.where(doc_blk[-1] == doc_before, jnp.exp(-decay_rates * whole_span), 0.0)
    return local_state, link_decay


def inter_terms(key_blk, carried, decay_rates, doc_blk, pos_blk):
    spans = (pos_blk[-1] - pos_blk).astype(jnp.float32)
    tail_decay = jnp.where((doc_blk == doc_blk[-1])[:, None], jnp.exp(-decay_rates[None, :] * spans[:, None]), 0.0)
    rounded_state = carried.astype(jnp.bfloat16).astype(jnp.float32)
    product = jnp.einsum("she,hef->shf", key_blk.astype(jnp.float32), rounded_state) / HEAD_DIM
    return product * tail_decay[:, :, None]


def reference(queries, key_vectors, output_grad, value_weight, decay_rate, doc_lengths, owner_block, row_offset):
    block_count = TOKENS // TOK_DEV
    doc_ends = jnp.cumsum(doc_lengths).astype(jnp.int32)
    positions = jnp.arange(TOKENS, dtype=jnp.int32)
    doc_index = doc_of(positions, doc_ends)
    query_blocks = queries.reshape(block_count, TOK_DEV, HEADS, HEAD_DIM)
    key_blocks = key_vectors.reshape(block_count, TOK_DEV, HEADS, HEAD_DIM)
    grad_blocks = output_grad.reshape(block_count, TOK_DEV, HEADS, HEAD_DIM)
    pos_blocks = positions.reshape(block_count, TOK_DEV)
    doc_blocks = doc_index.reshape(block_count, TOK_DEV)

    def visit(carried, block_id):
        query_blk = query_blocks[block_id]
        key_blk = key_blocks[block_id]
        grad_blk = grad_blocks[block_id]
        pos_blk = pos_blocks[block_id]
        doc_blk = doc_blocks[block_id]
        pos_before = pos_blk[0] - 1
        doc_before = doc_of(jnp.maximum(pos_before, 0)[None], doc_ends)[0]
        intra_part = intra_terms(query_blk, key_blk, grad_blk, decay_rate, doc_blk, pos_blk)
        local_state, link_decay = state_terms(query_blk, grad_blk, decay_rate, doc_blk, pos_blk, doc_before, pos_before)
        inter_part = inter_terms(key_blk, carried, decay_rate, doc_blk, pos_blk)
        value_grad = (intra_part + inter_part).astype(jnp.bfloat16)
        carried_next = link_decay[:, None, None] * carried + local_state
        return carried_next, value_grad

    block_ids = jnp.arange(block_count - 1, -1, -1, dtype=jnp.int32)
    carried_init = jnp.zeros((HEADS, HEAD_DIM, HEAD_DIM), jnp.float32)
    final_state, grads_back = lax.scan(visit, carried_init, block_ids)
    value_grad = jnp.flip(grads_back, 0).reshape(TOKENS, HEADS * HEAD_DIM)

    group_width = HEADS * HEAD_DIM // N_HEAD
    token_grad = jnp.zeros((TOKENS, D), jnp.float32)
    for group_id in range(N_HEAD):
        low_col = group_id * group_width
        group_part = jnp.dot(value_grad[:, low_col:low_col + group_width], value_weight[:, low_col:low_col + group_width].T, preferred_element_type=jnp.float32)
        rounded = lax.optimization_barrier(group_part.astype(jnp.bfloat16))
        token_grad = token_grad + rounded.astype(jnp.float32)
    token_grad = lax.optimization_barrier(token_grad.astype(jnp.bfloat16)).astype(jnp.float32)

    owners = owner_block[:, 0].astype(jnp.int32)
    token_ids = owners * VROWS + row_offset.astype(jnp.int32)
    sort_order = jnp.argsort(token_ids, stable=True).astype(jnp.int32)
    sorted_ids = token_ids[sort_order]
    new_group = jnp.concatenate([jnp.zeros((1,), jnp.int32), (sorted_ids[1:] != sorted_ids[:-1]).astype(jnp.int32)])
    group_index = jnp.cumsum(new_group).astype(jnp.int32)
    group_sums = jax.ops.segment_sum(token_grad[sort_order], group_index, num_segments=TOKENS)
    row_total = jnp.zeros_like(token_grad).at[sort_order].set(group_sums[group_index])

    block_owners = owners.reshape(DEVICES, ROWS_BLK)
    same_owner = block_owners[:, :, None] == block_owners[:, None, :]
    lower_index = jnp.arange(ROWS_BLK, dtype=jnp.int32)
    earlier = lower_index[None, :] < lower_index[:, None]
    slot_rank = jnp.sum((same_owner & earlier[None]).astype(jnp.int32), axis=2).reshape(-1)
    block_of = (positions // ROWS_BLK).astype(jnp.int32)
    row_grads = jnp.zeros((DEVICES, DEVICES, CAP, D), jnp.bfloat16)
    row_grads = row_grads.at[owners, block_of, slot_rank].set(row_total.astype(jnp.bfloat16))
    return row_grads
```

```python
import jax
import jax.numpy as jnp
from jax import lax
from jax.experimental import pallas as pl
from jax.experimental.pallas import tpu as pltpu
from jax.sharding import PartitionSpec as P

BF16 = jnp.bfloat16
F32 = jnp.float32
CAPACITY = 2
ROWS_BLK = 128


def doc_of(positions, doc_ends):
    return jnp.sum((positions[:, None] >= doc_ends[None, :]).astype(jnp.int32), axis=1)


def intra_terms(query_blk, key_blk, grad_blk, decay_rates, doc_blk, pos_blk):
    head_dim = query_blk.shape[-1]
    scores = (
        jnp.einsum("she,the->hst", key_blk, query_blk, preferred_element_type=F32) / head_dim
    )
    distance = pos_blk[None, :] - pos_blk[:, None]
    allowed = (distance >= 0) & (doc_blk[:, None] == doc_blk[None, :])
    spans = jnp.maximum(distance, 0).astype(F32)
    decayed = jnp.where(allowed[None], jnp.exp(-decay_rates[:, None, None] * spans[None]), 0.0)
    weights = (decayed * scores).astype(BF16)
    return jnp.einsum("hst,thf->shf", weights, grad_blk, preferred_element_type=F32)


def state_terms(query_blk, grad_blk, decay_rates, doc_blk, pos_blk, doc_before, pos_before):
    spans = (pos_blk - pos_before).astype(F32)
    lead_decay = jnp.where(
        (doc_blk == doc_before)[:, None], jnp.exp(-decay_rates[None, :] * spans[:, None]), 0.0
    )
    scaled = (query_blk.astype(F32) * lead_decay[:, :, None]).astype(BF16)
    return jnp.einsum("the,thf->hef", scaled, grad_blk, preferred_element_type=F32)


def inter_terms(key_blk, carried, decay_rates, doc_blk, pos_blk):
    head_dim = key_blk.shape[-1]
    spans = (pos_blk[-1] - pos_blk).astype(F32)
    tail_decay = jnp.where(
        (doc_blk == doc_blk[-1])[:, None], jnp.exp(-decay_rates[None, :] * spans[:, None]), 0.0
    )
    product = jnp.einsum("she,hef->shf", key_blk, carried, preferred_element_type=F32) / head_dim
    return product * tail_decay[:, :, None]


def project_body(slot_ref, grads_ref, weight_ref, out_ref, pick_ref):
    slots, toks = pick_ref.shape

    @pl.when(pl.program_id(0) == 0)
    def _():
        rows = lax.broadcasted_iota(jnp.int32, (slots, toks), 0)
        pick_ref[...] = (rows == slot_ref[...]).astype(F32).astype(BF16)

    total = None
    for group in range(grads_ref.shape[0]):
        part = lax.dot_general(
            grads_ref[group],
            weight_ref[group],
            (((1,), (1,)), ((), ())),
            preferred_element_type=F32,
        )
        part = part.astype(BF16).astype(F32)
        total = part if total is None else total + part
    out_ref[...] = jnp.dot(
        pick_ref[...], total.astype(BF16), preferred_element_type=F32
    ).astype(BF16)


def project(slot_index, grads, weight, slots, tile):
    groups, toks, depth = grads.shape
    width = weight.shape[1]
    return pl.pallas_call(
        project_body,
        grid=(width // tile,),
        in_specs=[
            pl.BlockSpec((1, toks), lambda i: (0, 0)),
            pl.BlockSpec((groups, toks, depth), lambda i: (0, 0, 0)),
            pl.BlockSpec((groups, tile, depth), lambda i: (0, i, 0)),
        ],
        out_specs=pl.BlockSpec((slots, tile), lambda i: (0, i)),
        out_shape=jax.ShapeDtypeStruct((slots, width), BF16),
        scratch_shapes=[pltpu.VMEM((slots, toks), BF16)],
        compiler_params=pltpu.CompilerParams(
            dimension_semantics=("arbitrary",), vmem_limit_bytes=56 << 20
        ),
        name="project",
    )(slot_index[None, :], grads, weight)


def merge_body(column_ref, row_ref, rows_ref, out_ref):
    slots = column_ref.shape[0]
    width = rows_ref.shape[-1]
    same = (column_ref[...] == row_ref[...]) & (column_ref[...] >= 0)
    same = same.astype(F32).astype(BF16)
    rows = rows_ref[...].reshape(slots, width)
    total = jnp.dot(same, rows, preferred_element_type=F32).astype(BF16)
    out_ref[...] = total.reshape(out_ref.shape)


def merge(offsets, got, capacity):
    n_seq, n_head, per, width = got.shape
    slots = n_seq * per
    return pl.pallas_call(
        merge_body,
        grid=(n_head,),
        in_specs=[
            pl.BlockSpec((slots, 1), lambda i: (0, 0)),
            pl.BlockSpec((1, slots), lambda i: (0, 0)),
            pl.BlockSpec((n_seq, 1, per, width), lambda i: (0, i, 0, 0)),
        ],
        out_specs=pl.BlockSpec((1, slots // capacity, capacity, width), lambda i: (0, 0, 0, i)),
        out_shape=jax.ShapeDtypeStruct((1, slots // capacity, capacity, n_head * width), BF16),
        compiler_params=pltpu.CompilerParams(
            dimension_semantics=("arbitrary",), vmem_limit_bytes=56 << 20
        ),
        name="merge",
    )(offsets.reshape(slots, 1), offsets.reshape(1, slots), got)


def slots_of(owners, blocks, capacity):
    toks = owners.shape[0]
    width = toks // blocks
    grouped = owners.reshape(blocks, width)
    same_owner = grouped[:, :, None] == grouped[:, None, :]
    lower = jnp.arange(width, dtype=jnp.int32)
    earlier = lower[None, :] < lower[:, None]
    rank = jnp.sum((same_owner & earlier[None]).astype(jnp.int32), axis=2)
    block_ids = jnp.arange(blocks, dtype=jnp.int32)[:, None]
    return ((grouped * blocks + block_ids) * capacity + rank).reshape(toks)


def per_device(
    queries,
    key_vectors,
    output_grad,
    value_weight,
    decay_rate,
    doc_lengths,
    owner_block,
    row_offset,
):
    n_seq = lax.axis_size("seq")
    n_head = lax.axis_size("head")
    devices_all = n_seq * n_head
    tok_rows = queries.shape[0]
    head_local = decay_rate.shape[0]
    head_dim = queries.shape[1] // head_local
    seq_rank = lax.axis_index("seq")
    head_rank = lax.axis_index("head")

    plane = n_seq // n_head
    swap = [
        ((a * plane + p) * n_head + b, (b * plane + p) * n_head + a)
        for a in range(n_head)
        for p in range(plane)
        for b in range(n_head)
    ]
    swapped = lax.ppermute(value_weight, ("seq", "head"), swap)
    weight = lax.all_gather(swapped, "seq", axis=0, tiled=True)
    weight = weight.reshape(n_head, -1, value_weight.shape[1])

    first_row = seq_rank * tok_rows
    positions = first_row + jnp.arange(tok_rows, dtype=jnp.int32)
    doc_ends = jnp.cumsum(doc_lengths)
    doc_index = doc_of(positions, doc_ends)
    pos_before = first_row - 1
    doc_before = doc_of(jnp.maximum(pos_before, 0)[None], doc_ends)[0]
    query_blk = queries.reshape(tok_rows, head_local, head_dim)
    key_blk = key_vectors.reshape(tok_rows, head_local, head_dim)
    grad_blk = output_grad.reshape(tok_rows, head_local, head_dim)

    blocks = tok_rows // ROWS_BLK
    per = blocks * CAPACITY
    slot_index = slots_of(owner_block[:, 0], blocks, CAPACITY)
    my_slots = (
        (jnp.arange(n_seq, dtype=jnp.int32)[:, None] * n_head + head_rank) * per
        + jnp.arange(per, dtype=jnp.int32)[None, :]
    )
    hit = my_slots[:, :, None] == slot_index[None, None, :]
    named = jnp.sum(jnp.where(hit, row_offset[None, None, :] + 1, 0), axis=2)
    high, low = (named // 32).astype(BF16), (named % 32).astype(BF16)

    local_state = state_terms(
        query_blk, grad_blk, decay_rate, doc_index, positions, doc_before, pos_before
    )
    share = head_local * head_dim * head_dim // n_seq // head_dim
    note = jnp.concatenate([high, low], axis=1)
    note = jnp.pad(note, ((0, 0), (0, head_dim - 2 * per)))[:, None, :]
    note = jnp.pad(note, ((0, 0), (0, 7), (0, 0)))
    sent = jnp.concatenate(
        [local_state.astype(BF16).reshape(n_seq, share, head_dim), note], axis=1
    )
    state_in = lax.all_to_all(sent, "seq", split_axis=0, concat_axis=0, tiled=True)
    offsets = (
        state_in[:, share, :per].astype(jnp.int32) * 32
        + state_in[:, share, per : 2 * per].astype(jnp.int32)
        - 1
    )
    ranks = jnp.arange(n_seq, dtype=jnp.int32)
    doc_last = doc_of((ranks + 1) * tok_rows - 1, doc_ends)
    doc_prior = doc_of(jnp.maximum(ranks * tok_rows - 1, 0), doc_ends)
    my_rate = decay_rate[seq_rank // (n_seq // head_local)]
    ahead = ranks[None, :] - ranks[:, None] - 1
    reach = (ahead >= 0) & (doc_last[:, None] == doc_prior[None, :])
    chain = jnp.where(
        reach, jnp.exp(-my_rate * (jnp.maximum(ahead, 0) * tok_rows).astype(F32)), 0.0
    )
    carried_all = jnp.einsum(
        "bc,cxy->bxy",
        chain,
        state_in[:, :share].astype(F32),
        precision=lax.Precision.HIGHEST,
        preferred_element_type=F32,
    ).astype(BF16)
    carried = lax.all_to_all(carried_all, "seq", split_axis=0, concat_axis=0, tiled=True)
    carried = carried.reshape(head_local, head_dim, head_dim)

    intra_part = intra_terms(query_blk, key_blk, grad_blk, decay_rate, doc_index, positions)
    inter_part = inter_terms(key_blk, carried, decay_rate, doc_index, positions)
    value_grad = (intra_part + inter_part).astype(BF16).reshape(tok_rows, head_local * head_dim)
    grads = lax.all_gather(value_grad, "head", axis=0)

    send = project(slot_index, grads, weight, devices_all * per, 256)
    send = send.reshape(devices_all, per, -1)
    got = lax.all_to_all(send, ("seq", "head"), split_axis=0, concat_axis=0, tiled=True)
    got = got.reshape(n_seq, n_head, per, -1)
    return merge(offsets, got, CAPACITY)


def solution(mesh):
    return jax.shard_map(
        per_device,
        mesh=mesh,
        in_specs=(
            P("seq", "head"),
            P("seq", "head"),
            P("seq", "head"),
            P("seq", "head"),
            P("head"),
            P(),
            P("seq", None),
            P("seq"),
        ),
        out_specs=P(("seq", "head"), None, None, None),
        check_vma=False,
    )
```

```python
import jax
import jax.numpy as jnp
from jax import lax
from jax.experimental import pallas as pl
from jax.experimental.pallas import tpu as pltpu
from jax.sharding import PartitionSpec as P

BF16 = jnp.bfloat16
F32 = jnp.float32
CAPACITY = 2
ROWS_BLK = 128


def doc_of(positions, doc_ends):
    return jnp.sum((positions[:, None] >= doc_ends[None, :]).astype(jnp.int32), axis=1)


BIG = 1 << 30


def doc_limit(positions, lengths_ref):
    end = lengths_ref[0]
    limit = jnp.where(positions < end, end, BIG)
    for doc in range(1, lengths_ref.shape[0]):
        end = end + lengths_ref[doc]
        limit = jnp.minimum(limit, jnp.where(positions < end, end, BIG))
    return limit


def local_state_body(rate_ref, lengths_ref, query_ref, grad_ref, out_ref):
    toks = query_ref.shape[0]
    rate = rate_ref[pl.program_id(0)]
    first = lax.axis_index("seq") * toks
    limit = doc_limit(jnp.maximum(first - 1, 0), lengths_ref)
    step = lax.broadcasted_iota(jnp.int32, (toks, 1), 0)
    lead = jnp.where(first + step < limit, jnp.exp(-rate * (step + 1).astype(F32)), 0.0)
    scaled = (query_ref[...].astype(F32) * lead).astype(BF16)
    out_ref[0] = lax.dot_general(
        scaled, grad_ref[...], (((0,), (0,)), ((), ())), preferred_element_type=F32
    ).astype(out_ref.dtype)


def local_states(rates, lengths, queries, grads):
    heads = rates.shape[0]
    toks, dim = queries.shape[0], queries.shape[1] // heads
    blk = pl.BlockSpec((toks, dim), lambda h: (0, h))
    return pl.pallas_call(
        local_state_body,
        grid=(heads,),
        in_specs=[
            pl.BlockSpec(memory_space=pltpu.SMEM),
            pl.BlockSpec(memory_space=pltpu.SMEM),
            blk,
            blk,
        ],
        out_specs=pl.BlockSpec((1, dim, dim), lambda h: (h, 0, 0)),
        out_shape=jax.ShapeDtypeStruct((heads, dim, dim), BF16),
        compiler_params=pltpu.CompilerParams(dimension_semantics=("arbitrary",)),
        name="local_states",
    )(rates, lengths, queries, grads)


def within_body(rate_ref, lengths_ref, query_ref, key_ref, grad_ref, out_ref):
    toks, dim = query_ref.shape
    rate = rate_ref[pl.program_id(0)]
    first = lax.axis_index("seq") * toks
    half = toks // 2
    for lo in (0, half):
        src = lax.broadcasted_iota(jnp.int32, (half, 1), 0) + lo
        dst = lax.broadcasted_iota(jnp.int32, (1, toks - lo), 1) + lo
        limit = doc_limit(src + first, lengths_ref) - first
        rise = jnp.exp(rate * src.astype(F32)) * (1.0 / dim)
        fall = jnp.exp(-rate * dst.astype(F32))
        scores = lax.dot_general(
            key_ref[lo : lo + half, :],
            query_ref[lo:, :],
            (((1,), (1,)), ((), ())),
            preferred_element_type=F32,
        )
        seen = (dst >= src) & (dst < limit)
        weights = jnp.where(seen, scores * rise * fall, 0.0).astype(BF16)
        out_ref[lo : lo + half, :] = jnp.dot(
            weights, grad_ref[lo:, :], preferred_element_type=F32
        )


def within(rates, lengths, queries, keys, grads):
    heads = rates.shape[0]
    toks, dim = queries.shape[0], queries.shape[1] // heads
    blk = pl.BlockSpec((toks, dim), lambda h: (0, h))
    return pl.pallas_call(
        within_body,
        grid=(heads,),
        in_specs=[
            pl.BlockSpec(memory_space=pltpu.SMEM),
            pl.BlockSpec(memory_space=pltpu.SMEM),
            blk,
            blk,
            blk,
        ],
        out_specs=blk,
        out_shape=jax.ShapeDtypeStruct((toks, heads * dim), F32),
        compiler_params=pltpu.CompilerParams(dimension_semantics=("arbitrary",)),
        name="within",
    )(rates, lengths, queries, keys, grads)


def across_body(start, rate_ref, lengths_ref, key_ref, state_ref, intra_ref, out_ref):
    toks, dim = key_ref.shape
    rate = rate_ref[pl.program_id(0) + start]
    first = lax.axis_index("seq") * toks
    src = lax.broadcasted_iota(jnp.int32, (toks, 1), 0)
    limit = doc_limit(src + first, lengths_ref) - first
    tail = jnp.where(
        toks - 1 < limit, jnp.exp(-rate * (toks - 1 - src).astype(F32)) * (1.0 / dim), 0.0
    )
    product = jnp.dot(key_ref[...], state_ref[0], preferred_element_type=F32)
    out_ref[...] = (intra_ref[...] + product * tail).astype(BF16)


def across(rates, lengths, keys, states, intra, start, count):
    dim = states.shape[-1]
    toks = keys.shape[0]
    blk = pl.BlockSpec((toks, dim), lambda h: (0, h + start))
    return pl.pallas_call(
        lambda *refs: across_body(start, *refs),
        grid=(count,),
        in_specs=[
            pl.BlockSpec(memory_space=pltpu.SMEM),
            pl.BlockSpec(memory_space=pltpu.SMEM),
            blk,
            pl.BlockSpec((1, dim, dim), lambda h: (h + start, 0, 0)),
            blk,
        ],
        out_specs=pl.BlockSpec((toks, dim), lambda h: (0, h)),
        out_shape=jax.ShapeDtypeStruct((toks, count * dim), BF16),
        compiler_params=pltpu.CompilerParams(dimension_semantics=("arbitrary",)),
        name="across",
    )(rates, lengths, keys, states, intra)


def times(rows, weight):
    return lax.dot_general(rows, weight, (((1,), (1,)), ((), ())), preferred_element_type=F32)


def near_body(which_ref, a0, a1, b0, b1, c0, c1, wa, wb, wc, out_ref):
    half = a0.shape[1]
    total = None
    for lo, hi, weight in ((a0, a1, wa), (b0, b1, wb), (c0, c1, wc)):
        part = times(lo[...], weight[0, :, :half]) + times(hi[...], weight[0, :, half:])
        part = part.astype(BF16).astype(F32)
        total = part if total is None else total + part
    out_ref[...] = total


def project_near(which, pieces, weight, tile):
    toks, half = pieces[0].shape
    width, depth = weight.shape[1:]
    whole = pl.BlockSpec((toks, half), lambda i, w: (0, 0))
    return pl.pallas_call(
        near_body,
        grid_spec=pltpu.PrefetchScalarGridSpec(
            num_scalar_prefetch=1,
            grid=(width // tile,),
            in_specs=[whole] * 6
            + [
                pl.BlockSpec((1, tile, depth), lambda i, w, k=k: (w[k], i, 0))
                for k in range(3)
            ],
            out_specs=pl.BlockSpec((toks, tile), lambda i, w: (0, i)),
        ),
        out_shape=jax.ShapeDtypeStruct((toks, width), F32),
        compiler_params=pltpu.CompilerParams(
            dimension_semantics=("arbitrary",), vmem_limit_bytes=50 << 20
        ),
        name="project_near",
    )(which, *pieces, weight, weight, weight)


def far_body(which_ref, slot_ref, lo, hi, weight, near_ref, out_ref, pick_ref):
    slots, toks = pick_ref.shape
    half = lo.shape[1]

    @pl.when(pl.program_id(0) == 0)
    def _():
        rows = lax.broadcasted_iota(jnp.int32, (slots, toks), 0)
        pick_ref[...] = (rows == slot_ref[...]).astype(F32).astype(BF16)

    part = times(lo[...], weight[0, :, :half]) + times(hi[...], weight[0, :, half:])
    total = near_ref[...] + part.astype(BF16).astype(F32)
    out_ref[...] = jnp.dot(
        pick_ref[...], total.astype(BF16), preferred_element_type=F32
    ).astype(BF16)


def project_far(which, slot_index, lo, hi, weight, near, slots, tile):
    toks, half = lo.shape
    width, depth = weight.shape[1:]
    whole = pl.BlockSpec((toks, half), lambda i, w: (0, 0))
    return pl.pallas_call(
        far_body,
        grid_spec=pltpu.PrefetchScalarGridSpec(
            num_scalar_prefetch=1,
            grid=(width // tile,),
            in_specs=[
                pl.BlockSpec((1, toks), lambda i, w: (0, 0)),
                whole,
                whole,
                pl.BlockSpec((1, tile, depth), lambda i, w: (w[3], i, 0)),
                pl.BlockSpec((toks, tile), lambda i, w: (0, i)),
            ],
            out_specs=pl.BlockSpec((slots, tile), lambda i, w: (0, i)),
            scratch_shapes=[pltpu.VMEM((slots, toks), BF16)],
        ),
        out_shape=jax.ShapeDtypeStruct((slots, width), BF16),
        compiler_params=pltpu.CompilerParams(
            dimension_semantics=("arbitrary",), vmem_limit_bytes=50 << 20
        ),
        name="project_far",
    )(which, slot_index[None, :], lo, hi, weight, near)


def merge_body(column_ref, row_ref, rows_ref, out_ref):
    slots = column_ref.shape[0]
    width = rows_ref.shape[-1]
    same = (column_ref[...] == row_ref[...]) & (column_ref[...] >= 0)
    same = same.astype(F32).astype(BF16)
    rows = rows_ref[...].reshape(slots, width)
    total = jnp.dot(same, rows, preferred_element_type=F32).astype(BF16)
    out_ref[...] = total.reshape(out_ref.shape)


def merge(offsets, got, capacity):
    n_seq, n_head, per, width = got.shape
    slots = n_seq * per
    return pl.pallas_call(
        merge_body,
        grid=(n_head,),
        in_specs=[
            pl.BlockSpec((slots, 1), lambda i: (0, 0)),
            pl.BlockSpec((1, slots), lambda i: (0, 0)),
            pl.BlockSpec((n_seq, 1, per, width), lambda i: (0, i, 0, 0)),
        ],
        out_specs=pl.BlockSpec((1, slots // capacity, capacity, width), lambda i: (0, 0, 0, i)),
        out_shape=jax.ShapeDtypeStruct((1, slots // capacity, capacity, n_head * width), BF16),
        compiler_params=pltpu.CompilerParams(
            dimension_semantics=("arbitrary",), vmem_limit_bytes=56 << 20
        ),
        name="merge",
    )(offsets.reshape(slots, 1), offsets.reshape(1, slots), got)


def slots_of(owners, blocks, capacity):
    toks = owners.shape[0]
    width = toks // blocks
    grouped = owners.reshape(blocks, width)
    same_owner = grouped[:, :, None] == grouped[:, None, :]
    lower = jnp.arange(width, dtype=jnp.int32)
    earlier = lower[None, :] < lower[:, None]
    rank = jnp.sum((same_owner & earlier[None]).astype(jnp.int32), axis=2)
    block_ids = jnp.arange(blocks, dtype=jnp.int32)[:, None]
    return ((grouped * blocks + block_ids) * capacity + rank).reshape(toks)


def per_device(
    queries,
    key_vectors,
    output_grad,
    value_weight,
    decay_rate,
    doc_lengths,
    owner_block,
    row_offset,
):
    n_seq = lax.axis_size("seq")
    n_head = lax.axis_size("head")
    devices_all = n_seq * n_head
    tok_rows = queries.shape[0]
    head_local = decay_rate.shape[0]
    head_dim = queries.shape[1] // head_local
    seq_rank = lax.axis_index("seq")
    head_rank = lax.axis_index("head")

    plane = n_seq // n_head
    swap = [
        ((a * plane + p) * n_head + b, (b * plane + p) * n_head + a)
        for a in range(n_head)
        for p in range(plane)
        for b in range(n_head)
    ]
    swapped = lax.ppermute(value_weight, ("seq", "head"), swap)
    weight = lax.all_gather(swapped, "seq", axis=0, tiled=True)
    weight = weight.reshape(n_head, -1, value_weight.shape[1])

    blocks = tok_rows // ROWS_BLK
    per = blocks * CAPACITY
    slot_index = slots_of(owner_block[:, 0], blocks, CAPACITY)
    my_slots = (
        (jnp.arange(n_seq, dtype=jnp.int32)[:, None] * n_head + head_rank) * per
        + jnp.arange(per, dtype=jnp.int32)[None, :]
    )
    hit = my_slots[:, :, None] == slot_index[None, None, :]
    named = jnp.sum(jnp.where(hit, row_offset[None, None, :] + 1, 0), axis=2)
    note = jnp.concatenate([(named // 32).astype(BF16), (named % 32).astype(BF16)], axis=1)
    note = jnp.pad(note[:, None, :], ((0, 0), (0, 7), (0, head_dim - 2 * per)))

    state = local_states(decay_rate, doc_lengths, queries, output_grad)
    share = head_local * head_dim // n_seq
    state_in = lax.all_to_all(
        state.reshape(n_seq, share, head_dim), "seq", split_axis=0, concat_axis=0, tiled=True
    )
    intra = within(decay_rate, doc_lengths, queries, key_vectors, output_grad)

    doc_ends = jnp.cumsum(doc_lengths)
    ranks = jnp.arange(n_seq, dtype=jnp.int32)
    doc_last = doc_of((ranks + 1) * tok_rows - 1, doc_ends)
    doc_prior = doc_of(jnp.maximum(ranks * tok_rows - 1, 0), doc_ends)
    my_rate = decay_rate[seq_rank // (n_seq // head_local)]
    ahead = ranks[None, :] - ranks[:, None] - 1
    reach = (ahead >= 0) & (doc_last[:, None] == doc_prior[None, :])
    chain = jnp.where(
        reach, jnp.exp(-my_rate * (jnp.maximum(ahead, 0) * tok_rows).astype(F32)), 0.0
    )
    carried_all = jnp.einsum(
        "bc,cxy->bxy",
        chain,
        state_in.astype(F32),
        precision=lax.Precision.HIGHEST,
        preferred_element_type=F32,
    ).astype(BF16)
    carried = lax.all_to_all(
        jnp.concatenate([carried_all, note], axis=1),
        "seq",
        split_axis=0,
        concat_axis=0,
        tiled=True,
    )
    offsets = (
        carried[:, share, :per].astype(jnp.int32) * 32
        + carried[:, share, per : 2 * per].astype(jnp.int32)
        - 1
    )
    carried = carried[:, :share].reshape(head_local, head_dim, head_dim)

    half = head_local // 2
    own = [
        across(decay_rate, doc_lengths, key_vectors, carried, intra, start, half)
        for start in (0, half)
    ]
    up = [(i, (i + 1) % n_head) for i in range(n_head)]
    down = [(i, (i - 1) % n_head) for i in range(n_head)]
    left_lo = lax.ppermute(own[0], "head", up)
    right_hi = lax.ppermute(own[1], "head", down)
    left_hi = lax.ppermute(own[1], "head", up)
    right_lo = lax.ppermute(own[0], "head", down)
    far_lo = lax.ppermute(left_lo, "head", up)
    far_hi = lax.ppermute(right_hi, "head", down)
    which = (head_rank + jnp.array([0, n_head - 1, 1, 2], jnp.int32)) % n_head

    near = project_near(
        which, (own[0], own[1], left_lo, left_hi, right_lo, right_hi), weight, 256
    )
    send = project_far(which, slot_index, far_lo, far_hi, weight, near, devices_all * per, 256)
    send = send.reshape(devices_all, per, -1)
    got = lax.all_to_all(send, ("seq", "head"), split_axis=0, concat_axis=0, tiled=True)
    got = got.reshape(n_seq, n_head, per, -1)
    return merge(offsets, got, CAPACITY)


def solution(mesh):
    return jax.shard_map(
        per_device,
        mesh=mesh,
        in_specs=(
            P("seq", "head"),
            P("seq", "head"),
            P("seq", "head"),
            P("seq", "head"),
            P("head"),
            P(),
            P("seq", None),
            P("seq"),
        ),
        out_specs=P(("seq", "head"), None, None, None),
        check_vma=False,
    )
```

```python
import functools

import jax
import jax.numpy as jnp
from jax import lax
from jax.experimental import pallas as pl
from jax.experimental.pallas import tpu as pltpu
from jax.sharding import PartitionSpec as P

BF16 = jnp.bfloat16
F32 = jnp.float32
CAPACITY = 2
ROWS_BLK = 128
BIG = 1 << 30
CORES = 2


def doc_of(positions, doc_ends):
    return jnp.sum((positions[:, None] >= doc_ends[None, :]).astype(jnp.int32), axis=1)


def doc_limit(positions, lengths_ref):
    end = lengths_ref[0]
    limit = jnp.where(positions < end, end, BIG)
    for doc in range(1, lengths_ref.shape[0]):
        end = end + lengths_ref[doc]
        limit = jnp.minimum(limit, jnp.where(positions < end, end, BIG))
    return limit


def params(mib=48):
    return pltpu.CompilerParams(
        dimension_semantics=("arbitrary",), vmem_limit_bytes=mib << 20
    )


SCALARS = pl.BlockSpec(memory_space=pltpu.SMEM)


def local_state_body(rate_ref, lengths_ref, query_ref, grad_ref, out_ref):
    count, dim = out_ref.shape[:2]
    toks = query_ref.shape[0]
    first = lax.axis_index("seq") * toks
    limit = doc_limit(jnp.maximum(first - 1, 0), lengths_ref)
    step = lax.broadcasted_iota(jnp.int32, (toks, dim), 0)
    inside = first + step < limit
    span = (step + 1).astype(F32)
    for h in range(count):
        rate = rate_ref[pl.program_id(0) * count + h]
        cols = slice(h * dim, (h + 1) * dim)
        lead = jnp.where(inside, jnp.exp(-rate * span), 0.0)
        scaled = (query_ref[:, cols].astype(F32) * lead).astype(BF16)
        out_ref[h] = lax.dot_general(
            scaled, grad_ref[:, cols], (((0,), (0,)), ((), ())), preferred_element_type=F32
        ).astype(out_ref.dtype)


def local_states(rates, lengths, queries, grads, count):
    heads = rates.shape[0]
    toks, dim = queries.shape[0], queries.shape[1] // heads
    blk = pl.BlockSpec((toks, count * dim), lambda h: (0, h))
    return pl.pallas_call(
        local_state_body,
        grid=(heads // count,),
        in_specs=[SCALARS, SCALARS, blk, blk],
        out_specs=pl.BlockSpec((count, dim, dim), lambda h: (h, 0, 0)),
        out_shape=jax.ShapeDtypeStruct((heads, dim, dim), BF16),
        compiler_params=params(),
        name="local_states",
    )(rates, lengths, queries, grads)


def within_body(count, rate_ref, lengths_ref, query_ref, key_ref, grad_ref, out_ref):
    toks = query_ref.shape[0]
    dim = query_ref.shape[1] // count
    first = lax.axis_index("seq") * toks
    half = toks // 2
    for lo in (0, half):
        src = lax.broadcasted_iota(jnp.int32, (half, 1), 0) + lo
        dst = lax.broadcasted_iota(jnp.int32, (1, toks - lo), 1) + lo
        limit = doc_limit(src + first, lengths_ref) - first
        seen = (dst >= src) & (dst < limit)
        for h in range(count):
            rate = rate_ref[pl.program_id(0) * count + h]
            cols = slice(h * dim, (h + 1) * dim)
            rise = jnp.exp(rate * src.astype(F32)) * (1.0 / dim)
            fall = jnp.exp(-rate * dst.astype(F32))
            scores = lax.dot_general(
                key_ref[lo : lo + half, cols],
                query_ref[lo:, cols],
                (((1,), (1,)), ((), ())),
                preferred_element_type=F32,
            )
            weights = jnp.where(seen, scores * rise * fall, 0.0).astype(BF16)
            out_ref[lo : lo + half, cols] = jnp.dot(
                weights, grad_ref[lo:, cols], preferred_element_type=F32
            )


def within(rates, lengths, queries, keys, grads, count):
    heads = rates.shape[0]
    toks, dim = queries.shape[0], queries.shape[1] // heads
    blk = pl.BlockSpec((toks, count * dim), lambda h: (0, h))
    return pl.pallas_call(
        functools.partial(within_body, count),
        grid=(heads // count,),
        in_specs=[SCALARS, SCALARS, blk, blk, blk],
        out_specs=blk,
        out_shape=jax.ShapeDtypeStruct((toks, heads * dim), F32),
        compiler_params=params(),
        name="within",
    )(rates, lengths, queries, keys, grads)


def across_body(start, rate_ref, lengths_ref, key_ref, state_ref, intra_ref, out_ref):
    count, dim = state_ref.shape[:2]
    toks = key_ref.shape[0]
    first = lax.axis_index("seq") * toks
    src = lax.broadcasted_iota(jnp.int32, (toks, dim), 0)
    last = first + toks - 1
    inside = last < doc_limit(src + first, lengths_ref)
    span = (toks - 1 - src).astype(F32)
    for h in range(count):
        rate = rate_ref[start + h]
        cols = slice(h * dim, (h + 1) * dim)
        tail = jnp.where(inside, jnp.exp(-rate * span) * (1.0 / dim), 0.0)
        product = jnp.dot(key_ref[:, cols], state_ref[h], preferred_element_type=F32)
        out_ref[:, cols] = (intra_ref[:, cols] + product * tail).astype(BF16)


def across(rates, lengths, keys, states, intra, part, count):
    dim = states.shape[-1]
    toks = keys.shape[0]
    blk = pl.BlockSpec((toks, count * dim), lambda i: (0, part))
    return pl.pallas_call(
        functools.partial(across_body, part * count),
        grid=(1,),
        in_specs=[
            SCALARS,
            SCALARS,
            blk,
            pl.BlockSpec((count, dim, dim), lambda i: (part, 0, 0)),
            blk,
        ],
        out_specs=pl.BlockSpec((toks, count * dim), lambda i: (0, 0)),
        out_shape=jax.ShapeDtypeStruct((toks, count * dim), BF16),
        compiler_params=params(),
        name="across",
    )(rates, lengths, keys, states, intra)


def times(lo, hi, weight):
    half = lo.shape[1]
    dims = (((1,), (1,)), ((), ()))
    part = lax.dot_general(lo[...], weight[0, :, :half], dims, preferred_element_type=F32)
    part += lax.dot_general(hi[...], weight[0, :, half:], dims, preferred_element_type=F32)
    return part.astype(BF16).astype(F32)


def near_body(place, a0, a1, b0, b1, c0, c1, wa, wb, wc, out_ref):
    total = times(a0, a1, wa) + times(b0, b1, wb)
    out_ref[...] = total + times(c0, c1, wc)


def project_near(place, pieces, weight, tile):
    toks, half = pieces[0].shape
    width, depth = weight.shape[1:]
    whole = pl.BlockSpec((toks, half), lambda i, p: (0, 0))
    return pl.pallas_call(
        near_body,
        grid_spec=pltpu.PrefetchScalarGridSpec(
            num_scalar_prefetch=1,
            grid=(width // tile,),
            in_specs=[whole] * 6
            + [
                pl.BlockSpec((1, tile, depth), lambda i, p, k=k: (p[k], i, 0))
                for k in range(3)
            ],
            out_specs=pl.BlockSpec((toks, tile), lambda i, p: (0, i)),
        ),
        out_shape=jax.ShapeDtypeStruct((toks, width), F32),
        compiler_params=params(),
        name="project_near",
    )(place, *pieces, weight, weight, weight)


def far_body(tiles, place, pick, lo, hi, mine, other, near_mine, near_other, out_ref):
    def fill(weight, near):
        total = near[...] + times(lo, hi, weight)
        out_ref[...] = jnp.dot(
            pick[...], total.astype(BF16), preferred_element_type=F32
        ).astype(BF16)

    first = pl.program_id(0) < tiles
    pl.when(first)(lambda: fill(mine, near_mine))
    pl.when(jnp.logical_not(first))(lambda: fill(other, near_other))


def project_far(place, pick, lo, hi, mine, other, near_mine, near_other, tile):
    toks, half = lo.shape
    slots = pick.shape[0]
    width, depth = mine.shape[1:]
    tiles = width // tile
    whole = pl.BlockSpec((toks, half), lambda i, p: (0, 0))

    def early(i):
        return jnp.minimum(i, tiles - 1)

    def late(i):
        return jnp.maximum(i - tiles, 0)

    def target(i, p):
        turn = jnp.where(i < tiles, p[4], CORES - 1 - p[4])
        return (0, turn * tiles + jnp.where(i < tiles, i, i - tiles))

    return pl.pallas_call(
        functools.partial(far_body, tiles),
        grid_spec=pltpu.PrefetchScalarGridSpec(
            num_scalar_prefetch=1,
            grid=(CORES * tiles,),
            in_specs=[
                pl.BlockSpec((slots, toks), lambda i, p: (0, 0)),
                whole,
                whole,
                pl.BlockSpec((1, tile, depth), lambda i, p: (p[3], early(i), 0)),
                pl.BlockSpec((1, tile, depth), lambda i, p: (p[3], late(i), 0)),
                pl.BlockSpec((toks, tile), lambda i, p: (0, early(i))),
                pl.BlockSpec((toks, tile), lambda i, p: (0, late(i))),
            ],
            out_specs=pl.BlockSpec((slots, tile), target),
        ),
        out_shape=jax.ShapeDtypeStruct((slots, CORES * width), BF16),
        compiler_params=params(),
        name="project_far",
    )(place, pick, lo, hi, mine, other, near_mine, near_other)


def merge_body(column_ref, row_ref, rows_ref, out_ref):
    slots = column_ref.shape[0]
    width = rows_ref.shape[-1]
    same = (column_ref[...] == row_ref[...]) & (column_ref[...] >= 0)
    same = same.astype(F32).astype(BF16)
    rows = rows_ref[...].reshape(slots, width)
    total = jnp.dot(same, rows, preferred_element_type=F32).astype(BF16)
    out_ref[...] = total.reshape(out_ref.shape)


def merge(offsets, got, tile):
    n_seq, n_head, per, width = got.shape
    slots = n_seq * per
    tiles = width // tile
    return pl.pallas_call(
        merge_body,
        grid=(n_head * tiles,),
        in_specs=[
            pl.BlockSpec((slots, 1), lambda i: (0, 0)),
            pl.BlockSpec((1, slots), lambda i: (0, 0)),
            pl.BlockSpec((n_seq, 1, per, tile), lambda i: (0, i // tiles, 0, i % tiles)),
        ],
        out_specs=pl.BlockSpec((1, slots // CAPACITY, CAPACITY, tile), lambda i: (0, 0, 0, i)),
        out_shape=jax.ShapeDtypeStruct((1, slots // CAPACITY, CAPACITY, n_head * width), BF16),
        compiler_params=params(),
        name="merge",
    )(offsets.reshape(slots, 1), offsets.reshape(1, slots), got)


def slots_of(owners, blocks, capacity):
    toks = owners.shape[0]
    width = toks // blocks
    grouped = owners.reshape(blocks, width)
    same_owner = grouped[:, :, None] == grouped[:, None, :]
    lower = jnp.arange(width, dtype=jnp.int32)
    earlier = lower[None, :] < lower[:, None]
    rank = jnp.sum((same_owner & earlier[None]).astype(jnp.int32), axis=2)
    block_ids = jnp.arange(blocks, dtype=jnp.int32)[:, None]
    return ((grouped * blocks + block_ids) * capacity + rank).reshape(toks)


def weight_route(n_seq, n_head):
    rows = n_seq // n_head // CORES
    pairs = []
    for z in range(n_head):
        for y in range(rows):
            for core in range(CORES):
                for x in range(n_head):
                    spot = y * CORES + core
                    to_core, to_y = spot // rows, spot % rows
                    source = ((z * rows + y) * CORES + core) * n_head + x
                    target = ((x * rows + to_y) * CORES + to_core) * n_head + z
                    pairs.append((source, target))
    return pairs


def per_device(
    queries,
    key_vectors,
    output_grad,
    value_weight,
    decay_rate,
    doc_lengths,
    owner_block,
    row_offset,
):
    n_seq = lax.axis_size("seq")
    n_head = lax.axis_size("head")
    devices_all = n_seq * n_head
    tok_rows = queries.shape[0]
    head_local = decay_rate.shape[0]
    head_dim = queries.shape[1] // head_local
    seq_rank = lax.axis_index("seq")
    head_rank = lax.axis_index("head")

    swapped = lax.ppermute(value_weight, ("seq", "head"), weight_route(n_seq, n_head))
    state = local_states(decay_rate, doc_lengths, queries, output_grad, head_local // 2)

    blocks = tok_rows // ROWS_BLK
    per = blocks * CAPACITY
    slot_index = slots_of(owner_block[:, 0], blocks, CAPACITY)
    my_slots = (
        (jnp.arange(n_seq, dtype=jnp.int32)[:, None] * n_head + head_rank) * per
        + jnp.arange(per, dtype=jnp.int32)[None, :]
    )
    hit = my_slots[:, :, None] == slot_index[None, None, :]
    named = jnp.sum(jnp.where(hit, row_offset[None, None, :] + 1, 0), axis=2)
    note = jnp.concatenate([(named // 32).astype(BF16), (named % 32).astype(BF16)], axis=1)
    note = jnp.pad(note[:, None, :], ((0, 0), (0, 7), (0, head_dim - 2 * per)))
    all_slots = jnp.arange(devices_all * per, dtype=jnp.int32)
    pick = (all_slots[:, None] == slot_index[None, :]).astype(BF16)

    share = head_local * head_dim // n_seq
    state_in = lax.all_to_all(
        state.reshape(n_seq, share, head_dim), "seq", split_axis=0, concat_axis=0, tiled=True
    )
    intra = within(
        decay_rate, doc_lengths, queries, key_vectors, output_grad, head_local // 2
    )

    doc_ends = jnp.cumsum(doc_lengths)
    ranks = jnp.arange(n_seq, dtype=jnp.int32)
    doc_last = doc_of((ranks + 1) * tok_rows - 1, doc_ends)
    doc_prior = doc_of(jnp.maximum(ranks * tok_rows - 1, 0), doc_ends)
    my_rate = decay_rate[seq_rank // (n_seq // head_local)]
    ahead = ranks[None, :] - ranks[:, None] - 1
    reach = (ahead >= 0) & (doc_last[:, None] == doc_prior[None, :])
    chain = jnp.where(
        reach, jnp.exp(-my_rate * (jnp.maximum(ahead, 0) * tok_rows).astype(F32)), 0.0
    )
    carried_all = jnp.einsum(
        "bc,cxy->bxy",
        chain,
        state_in.astype(F32),
        precision=lax.Precision.HIGHEST,
        preferred_element_type=F32,
    ).astype(BF16)
    carried_all = jnp.concatenate([carried_all, note], axis=1)
    swapped, _ = lax.optimization_barrier((swapped, carried_all))
    groups = [list(range(core, n_seq, CORES)) for core in range(CORES)]
    mine = lax.all_gather(swapped, "seq", axis=0, tiled=True, axis_index_groups=groups)
    mine = mine.reshape(n_head, -1, value_weight.shape[1])

    carried = lax.all_to_all(
        carried_all,
        "seq",
        split_axis=0,
        concat_axis=0,
        tiled=True,
    )
    offsets = (
        carried[:, share, :per].astype(jnp.int32) * 32
        + carried[:, share, per : 2 * per].astype(jnp.int32)
        - 1
    )
    carried = carried[:, :share].reshape(head_local, head_dim, head_dim)

    own = [
        across(decay_rate, doc_lengths, key_vectors, carried, intra, part, head_local // 2)
        for part in range(2)
    ]
    up = [(i, (i + 1) % n_head) for i in range(n_head)]
    down = [(i, (i - 1) % n_head) for i in range(n_head)]
    left_lo = lax.ppermute(own[0], "head", up)
    right_hi = lax.ppermute(own[1], "head", down)
    left_hi = lax.ppermute(own[1], "head", up)
    right_lo = lax.ppermute(own[0], "head", down)
    far_lo = lax.ppermute(left_lo, "head", up)
    far_hi = lax.ppermute(right_hi, "head", down)
    mine, *_ = lax.optimization_barrier((mine, left_lo, right_hi, left_hi, right_lo))
    other = lax.ppermute(mine, "seq", [(i, i ^ 1) for i in range(n_seq)])
    ring = (head_rank + jnp.array([0, n_head - 1, 1, 2], jnp.int32)) % n_head
    place = jnp.concatenate([ring, (seq_rank % CORES)[None]])

    pieces = (own[0], own[1], left_lo, left_hi, right_lo, right_hi)
    near_mine = project_near(place, pieces, mine, 256)
    near_other = project_near(place, pieces, other, 256)
    send = project_far(place, pick, far_lo, far_hi, mine, other, near_mine, near_other, 256)
    send = send.reshape(devices_all, per, -1)
    got = lax.all_to_all(send, ("seq", "head"), split_axis=0, concat_axis=0, tiled=True)
    return merge(offsets, got.reshape(n_seq, n_head, per, -1), 768)


def solution(mesh):
    return jax.shard_map(
        per_device,
        mesh=mesh,
        in_specs=(
            P("seq", "head"),
            P("seq", "head"),
            P("seq", "head"),
            P("seq", "head"),
            P("head"),
            P(),
            P("seq", None),
            P("seq"),
        ),
        out_specs=P(("seq", "head"), None, None, None),
        check_vma=False,
    )
```

```python
import functools

import jax
import jax.numpy as jnp
from jax import lax
from jax.experimental import pallas as pl
from jax.experimental.pallas import tpu as pltpu
from jax.sharding import PartitionSpec as P

BF16 = jnp.bfloat16
F32 = jnp.float32
CAPACITY = 2
ROWS_BLK = 128
BIG = 1 << 30


def doc_of(positions, doc_ends):
    return jnp.sum((positions[:, None] >= doc_ends[None, :]).astype(jnp.int32), axis=1)


def doc_limit(positions, lengths_ref):
    end = lengths_ref[0]
    limit = jnp.where(positions < end, end, BIG)
    for doc in range(1, lengths_ref.shape[0]):
        end = end + lengths_ref[doc]
        limit = jnp.minimum(limit, jnp.where(positions < end, end, BIG))
    return limit


def params(mib=48):
    return pltpu.CompilerParams(
        dimension_semantics=("arbitrary",), vmem_limit_bytes=mib << 20
    )


SCALARS = pl.BlockSpec(memory_space=pltpu.SMEM)


def local_state_body(rate_ref, lengths_ref, query_ref, grad_ref, out_ref):
    count, dim = out_ref.shape[:2]
    toks = query_ref.shape[0]
    first = lax.axis_index("seq") * toks
    limit = doc_limit(jnp.maximum(first - 1, 0), lengths_ref)
    step = lax.broadcasted_iota(jnp.int32, (toks, dim), 0)
    inside = first + step < limit
    span = (step + 1).astype(F32)
    for h in range(count):
        rate = rate_ref[pl.program_id(0) * count + h]
        cols = slice(h * dim, (h + 1) * dim)
        lead = jnp.where(inside, jnp.exp(-rate * span), 0.0)
        scaled = (query_ref[:, cols].astype(F32) * lead).astype(BF16)
        out_ref[h] = lax.dot_general(
            scaled, grad_ref[:, cols], (((0,), (0,)), ((), ())), preferred_element_type=F32
        ).astype(out_ref.dtype)


def local_states(rates, lengths, queries, grads, count):
    heads = rates.shape[0]
    toks, dim = queries.shape[0], queries.shape[1] // heads
    blk = pl.BlockSpec((toks, count * dim), lambda h: (0, h))
    return pl.pallas_call(
        local_state_body,
        grid=(heads // count,),
        in_specs=[SCALARS, SCALARS, blk, blk],
        out_specs=pl.BlockSpec((count, dim, dim), lambda h: (h, 0, 0)),
        out_shape=jax.ShapeDtypeStruct((heads, dim, dim), BF16),
        compiler_params=params(),
        name="local_states",
    )(rates, lengths, queries, grads)


def within_body(count, rate_ref, lengths_ref, query_ref, key_ref, grad_ref, out_ref):
    toks = query_ref.shape[0]
    dim = query_ref.shape[1] // count
    first = lax.axis_index("seq") * toks
    half = toks // 2
    for lo in (0, half):
        src = lax.broadcasted_iota(jnp.int32, (half, 1), 0) + lo
        dst = lax.broadcasted_iota(jnp.int32, (1, toks - lo), 1) + lo
        limit = doc_limit(src + first, lengths_ref) - first
        seen = (dst >= src) & (dst < limit)
        for h in range(count):
            rate = rate_ref[pl.program_id(0) * count + h]
            cols = slice(h * dim, (h + 1) * dim)
            rise = jnp.exp(rate * src.astype(F32)) * (1.0 / dim)
            fall = jnp.exp(-rate * dst.astype(F32))
            scores = lax.dot_general(
                key_ref[lo : lo + half, cols],
                query_ref[lo:, cols],
                (((1,), (1,)), ((), ())),
                preferred_element_type=F32,
            )
            weights = jnp.where(seen, scores * rise * fall, 0.0).astype(BF16)
            out_ref[lo : lo + half, cols] = jnp.dot(
                weights, grad_ref[lo:, cols], preferred_element_type=F32
            )


def within(rates, lengths, queries, keys, grads, count):
    heads = rates.shape[0]
    toks, dim = queries.shape[0], queries.shape[1] // heads
    blk = pl.BlockSpec((toks, count * dim), lambda h: (0, h))
    return pl.pallas_call(
        functools.partial(within_body, count),
        grid=(heads // count,),
        in_specs=[SCALARS, SCALARS, blk, blk, blk],
        out_specs=blk,
        out_shape=jax.ShapeDtypeStruct((toks, heads * dim), F32),
        compiler_params=params(),
        name="within",
    )(rates, lengths, queries, keys, grads)


def across_body(start, rate_ref, lengths_ref, key_ref, state_ref, intra_ref, out_ref):
    count, dim = state_ref.shape[:2]
    toks = key_ref.shape[0]
    first = lax.axis_index("seq") * toks
    src = lax.broadcasted_iota(jnp.int32, (toks, dim), 0)
    last = first + toks - 1
    inside = last < doc_limit(src + first, lengths_ref)
    span = (toks - 1 - src).astype(F32)
    for h in range(count):
        rate = rate_ref[start + h]
        cols = slice(h * dim, (h + 1) * dim)
        tail = jnp.where(inside, jnp.exp(-rate * span) * (1.0 / dim), 0.0)
        product = jnp.dot(key_ref[:, cols], state_ref[h], preferred_element_type=F32)
        out_ref[:, cols] = (intra_ref[:, cols] + product * tail).astype(BF16)


def across(rates, lengths, keys, states, intra, part, count):
    dim = states.shape[-1]
    toks = keys.shape[0]
    blk = pl.BlockSpec((toks, count * dim), lambda i: (0, part))
    return pl.pallas_call(
        functools.partial(across_body, part * count),
        grid=(1,),
        in_specs=[
            SCALARS,
            SCALARS,
            blk,
            pl.BlockSpec((count, dim, dim), lambda i: (part, 0, 0)),
            blk,
        ],
        out_specs=pl.BlockSpec((toks, count * dim), lambda i: (0, 0)),
        out_shape=jax.ShapeDtypeStruct((toks, count * dim), BF16),
        compiler_params=params(),
        name="across",
    )(rates, lengths, keys, states, intra)


def times(rows, weight):
    return lax.dot_general(
        rows[...], weight[0], (((1,), (1,)), ((), ())), preferred_element_type=F32
    )


def near_body(count, place, *refs):
    out_ref = refs[-1]
    total = None
    for rows, weight in zip(refs[:count], refs[count : 2 * count]):
        part = times(rows, weight)
        total = part if total is None else total + part
    for held in refs[2 * count : -1]:
        total = total + held[...]
    out_ref[...] = total


def project_near(place, pieces, weight, held, tile):
    count = len(pieces)
    toks, half = pieces[0].shape
    width, depth = weight.shape[1:]
    whole = pl.BlockSpec((toks, half), lambda i, p: (0, 0))
    part = pl.BlockSpec((toks, tile), lambda i, p: (0, i))
    return pl.pallas_call(
        functools.partial(near_body, count),
        grid_spec=pltpu.PrefetchScalarGridSpec(
            num_scalar_prefetch=1,
            grid=(width // tile,),
            in_specs=[whole] * count
            + [
                pl.BlockSpec((1, tile, depth), lambda i, p, k=k: (p[k], i, 0))
                for k in range(count)
            ]
            + [part] * len(held),
            out_specs=part,
        ),
        out_shape=jax.ShapeDtypeStruct((toks, width), F32),
        compiler_params=params(),
        name="project_near",
    )(place, *pieces, *[weight] * count, *held)


def far_body(place, pick, lo, hi, weight_lo, weight_hi, near, out_ref):
    total = near[...] + times(lo, weight_lo) + times(hi, weight_hi)
    out_ref[...] = jnp.dot(
        pick[...], total.astype(BF16), preferred_element_type=F32
    ).astype(BF16)


def project_far(place, pick, lo, hi, weight_lo, weight_hi, near, tile):
    toks, half = lo.shape
    slots = pick.shape[0]
    width, depth = weight_lo.shape[1:]
    whole = pl.BlockSpec((toks, half), lambda i, p: (0, 0))
    part = pl.BlockSpec((1, tile, depth), lambda i, p: (p[3], i, 0))
    return pl.pallas_call(
        far_body,
        grid_spec=pltpu.PrefetchScalarGridSpec(
            num_scalar_prefetch=1,
            grid=(width // tile,),
            in_specs=[
                pl.BlockSpec((slots, toks), lambda i, p: (0, 0)),
                whole,
                whole,
                part,
                part,
                pl.BlockSpec((toks, tile), lambda i, p: (0, i)),
            ],
            out_specs=pl.BlockSpec((slots, tile), lambda i, p: (0, i)),
        ),
        out_shape=jax.ShapeDtypeStruct((slots, width), BF16),
        compiler_params=params(),
        name="project_far",
    )(place, pick, lo, hi, weight_lo, weight_hi, near)


def merge_body(column_ref, row_ref, rows_ref, out_ref):
    slots = column_ref.shape[0]
    width = rows_ref.shape[-1]
    same = (column_ref[...] == row_ref[...]) & (column_ref[...] >= 0)
    same = same.astype(F32).astype(BF16)
    rows = rows_ref[...].reshape(slots, width)
    total = jnp.dot(same, rows, preferred_element_type=F32).astype(BF16)
    out_ref[...] = total.reshape(out_ref.shape)


def merge(offsets, got, tile):
    n_seq, n_head, per, width = got.shape
    slots = n_seq * per
    tiles = width // tile
    return pl.pallas_call(
        merge_body,
        grid=(n_head * tiles,),
        in_specs=[
            pl.BlockSpec((slots, 1), lambda i: (0, 0)),
            pl.BlockSpec((1, slots), lambda i: (0, 0)),
            pl.BlockSpec((n_seq, 1, per, tile), lambda i: (0, i // tiles, 0, i % tiles)),
        ],
        out_specs=pl.BlockSpec((1, slots // CAPACITY, CAPACITY, tile), lambda i: (0, 0, 0, i)),
        out_shape=jax.ShapeDtypeStruct((1, slots // CAPACITY, CAPACITY, n_head * width), BF16),
        compiler_params=params(),
        name="merge",
    )(offsets.reshape(slots, 1), offsets.reshape(1, slots), got)


def slots_of(owners, blocks, capacity):
    toks = owners.shape[0]
    width = toks // blocks
    grouped = owners.reshape(blocks, width)
    same_owner = grouped[:, :, None] == grouped[:, None, :]
    lower = jnp.arange(width, dtype=jnp.int32)
    earlier = lower[None, :] < lower[:, None]
    rank = jnp.sum((same_owner & earlier[None]).astype(jnp.int32), axis=2)
    block_ids = jnp.arange(blocks, dtype=jnp.int32)[:, None]
    return ((grouped * blocks + block_ids) * capacity + rank).reshape(toks)


def weight_route(n_seq, n_head):
    plane = n_seq // n_head
    return [
        ((a * plane + p) * n_head + b, (b * plane + p) * n_head + a)
        for a in range(n_head)
        for p in range(plane)
        for b in range(n_head)
    ]


def per_device(
    queries,
    key_vectors,
    output_grad,
    value_weight,
    decay_rate,
    doc_lengths,
    owner_block,
    row_offset,
):
    n_seq = lax.axis_size("seq")
    n_head = lax.axis_size("head")
    devices_all = n_seq * n_head
    tok_rows = queries.shape[0]
    head_local = decay_rate.shape[0]
    head_dim = queries.shape[1] // head_local
    seq_rank = lax.axis_index("seq")
    head_rank = lax.axis_index("head")

    state = local_states(decay_rate, doc_lengths, queries, output_grad, head_local // 2)
    route = weight_route(n_seq, n_head)
    middle = value_weight.shape[1] // 2
    swap_lo = lax.ppermute(value_weight[:, :middle], ("seq", "head"), route)
    state, swap_lo = lax.optimization_barrier((state, swap_lo))
    weight_lo = lax.all_gather(swap_lo, "seq", axis=0, tiled=True)
    weight_lo = weight_lo.reshape(n_head, -1, middle)

    blocks = tok_rows // ROWS_BLK
    per = blocks * CAPACITY
    slot_index = slots_of(owner_block[:, 0], blocks, CAPACITY)
    my_slots = (
        (jnp.arange(n_seq, dtype=jnp.int32)[:, None] * n_head + head_rank) * per
        + jnp.arange(per, dtype=jnp.int32)[None, :]
    )
    hit = my_slots[:, :, None] == slot_index[None, None, :]
    named = jnp.sum(jnp.where(hit, row_offset[None, None, :] + 1, 0), axis=2)
    note = jnp.concatenate([(named // 32).astype(BF16), (named % 32).astype(BF16)], axis=1)
    note = jnp.pad(note[:, None, :], ((0, 0), (0, 7), (0, head_dim - 2 * per)))
    all_slots = jnp.arange(devices_all * per, dtype=jnp.int32)
    pick = (all_slots[:, None] == slot_index[None, :]).astype(BF16)

    share = head_local * head_dim // n_seq
    state_in = lax.all_to_all(
        state.reshape(n_seq, share, head_dim), "seq", split_axis=0, concat_axis=0, tiled=True
    )
    tail, _ = lax.optimization_barrier((value_weight[:, middle:], state_in))
    swap_hi = lax.ppermute(tail, ("seq", "head"), route)
    intra = within(
        decay_rate, doc_lengths, queries, key_vectors, output_grad, head_local // 2
    )

    doc_ends = jnp.cumsum(doc_lengths)
    ranks = jnp.arange(n_seq, dtype=jnp.int32)
    doc_last = doc_of((ranks + 1) * tok_rows - 1, doc_ends)
    doc_prior = doc_of(jnp.maximum(ranks * tok_rows - 1, 0), doc_ends)
    my_rate = decay_rate[seq_rank // (n_seq // head_local)]
    ahead = ranks[None, :] - ranks[:, None] - 1
    reach = (ahead >= 0) & (doc_last[:, None] == doc_prior[None, :])
    chain = jnp.where(
        reach, jnp.exp(-my_rate * (jnp.maximum(ahead, 0) * tok_rows).astype(F32)), 0.0
    )
    carried_all = jnp.einsum(
        "bc,cxy->bxy",
        chain,
        state_in.astype(F32),
        precision=lax.Precision.HIGHEST,
        preferred_element_type=F32,
    ).astype(BF16)
    carried_all = jnp.concatenate([carried_all, note], axis=1)
    carried = lax.all_to_all(
        carried_all,
        "seq",
        split_axis=0,
        concat_axis=0,
        tiled=True,
    )
    swap_hi, carried, intra = lax.optimization_barrier((swap_hi, carried, intra))
    weight_hi = lax.all_gather(swap_hi, "seq", axis=0, tiled=True)
    weight_hi = weight_hi.reshape(n_head, -1, middle)
    offsets = (
        carried[:, share, :per].astype(jnp.int32) * 32
        + carried[:, share, per : 2 * per].astype(jnp.int32)
        - 1
    )
    carried = carried[:, :share].reshape(head_local, head_dim, head_dim)

    own = [
        across(decay_rate, doc_lengths, key_vectors, carried, intra, part, head_local // 2)
        for part in range(2)
    ]
    up = [(i, (i + 1) % n_head) for i in range(n_head)]
    down = [(i, (i - 1) % n_head) for i in range(n_head)]
    left_lo = lax.ppermute(own[0], "head", up)
    right_hi = lax.ppermute(own[1], "head", down)
    left_hi = lax.ppermute(own[1], "head", up)
    right_lo = lax.ppermute(own[0], "head", down)
    far_lo = lax.ppermute(left_lo, "head", up)
    far_hi = lax.ppermute(right_hi, "head", down)
    place = (head_rank + jnp.array([0, n_head - 1, 1, 2], jnp.int32)) % n_head

    near = project_near(place, (own[0], left_lo, right_lo), weight_lo, (), 256)
    near = project_near(place, (own[1], left_hi, right_hi), weight_hi, (near,), 256)
    send = project_far(place, pick, far_lo, far_hi, weight_lo, weight_hi, near, 256)
    send = send.reshape(devices_all, per, -1)
    got = lax.all_to_all(send, ("seq", "head"), split_axis=0, concat_axis=0, tiled=True)
    return merge(offsets, got.reshape(n_seq, n_head, per, -1), 768)


def solution(mesh):
    return jax.shard_map(
        per_device,
        mesh=mesh,
        in_specs=(
            P("seq", "head"),
            P("seq", "head"),
            P("seq", "head"),
            P("seq", "head"),
            P("head"),
            P(),
            P("seq", None),
            P("seq"),
        ),
        out_specs=P(("seq", "head"), None, None, None),
        check_vma=False,
    )
```

```python
import functools

import jax
import jax.numpy as jnp
from jax import lax
from jax.experimental import pallas as pl
from jax.experimental.pallas import tpu as pltpu
from jax.sharding import Mesh, PartitionSpec as P

BF16 = jnp.bfloat16
F32 = jnp.float32
CAPACITY = 2
ROWS_BLK = 128
BIG = 1 << 30
SEQ = ("z", "y", "core")
ALL = ("z", "y", "core", "head")
TURNS = (0, 3, 1, 2)


def doc_of(positions, doc_ends):
    return jnp.sum((positions[:, None] >= doc_ends[None, :]).astype(jnp.int32), axis=1)


def doc_limit(positions, lengths_ref):
    end = lengths_ref[0]
    limit = jnp.where(positions < end, end, BIG)
    for doc in range(1, lengths_ref.shape[0]):
        end = end + lengths_ref[doc]
        limit = jnp.minimum(limit, jnp.where(positions < end, end, BIG))
    return limit


def params(mib=48):
    return pltpu.CompilerParams(
        dimension_semantics=("arbitrary",), vmem_limit_bytes=mib << 20
    )


SCALARS = pl.BlockSpec(memory_space=pltpu.SMEM)


def local_state_body(rate_ref, lengths_ref, query_ref, grad_ref, out_ref):
    count, dim = out_ref.shape[:2]
    toks = query_ref.shape[0]
    first = lax.axis_index(SEQ) * toks
    limit = doc_limit(jnp.maximum(first - 1, 0), lengths_ref)
    step = lax.broadcasted_iota(jnp.int32, (toks, dim), 0)
    inside = first + step < limit
    span = (step + 1).astype(F32)
    for h in range(count):
        rate = rate_ref[pl.program_id(0) * count + h]
        cols = slice(h * dim, (h + 1) * dim)
        lead = jnp.where(inside, jnp.exp(-rate * span), 0.0)
        scaled = (query_ref[:, cols].astype(F32) * lead).astype(BF16)
        out_ref[h] = lax.dot_general(
            scaled, grad_ref[:, cols], (((0,), (0,)), ((), ())), preferred_element_type=F32
        ).astype(out_ref.dtype)


def local_states(rates, lengths, queries, grads, count):
    heads = rates.shape[0]
    toks, dim = queries.shape[0], queries.shape[1] // heads
    blk = pl.BlockSpec((toks, count * dim), lambda h: (0, h))
    return pl.pallas_call(
        local_state_body,
        grid=(heads // count,),
        in_specs=[SCALARS, SCALARS, blk, blk],
        out_specs=pl.BlockSpec((count, dim, dim), lambda h: (h, 0, 0)),
        out_shape=jax.ShapeDtypeStruct((heads, dim, dim), BF16),
        compiler_params=params(),
        name="local_states",
    )(rates, lengths, queries, grads)


def within_body(count, rate_ref, lengths_ref, query_ref, key_ref, grad_ref, out_ref):
    toks = query_ref.shape[0]
    dim = query_ref.shape[1] // count
    first = lax.axis_index(SEQ) * toks
    half = toks // 2
    for lo in (0, half):
        src = lax.broadcasted_iota(jnp.int32, (half, 1), 0) + lo
        dst = lax.broadcasted_iota(jnp.int32, (1, toks - lo), 1) + lo
        limit = doc_limit(src + first, lengths_ref) - first
        seen = (dst >= src) & (dst < limit)
        for h in range(count):
            rate = rate_ref[pl.program_id(0) * count + h]
            cols = slice(h * dim, (h + 1) * dim)
            rise = jnp.exp(rate * src.astype(F32)) * (1.0 / dim)
            fall = jnp.exp(-rate * dst.astype(F32))
            scores = lax.dot_general(
                key_ref[lo : lo + half, cols],
                query_ref[lo:, cols],
                (((1,), (1,)), ((), ())),
                preferred_element_type=F32,
            )
            weights = jnp.where(seen, scores * rise * fall, 0.0).astype(BF16)
            out_ref[lo : lo + half, cols] = jnp.dot(
                weights, grad_ref[lo:, cols], preferred_element_type=F32
            )


def within(rates, lengths, queries, keys, grads, count):
    heads = rates.shape[0]
    toks, dim = queries.shape[0], queries.shape[1] // heads
    blk = pl.BlockSpec((toks, count * dim), lambda h: (0, h))
    return pl.pallas_call(
        functools.partial(within_body, count),
        grid=(heads // count,),
        in_specs=[SCALARS, SCALARS, blk, blk, blk],
        out_specs=blk,
        out_shape=jax.ShapeDtypeStruct((toks, heads * dim), F32),
        compiler_params=params(),
        name="within",
    )(rates, lengths, queries, keys, grads)


def across_body(rate_ref, lengths_ref, key_ref, state_ref, intra_ref, *outs):
    heads, dim = state_ref.shape[:2]
    toks = key_ref.shape[0]
    rows = toks // len(outs)
    first = lax.axis_index(SEQ) * toks
    last = first + toks - 1
    here = lax.axis_index("head")
    for turn, out_ref in enumerate(outs):
        start = pl.multiple_of(lax.rem(here + TURNS[turn], len(outs)) * rows, rows)
        src = lax.broadcasted_iota(jnp.int32, (rows, dim), 0) + start
        inside = last < doc_limit(src + first, lengths_ref)
        span = (toks - 1 - src).astype(F32)
        for h in range(heads):
            cols = slice(h * dim, (h + 1) * dim)
            tail = jnp.where(inside, jnp.exp(-rate_ref[h] * span) * (1.0 / dim), 0.0)
            product = jnp.dot(
                key_ref[pl.ds(start, rows), cols], state_ref[h], preferred_element_type=F32
            )
            out_ref[:, cols] = (intra_ref[pl.ds(start, rows), cols] + product * tail).astype(
                BF16
            )


def across(rates, lengths, keys, states, intra):
    heads, dim = states.shape[:2]
    toks, width = keys.shape
    rows = toks // len(TURNS)
    return pl.pallas_call(
        across_body,
        grid=(1,),
        in_specs=[
            SCALARS,
            SCALARS,
            pl.BlockSpec((toks, width), lambda i: (0, 0)),
            pl.BlockSpec((heads, dim, dim), lambda i: (0, 0, 0)),
            pl.BlockSpec((toks, width), lambda i: (0, 0)),
        ],
        out_specs=[pl.BlockSpec((rows, width), lambda i: (0, 0))] * len(TURNS),
        out_shape=[jax.ShapeDtypeStruct((rows, width), BF16)] * len(TURNS),
        compiler_params=params(),
        name="across",
    )(rates, lengths, keys, states, intra)


def times(rows, weight):
    rows = jnp.concatenate([part[...] for part in rows], axis=0)
    return lax.dot_general(
        rows, weight[0], (((1,), (1,)), ((), ())), preferred_element_type=F32
    )


def near_body(count, place, *refs):
    out_ref = refs[-1]
    each = len(TURNS)
    total = None
    for k in range(count):
        part = times(refs[k * each : (k + 1) * each], refs[count * each + k])
        total = part if total is None else total + part
    for held in refs[count * (each + 1) : -1]:
        total = total + held[...]
    out_ref[...] = total


def project_near(place, pieces, turns, weight, held, tile):
    count = len(pieces)
    rows, depth = pieces[0][0].shape
    toks = rows * len(TURNS)
    width = weight.shape[1]
    whole = pl.BlockSpec((rows, depth), lambda i, p: (0, 0))
    part = pl.BlockSpec((toks, tile), lambda i, p: (0, i))
    return pl.pallas_call(
        functools.partial(near_body, count),
        grid_spec=pltpu.PrefetchScalarGridSpec(
            num_scalar_prefetch=1,
            grid=(width // tile,),
            in_specs=[whole] * (count * len(TURNS))
            + [pl.BlockSpec((1, tile, depth), lambda i, p, k=k: (p[k], i, 0)) for k in turns]
            + [part] * len(held),
            out_specs=part,
        ),
        out_shape=jax.ShapeDtypeStruct((toks, width), F32),
        compiler_params=params(),
        name="project_near",
    )(place, *[q for piece in pieces for q in piece], *[weight] * count, *held)


def far_body(place, pick, *refs):
    weight, near, out_ref = refs[-3:]
    total = near[...] + times(refs[:-3], weight)
    out_ref[...] = jnp.dot(
        pick[...], total.astype(BF16), preferred_element_type=F32
    ).astype(BF16)


def project_far(place, pick, piece, turn, weight, near, tile):
    rows, depth = piece[0].shape
    slots, toks = pick.shape
    width = weight.shape[1]
    whole = pl.BlockSpec((rows, depth), lambda i, p: (0, 0))
    return pl.pallas_call(
        far_body,
        grid_spec=pltpu.PrefetchScalarGridSpec(
            num_scalar_prefetch=1,
            grid=(width // tile,),
            in_specs=[pl.BlockSpec((slots, toks), lambda i, p: (0, 0))]
            + [whole] * len(piece)
            + [
                pl.BlockSpec((1, tile, depth), lambda i, p: (p[turn], i, 0)),
                pl.BlockSpec((toks, tile), lambda i, p: (0, i)),
            ],
            out_specs=pl.BlockSpec((slots, tile), lambda i, p: (0, i)),
        ),
        out_shape=jax.ShapeDtypeStruct((slots, width), BF16),
        compiler_params=params(),
        name="project_far",
    )(place, pick, *piece, weight, near)


def merge_body(column_ref, row_ref, rows_ref, out_ref, same_ref):
    slots = column_ref.shape[0]
    count, width = rows_ref.shape[0], rows_ref.shape[-1]

    @pl.when(pl.program_id(0) == 0)
    def _():
        same = (column_ref[...] == row_ref[...]) & (column_ref[...] >= 0)
        same_ref[...] = same.astype(F32).astype(BF16)

    for j in range(count):
        rows = rows_ref[j].reshape(slots, width)
        total = jnp.dot(same_ref[...], rows, preferred_element_type=F32).astype(BF16)
        out_ref[0, :, :, j * width : (j + 1) * width] = total.reshape(out_ref.shape[1:3] + (width,))


def merge(column, row, got, count):
    parts, n_from, per, width = got.shape
    slots = n_from * per
    return pl.pallas_call(
        merge_body,
        grid=(parts // count,),
        in_specs=[
            pl.BlockSpec((slots, 1), lambda i: (0, 0)),
            pl.BlockSpec((1, slots), lambda i: (0, 0)),
            pl.BlockSpec((count, n_from, per, width), lambda i: (i, 0, 0, 0)),
        ],
        out_specs=pl.BlockSpec(
            (1, slots // CAPACITY, CAPACITY, count * width), lambda i: (0, 0, 0, i)
        ),
        out_shape=jax.ShapeDtypeStruct((1, slots // CAPACITY, CAPACITY, parts * width), BF16),
        scratch_shapes=[pltpu.VMEM((slots, slots), BF16)],
        compiler_params=params(),
        name="merge",
    )(column, row, got)


def slots_of(owners, block_ids):
    blocks, width = owners.shape
    same_owner = owners[:, :, None] == owners[:, None, :]
    lower = jnp.arange(width, dtype=jnp.int32)
    earlier = lower[None, :] < lower[:, None]
    rank = jnp.sum((same_owner & earlier[None]).astype(jnp.int32), axis=2)
    return ((owners * blocks + block_ids[:, None]) * CAPACITY + rank).reshape(blocks * width)


def shift(size, step):
    return [(i, (i + step) % size) for i in range(size)]


def per_device(
    queries,
    key_vectors,
    output_grad,
    value_weight,
    decay_rate,
    doc_lengths,
    owner_block,
    row_offset,
):
    n_z = lax.axis_size("z")
    n_seq = lax.axis_size(SEQ)
    n_head = lax.axis_size("head")
    devices_all = n_seq * n_head
    tok_rows = queries.shape[0]
    head_local = decay_rate.shape[0]
    head_dim = queries.shape[1] // head_local
    seq_rank = lax.axis_index(SEQ)
    head_rank = lax.axis_index("head")
    z_rank = lax.axis_index("z")
    plane = n_seq // n_z
    turns = jnp.array(TURNS, jnp.int32)

    weight = lax.all_gather(value_weight, ("head", "y", "core"), axis=0, tiled=True)
    weight = weight.reshape(n_head, -1, value_weight.shape[1])

    state = local_states(decay_rate, doc_lengths, queries, output_grad, head_local // 2)
    blocks = tok_rows // ROWS_BLK
    per = blocks * CAPACITY
    owners = owner_block[:, 0].reshape(blocks, ROWS_BLK)
    slot_index = slots_of(owners, jnp.arange(blocks, dtype=jnp.int32))
    my_slots = (
        (jnp.arange(n_seq, dtype=jnp.int32)[:, None] * n_head + head_rank) * per
        + jnp.arange(per, dtype=jnp.int32)[None, :]
    )
    hit = my_slots[:, :, None] == slot_index[None, None, :]
    named = jnp.sum(jnp.where(hit, row_offset[None, None, :] + 1, 0), axis=2)
    note = jnp.concatenate([(named // 32).astype(BF16), (named % 32).astype(BF16)], axis=1)
    note = jnp.pad(note[:, None, :], ((0, 0), (0, 0), (0, head_dim - 2 * per)))
    names = lax.dynamic_slice_in_dim(owners, head_rank, 1, 0).astype(BF16)
    names = jnp.broadcast_to(names[None], (n_seq, 1, ROWS_BLK))
    note = jnp.pad(jnp.concatenate([note, names], axis=1), ((0, 0), (0, 6), (0, 0)))

    share = head_local * head_dim // n_seq
    state_in = lax.all_to_all(
        state.reshape(n_seq, share, head_dim), SEQ, split_axis=0, concat_axis=0, tiled=True
    )
    intra = within(
        decay_rate, doc_lengths, queries, key_vectors, output_grad, head_local // 2
    )

    doc_ends = jnp.cumsum(doc_lengths)
    ranks = jnp.arange(n_seq, dtype=jnp.int32)
    doc_last = doc_of((ranks + 1) * tok_rows - 1, doc_ends)
    doc_prior = doc_of(jnp.maximum(ranks * tok_rows - 1, 0), doc_ends)
    my_rate = decay_rate[seq_rank // (n_seq // head_local)]
    ahead = ranks[None, :] - ranks[:, None] - 1
    reach = (ahead >= 0) & (doc_last[:, None] == doc_prior[None, :])
    chain = jnp.where(
        reach, jnp.exp(-my_rate * (jnp.maximum(ahead, 0) * tok_rows).astype(F32)), 0.0
    )
    carried_all = jnp.einsum(
        "bc,cxy->bxy",
        chain,
        state_in.astype(F32),
        precision=lax.Precision.HIGHEST,
        preferred_element_type=F32,
    ).astype(BF16)
    carried = lax.all_to_all(
        jnp.concatenate([carried_all, note], axis=1),
        SEQ,
        split_axis=0,
        concat_axis=0,
        tiled=True,
    )
    offsets = (
        carried[:, share, :per].astype(jnp.int32) * 32
        + carried[:, share, per : 2 * per].astype(jnp.int32)
        - 1
    )
    column = offsets.reshape(-1, 1)
    row = offsets.reshape(n_z, plane, blocks, CAPACITY).transpose(1, 2, 0, 3).reshape(1, -1)
    near_z = (z_rank + turns) % n_z
    theirs = carried[:, share + 1].reshape(n_z, plane, ROWS_BLK)
    theirs = lax.dynamic_slice_in_dim(theirs, seq_rank % plane, 1, 1)[:, 0]
    theirs = theirs[near_z].astype(jnp.int32)
    their_slots = slots_of(theirs, near_z)
    all_slots = jnp.arange(devices_all * per, dtype=jnp.int32)
    pick = (all_slots[:, None] == their_slots[None, :]).astype(BF16)
    carried = carried[:, :share].reshape(head_local, head_dim, head_dim)

    own = across(decay_rate, doc_lengths, key_vectors, carried, intra)
    mine = [own[0]]
    for turn in range(1, len(TURNS)):
        mine.append(lax.ppermute(own[turn], "head", shift(n_head, TURNS[turn])))
    place = (head_rank - turns) % n_head

    pieces = []
    for turn, rows in enumerate(mine):
        below = lax.ppermute(rows, "z", shift(n_z, 1))
        above = lax.ppermute(rows, "z", shift(n_z, -1))
        if turn % 2 == 0:
            across_z = lax.ppermute(below, "z", shift(n_z, 1))
        else:
            across_z = lax.ppermute(above, "z", shift(n_z, -1))
        pieces.append((rows, below, above, across_z))

    near = project_near(place, pieces[:2], (0, 1), weight, (), 256)
    near = project_near(place, pieces[2:3], (2,), weight, (near,), 256)
    send = project_far(place, pick, pieces[3], 3, weight, near, 512)
    send = send.reshape(devices_all, per, -1)
    got = lax.all_to_all(send, ALL, split_axis=0, concat_axis=0, tiled=True)
    got = got.reshape(n_z, plane * n_head, per, -1)
    return merge(column, row, got, 2)


def solution(mesh):
    planes = mesh.shape["head"]
    devices = mesh.devices.reshape(planes, -1, 2, planes)
    return jax.shard_map(
        per_device,
        mesh=Mesh(devices, ALL),
        in_specs=(
            P(SEQ, "head"),
            P(SEQ, "head"),
            P(SEQ, "head"),
            P(SEQ, "head"),
            P("head"),
            P(),
            P(SEQ, None),
            P(SEQ),
        ),
        out_specs=P(ALL, None, None, None),
        check_vma=False,
    )
```

```python
import functools

import jax
import jax.numpy as jnp
from jax import lax
from jax.experimental import pallas as pl
from jax.experimental.pallas import tpu as pltpu
from jax.sharding import Mesh, PartitionSpec as P

BF16 = jnp.bfloat16
F32 = jnp.float32
CAPACITY = 2
ROWS_BLK = 128
BIG = 1 << 30
SEQ = ("z", "y", "core")
ALL = ("z", "y", "core", "head")
TURNS = (0, 3, 1, 2)


def doc_of(positions, doc_ends):
    return jnp.sum((positions[:, None] >= doc_ends[None, :]).astype(jnp.int32), axis=1)


def doc_limit(positions, lengths_ref):
    end = lengths_ref[0]
    limit = jnp.where(positions < end, end, BIG)
    for doc in range(1, lengths_ref.shape[0]):
        end = end + lengths_ref[doc]
        limit = jnp.minimum(limit, jnp.where(positions < end, end, BIG))
    return limit


def params(mib=48):
    return pltpu.CompilerParams(
        dimension_semantics=("arbitrary",), vmem_limit_bytes=mib << 20
    )


SCALARS = pl.BlockSpec(memory_space=pltpu.SMEM)


def local_state_body(rate_ref, lengths_ref, query_ref, grad_ref, out_ref):
    count, dim = out_ref.shape[:2]
    toks = query_ref.shape[0]
    first = lax.axis_index(SEQ) * toks
    limit = doc_limit(jnp.maximum(first - 1, 0), lengths_ref)
    step = lax.broadcasted_iota(jnp.int32, (toks, dim), 0)
    inside = first + step < limit
    span = (step + 1).astype(F32)
    for h in range(count):
        rate = rate_ref[pl.program_id(0) * count + h]
        cols = slice(h * dim, (h + 1) * dim)
        lead = jnp.where(inside, jnp.exp(-rate * span), 0.0)
        scaled = (query_ref[:, cols].astype(F32) * lead).astype(BF16)
        out_ref[h] = lax.dot_general(
            scaled, grad_ref[:, cols], (((0,), (0,)), ((), ())), preferred_element_type=F32
        ).astype(out_ref.dtype)


def local_states(rates, lengths, queries, grads, count):
    heads = rates.shape[0]
    toks, dim = queries.shape[0], queries.shape[1] // heads
    blk = pl.BlockSpec((toks, count * dim), lambda h: (0, h))
    return pl.pallas_call(
        local_state_body,
        grid=(heads // count,),
        in_specs=[SCALARS, SCALARS, blk, blk],
        out_specs=pl.BlockSpec((count, dim, dim), lambda h: (h, 0, 0)),
        out_shape=jax.ShapeDtypeStruct((heads, dim, dim), BF16),
        compiler_params=params(),
        name="local_states",
    )(rates, lengths, queries, grads)


def within_body(count, rate_ref, lengths_ref, query_ref, key_ref, grad_ref, out_ref):
    toks = query_ref.shape[0]
    dim = query_ref.shape[1] // count
    first = lax.axis_index(SEQ) * toks
    half = toks // 2
    for lo in (0, half):
        src = lax.broadcasted_iota(jnp.int32, (half, 1), 0) + lo
        dst = lax.broadcasted_iota(jnp.int32, (1, toks - lo), 1) + lo
        limit = doc_limit(src + first, lengths_ref) - first
        seen = (dst >= src) & (dst < limit)
        for h in range(count):
            rate = rate_ref[pl.program_id(0) * count + h]
            cols = slice(h * dim, (h + 1) * dim)
            rise = jnp.exp(rate * src.astype(F32)) * (1.0 / dim)
            fall = jnp.exp(-rate * dst.astype(F32))
            scores = lax.dot_general(
                key_ref[lo : lo + half, cols],
                query_ref[lo:, cols],
                (((1,), (1,)), ((), ())),
                preferred_element_type=F32,
            )
            weights = jnp.where(seen, scores * rise * fall, 0.0).astype(BF16)
            out_ref[lo : lo + half, cols] = jnp.dot(
                weights, grad_ref[lo:, cols], preferred_element_type=F32
            )


def within(rates, lengths, queries, keys, grads, count):
    heads = rates.shape[0]
    toks, dim = queries.shape[0], queries.shape[1] // heads
    blk = pl.BlockSpec((toks, count * dim), lambda h: (0, h))
    return pl.pallas_call(
        functools.partial(within_body, count),
        grid=(heads // count,),
        in_specs=[SCALARS, SCALARS, blk, blk, blk],
        out_specs=blk,
        out_shape=jax.ShapeDtypeStruct((toks, heads * dim), F32),
        compiler_params=params(),
        name="within",
    )(rates, lengths, queries, keys, grads)


def across_body(rate_ref, lengths_ref, key_ref, state_ref, intra_ref, *outs):
    heads, dim = state_ref.shape[:2]
    toks = key_ref.shape[0]
    rows = toks // len(outs)
    first = lax.axis_index(SEQ) * toks
    last = first + toks - 1
    here = lax.axis_index("head")
    for turn, out_ref in enumerate(outs):
        start = pl.multiple_of(lax.rem(here + TURNS[turn], len(outs)) * rows, rows)
        src = lax.broadcasted_iota(jnp.int32, (rows, dim), 0) + start
        inside = last < doc_limit(src + first, lengths_ref)
        span = (toks - 1 - src).astype(F32)
        for h in range(heads):
            cols = slice(h * dim, (h + 1) * dim)
            tail = jnp.where(inside, jnp.exp(-rate_ref[h] * span) * (1.0 / dim), 0.0)
            product = jnp.dot(
                key_ref[pl.ds(start, rows), cols], state_ref[h], preferred_element_type=F32
            )
            out_ref[:, cols] = (intra_ref[pl.ds(start, rows), cols] + product * tail).astype(
                BF16
            )


def across(rates, lengths, keys, states, intra):
    heads, dim = states.shape[:2]
    toks, width = keys.shape
    rows = toks // len(TURNS)
    return pl.pallas_call(
        across_body,
        grid=(1,),
        in_specs=[
            SCALARS,
            SCALARS,
            pl.BlockSpec((toks, width), lambda i: (0, 0)),
            pl.BlockSpec((heads, dim, dim), lambda i: (0, 0, 0)),
            pl.BlockSpec((toks, width), lambda i: (0, 0)),
        ],
        out_specs=[pl.BlockSpec((rows, width), lambda i: (0, 0))] * len(TURNS),
        out_shape=[jax.ShapeDtypeStruct((rows, width), BF16)] * len(TURNS),
        compiler_params=params(),
        name="across",
    )(rates, lengths, keys, states, intra)


def times(rows, weight):
    rows = jnp.concatenate([part[...] for part in rows], axis=0)
    return lax.dot_general(
        rows, weight[0], (((1,), (1,)), ((), ())), preferred_element_type=F32
    )


def project_body(turns, place, pick, *refs):
    out_ref = refs[-1]
    total = None
    for k in range(turns):
        part = times(refs[k * turns : (k + 1) * turns], refs[turns * turns + k])
        total = part if total is None else total + part
    out_ref[...] = jnp.dot(
        pick[...], total.astype(BF16), preferred_element_type=F32
    ).astype(BF16)


def project(place, pick, pieces, weight, tile):
    turns = len(pieces)
    rows, depth = pieces[0][0].shape
    slots, toks = pick.shape
    width = weight.shape[1]
    whole = pl.BlockSpec((rows, depth), lambda i, p: (0, 0))
    return pl.pallas_call(
        functools.partial(project_body, turns),
        grid_spec=pltpu.PrefetchScalarGridSpec(
            num_scalar_prefetch=1,
            grid=(width // tile,),
            in_specs=[pl.BlockSpec((slots, toks), lambda i, p: (0, 0))]
            + [whole] * (turns * turns)
            + [
                pl.BlockSpec((1, tile, depth), lambda i, p, k=k: (p[k], i, 0))
                for k in range(turns)
            ],
            out_specs=pl.BlockSpec((slots, tile), lambda i, p: (0, i)),
        ),
        out_shape=pltpu.HBM((slots, width), BF16),
        compiler_params=params(),
        name="project",
    )(place, pick, *[q for piece in pieces for q in piece], *[weight] * turns)


def merge_body(column_ref, row_ref, rows_ref, out_ref, same_ref):
    slots = column_ref.shape[0]
    count, width = rows_ref.shape[0], rows_ref.shape[-1]

    @pl.when(pl.program_id(0) == 0)
    def _():
        same = (column_ref[...] == row_ref[...]) & (column_ref[...] >= 0)
        same_ref[...] = same.astype(F32).astype(BF16)

    for j in range(count):
        rows = rows_ref[j].reshape(slots, width)
        total = jnp.dot(same_ref[...], rows, preferred_element_type=F32).astype(BF16)
        out_ref[0, :, :, j * width : (j + 1) * width] = total.reshape(out_ref.shape[1:3] + (width,))


def merge(column, row, got, count):
    parts, n_from, per, width = got.shape
    slots = n_from * per
    return pl.pallas_call(
        merge_body,
        grid=(parts // count,),
        in_specs=[
            pl.BlockSpec((slots, 1), lambda i: (0, 0)),
            pl.BlockSpec((1, slots), lambda i: (0, 0)),
            pl.BlockSpec((count, n_from, per, width), lambda i: (i, 0, 0, 0)),
        ],
        out_specs=pl.BlockSpec(
            (1, slots // CAPACITY, CAPACITY, count * width), lambda i: (0, 0, 0, i)
        ),
        out_shape=jax.ShapeDtypeStruct((1, slots // CAPACITY, CAPACITY, parts * width), BF16),
        scratch_shapes=[pltpu.VMEM((slots, slots), BF16)],
        compiler_params=params(),
        name="merge",
    )(column, row, got)


def slots_of(owners, block_ids):
    blocks, width = owners.shape
    same_owner = owners[:, :, None] == owners[:, None, :]
    lower = jnp.arange(width, dtype=jnp.int32)
    earlier = lower[None, :] < lower[:, None]
    rank = jnp.sum((same_owner & earlier[None]).astype(jnp.int32), axis=2)
    return ((owners * blocks + block_ids[:, None]) * CAPACITY + rank).reshape(blocks * width)


def shift(size, step):
    return [(i, (i + step) % size) for i in range(size)]


def per_device(
    queries,
    key_vectors,
    output_grad,
    value_weight,
    decay_rate,
    doc_lengths,
    owner_block,
    row_offset,
):
    n_z = lax.axis_size("z")
    n_seq = lax.axis_size(SEQ)
    n_head = lax.axis_size("head")
    devices_all = n_seq * n_head
    tok_rows = queries.shape[0]
    head_local = decay_rate.shape[0]
    head_dim = queries.shape[1] // head_local
    seq_rank = lax.axis_index(SEQ)
    head_rank = lax.axis_index("head")
    z_rank = lax.axis_index("z")
    plane = n_seq // n_z
    turns = jnp.array(TURNS, jnp.int32)

    weight = lax.all_gather(value_weight, ("head", "y", "core"), axis=0, tiled=True)
    weight = weight.reshape(n_head, -1, value_weight.shape[1])

    queries, key_vectors, output_grad = (
        pltpu.with_memory_space_constraint(array, pltpu.HBM)
        for array in (queries, key_vectors, output_grad)
    )
    state = local_states(decay_rate, doc_lengths, queries, output_grad, head_local // 2)
    blocks = tok_rows // ROWS_BLK
    per = blocks * CAPACITY
    owners = owner_block[:, 0].reshape(blocks, ROWS_BLK)
    slot_index = slots_of(owners, jnp.arange(blocks, dtype=jnp.int32))
    my_slots = (
        (jnp.arange(n_seq, dtype=jnp.int32)[:, None] * n_head + head_rank) * per
        + jnp.arange(per, dtype=jnp.int32)[None, :]
    )
    hit = my_slots[:, :, None] == slot_index[None, None, :]
    named = jnp.sum(jnp.where(hit, row_offset[None, None, :] + 1, 0), axis=2)
    note = jnp.concatenate([(named // 32).astype(BF16), (named % 32).astype(BF16)], axis=1)
    note = jnp.pad(note[:, None, :], ((0, 0), (0, 0), (0, head_dim - 2 * per)))
    names = lax.dynamic_slice_in_dim(owners, head_rank, 1, 0).astype(BF16)
    names = jnp.broadcast_to(names[None], (n_seq, 1, ROWS_BLK))
    note = jnp.pad(jnp.concatenate([note, names], axis=1), ((0, 0), (0, 6), (0, 0)))

    share = head_local * head_dim // n_seq
    state_in = lax.all_to_all(
        state.reshape(n_seq, share, head_dim), SEQ, split_axis=0, concat_axis=0, tiled=True
    )
    intra = within(
        decay_rate, doc_lengths, queries, key_vectors, output_grad, head_local // 2
    )

    state_in, intra = lax.optimization_barrier((state_in, intra))
    doc_ends = jnp.cumsum(doc_lengths)
    ranks = jnp.arange(n_seq, dtype=jnp.int32)
    doc_last = doc_of((ranks + 1) * tok_rows - 1, doc_ends)
    doc_prior = doc_of(jnp.maximum(ranks * tok_rows - 1, 0), doc_ends)
    my_rate = decay_rate[seq_rank // (n_seq // head_local)]
    ahead = ranks[None, :] - ranks[:, None] - 1
    reach = (ahead >= 0) & (doc_last[:, None] == doc_prior[None, :])
    chain = jnp.where(
        reach, jnp.exp(-my_rate * (jnp.maximum(ahead, 0) * tok_rows).astype(F32)), 0.0
    )
    carried_all = jnp.einsum(
        "bc,cxy->bxy",
        chain,
        state_in.astype(F32),
        precision=lax.Precision.HIGHEST,
        preferred_element_type=F32,
    ).astype(BF16)
    carried = lax.all_to_all(
        jnp.concatenate([carried_all, note], axis=1),
        SEQ,
        split_axis=0,
        concat_axis=0,
        tiled=True,
    )
    offsets = (
        carried[:, share, :per].astype(jnp.int32) * 32
        + carried[:, share, per : 2 * per].astype(jnp.int32)
        - 1
    )
    column = offsets.reshape(-1, 1)
    row = offsets.reshape(n_z, plane, blocks, CAPACITY).transpose(1, 2, 0, 3).reshape(1, -1)
    near_z = (z_rank + turns) % n_z
    theirs = carried[:, share + 1].reshape(n_z, plane, ROWS_BLK)
    theirs = lax.dynamic_slice_in_dim(theirs, seq_rank % plane, 1, 1)[:, 0]
    theirs = theirs[near_z].astype(jnp.int32)
    their_slots = slots_of(theirs, near_z)
    all_slots = jnp.arange(devices_all * per, dtype=jnp.int32)
    pick = (all_slots[:, None] == their_slots[None, :]).astype(BF16)
    carried = carried[:, :share].reshape(head_local, head_dim, head_dim)

    own = across(decay_rate, doc_lengths, key_vectors, carried, intra)
    mine = [own[0]]
    for turn in range(1, len(TURNS)):
        mine.append(lax.ppermute(own[turn], "head", shift(n_head, TURNS[turn])))
    place = (head_rank - turns) % n_head

    pieces = []
    for turn, rows in enumerate(mine):
        below = lax.ppermute(rows, "z", shift(n_z, 1))
        above = lax.ppermute(rows, "z", shift(n_z, -1))
        if turn % 2 == 0:
            across_z = lax.ppermute(below, "z", shift(n_z, 1))
        else:
            across_z = lax.ppermute(above, "z", shift(n_z, -1))
        group = (rows, below, above, across_z)
        pieces.append([pltpu.with_memory_space_constraint(q, pltpu.HBM) for q in group])

    send = project(place, pick, pieces, weight, 512)
    send = send.reshape(devices_all, per, -1)
    got = lax.all_to_all(send, ALL, split_axis=0, concat_axis=0, tiled=True)
    got = got.reshape(n_z, plane * n_head, per, -1)
    return merge(column, row, got, 2)


def solution(mesh):
    planes = mesh.shape["head"]
    devices = mesh.devices.reshape(planes, -1, 2, planes)
    return jax.shard_map(
        per_device,
        mesh=Mesh(devices, ALL),
        in_specs=(
            P(SEQ, "head"),
            P(SEQ, "head"),
            P(SEQ, "head"),
            P(SEQ, "head"),
            P("head"),
            P(),
            P(SEQ, None),
            P(SEQ),
        ),
        out_specs=P(ALL, None, None, None),
        check_vma=False,
    )
```

```python
import functools

import jax
import jax.numpy as jnp
from jax import lax
from jax.experimental import pallas as pl
from jax.experimental.pallas import tpu as pltpu
from jax.sharding import Mesh, PartitionSpec as P

BF16 = jnp.bfloat16
F32 = jnp.float32
CAPACITY = 2
ROWS_BLK = 128
BIG = 1 << 30
SEQ = ("z", "y", "core")
ALL = ("z", "y", "core", "head")
TURNS = (0, 3, 1, 2)
ZTURNS = (1, 3, 2)


def doc_of(positions, doc_ends):
    return jnp.sum((positions[:, None] >= doc_ends[None, :]).astype(jnp.int32), axis=1)


def doc_limit(positions, lengths_ref):
    end = lengths_ref[0]
    limit = jnp.where(positions < end, end, BIG)
    for doc in range(1, lengths_ref.shape[0]):
        end = end + lengths_ref[doc]
        limit = jnp.minimum(limit, jnp.where(positions < end, end, BIG))
    return limit


def params(mib=48):
    return pltpu.CompilerParams(
        dimension_semantics=("arbitrary",), vmem_limit_bytes=mib << 20
    )


SCALARS = pl.BlockSpec(memory_space=pltpu.SMEM)


def local_state_body(rate_ref, lengths_ref, query_ref, grad_ref, out_ref):
    count, dim = out_ref.shape[:2]
    toks = query_ref.shape[0]
    first = lax.axis_index(SEQ) * toks
    limit = doc_limit(jnp.maximum(first - 1, 0), lengths_ref)
    step = lax.broadcasted_iota(jnp.int32, (toks, dim), 0)
    inside = first + step < limit
    span = (step + 1).astype(F32)
    for h in range(count):
        rate = rate_ref[pl.program_id(0) * count + h]
        cols = slice(h * dim, (h + 1) * dim)
        lead = jnp.where(inside, jnp.exp(-rate * span), 0.0)
        scaled = (query_ref[:, cols].astype(F32) * lead).astype(BF16)
        out_ref[h] = lax.dot_general(
            scaled, grad_ref[:, cols], (((0,), (0,)), ((), ())), preferred_element_type=F32
        ).astype(out_ref.dtype)


def local_states(rates, lengths, queries, grads, count):
    heads = rates.shape[0]
    toks, dim = queries.shape[0], queries.shape[1] // heads
    blk = pl.BlockSpec((toks, count * dim), lambda h: (0, h))
    return pl.pallas_call(
        local_state_body,
        grid=(heads // count,),
        in_specs=[SCALARS, SCALARS, blk, blk],
        out_specs=pl.BlockSpec((count, dim, dim), lambda h: (h, 0, 0)),
        out_shape=jax.ShapeDtypeStruct((heads, dim, dim), BF16),
        compiler_params=params(),
        name="local_states",
    )(rates, lengths, queries, grads)


def within_body(count, rate_ref, lengths_ref, query_ref, key_ref, grad_ref, out_ref):
    toks = query_ref.shape[0]
    dim = query_ref.shape[1] // count
    first = lax.axis_index(SEQ) * toks
    half = toks // 2
    for lo in (0, half):
        src = lax.broadcasted_iota(jnp.int32, (half, 1), 0) + lo
        dst = lax.broadcasted_iota(jnp.int32, (1, toks - lo), 1) + lo
        limit = doc_limit(src + first, lengths_ref) - first
        seen = (dst >= src) & (dst < limit)
        for h in range(count):
            rate = rate_ref[pl.program_id(0) * count + h]
            cols = slice(h * dim, (h + 1) * dim)
            rise = jnp.exp(rate * src.astype(F32)) * (1.0 / dim)
            fall = jnp.exp(-rate * dst.astype(F32))
            scores = lax.dot_general(
                key_ref[lo : lo + half, cols],
                query_ref[lo:, cols],
                (((1,), (1,)), ((), ())),
                preferred_element_type=F32,
            )
            weights = jnp.where(seen, scores * rise * fall, 0.0).astype(BF16)
            out_ref[lo : lo + half, cols] = jnp.dot(
                weights, grad_ref[lo:, cols], preferred_element_type=F32
            )


def within(rates, lengths, queries, keys, grads, count):
    heads = rates.shape[0]
    toks, dim = queries.shape[0], queries.shape[1] // heads
    blk = pl.BlockSpec((toks, count * dim), lambda h: (0, h))
    return pl.pallas_call(
        functools.partial(within_body, count),
        grid=(heads // count,),
        in_specs=[SCALARS, SCALARS, blk, blk, blk],
        out_specs=blk,
        out_shape=jax.ShapeDtypeStruct((toks, heads * dim), F32),
        compiler_params=params(),
        name="within",
    )(rates, lengths, queries, keys, grads)


def across_body(rate_ref, lengths_ref, key_ref, state_ref, intra_ref, *outs):
    heads, dim = state_ref.shape[:2]
    toks = key_ref.shape[0]
    rows = toks // len(outs)
    first = lax.axis_index(SEQ) * toks
    last = first + toks - 1
    here = lax.axis_index("head")
    for turn, out_ref in enumerate(outs):
        start = pl.multiple_of(lax.rem(here + TURNS[turn], len(outs)) * rows, rows)
        src = lax.broadcasted_iota(jnp.int32, (rows, dim), 0) + start
        inside = last < doc_limit(src + first, lengths_ref)
        span = (toks - 1 - src).astype(F32)
        for h in range(heads):
            cols = slice(h * dim, (h + 1) * dim)
            tail = jnp.where(inside, jnp.exp(-rate_ref[h] * span) * (1.0 / dim), 0.0)
            product = jnp.dot(
                key_ref[pl.ds(start, rows), cols], state_ref[h], preferred_element_type=F32
            )
            out_ref[:, cols] = (intra_ref[pl.ds(start, rows), cols] + product * tail).astype(
                BF16
            )


def across(rates, lengths, keys, states, intra):
    heads, dim = states.shape[:2]
    toks, width = keys.shape
    rows = toks // len(TURNS)
    return pl.pallas_call(
        across_body,
        grid=(1,),
        in_specs=[
            SCALARS,
            SCALARS,
            pl.BlockSpec((toks, width), lambda i: (0, 0)),
            pl.BlockSpec((heads, dim, dim), lambda i: (0, 0, 0)),
            pl.BlockSpec((toks, width), lambda i: (0, 0)),
        ],
        out_specs=[pl.BlockSpec((rows, width), lambda i: (0, 0))] * len(TURNS),
        out_shape=[jax.ShapeDtypeStruct((rows, width), BF16)] * len(TURNS),
        compiler_params=params(),
        name="across",
    )(rates, lengths, keys, states, intra)


def times(rows, weight):
    rows = jnp.concatenate([part[...] for part in rows], axis=0)
    return lax.dot_general(
        rows, weight[0], (((1,), (1,)), ((), ())), preferred_element_type=F32
    )


def near_body(count, place, *refs):
    out_ref = refs[-1]
    each = len(TURNS)
    total = None
    for k in range(count):
        part = times(refs[k * each : (k + 1) * each], refs[count * each + k])
        total = part if total is None else total + part
    for held in refs[count * (each + 1) : -1]:
        total = total + held[...]
    out_ref[...] = total


def project_near(place, pieces, turns, weight, held, tile):
    count = len(pieces)
    rows, depth = pieces[0][0].shape
    toks = rows * len(TURNS)
    width = weight.shape[1]
    whole = pl.BlockSpec((rows, depth), lambda i, p: (0, 0))
    part = pl.BlockSpec((toks, tile), lambda i, p: (0, i))
    return pl.pallas_call(
        functools.partial(near_body, count),
        grid_spec=pltpu.PrefetchScalarGridSpec(
            num_scalar_prefetch=1,
            grid=(width // tile,),
            in_specs=[whole] * (count * len(TURNS))
            + [pl.BlockSpec((1, tile, depth), lambda i, p, k=k: (p[k], i, 0)) for k in turns]
            + [part] * len(held),
            out_specs=part,
        ),
        out_shape=pltpu.HBM((toks, width), F32),
        compiler_params=params(),
        name="project_near",
    )(place, *[q for piece in pieces for q in piece], *[weight] * count, *held)


def far_body(place, pick, *refs):
    weight, near, out_ref = refs[-3:]
    total = near[...] + times(refs[:-3], weight)
    out_ref[...] = jnp.dot(
        pick[...], total.astype(BF16), preferred_element_type=F32
    ).astype(BF16)


def project_far(place, pick, piece, turn, weight, near, tile):
    rows, depth = piece[0].shape
    slots, toks = pick.shape
    width = weight.shape[1]
    whole = pl.BlockSpec((rows, depth), lambda i, p: (0, 0))
    return pl.pallas_call(
        far_body,
        grid_spec=pltpu.PrefetchScalarGridSpec(
            num_scalar_prefetch=1,
            grid=(width // tile,),
            in_specs=[pl.BlockSpec((slots, toks), lambda i, p: (0, 0))]
            + [whole] * len(piece)
            + [
                pl.BlockSpec((1, tile, depth), lambda i, p: (p[turn], i, 0)),
                pl.BlockSpec((toks, tile), lambda i, p: (0, i)),
            ],
            out_specs=pl.BlockSpec((slots, tile), lambda i, p: (0, i)),
        ),
        out_shape=pltpu.HBM((slots, width), BF16),
        compiler_params=params(),
        name="project_far",
    )(place, pick, *piece, weight, near)


def merge_body(column_ref, row_ref, rows_ref, out_ref, same_ref):
    slots = column_ref.shape[0]
    count, width = rows_ref.shape[0], rows_ref.shape[-1]

    @pl.when(pl.program_id(0) == 0)
    def _():
        same = (column_ref[...] == row_ref[...]) & (column_ref[...] >= 0)
        same_ref[...] = same.astype(F32).astype(BF16)

    for j in range(count):
        rows = rows_ref[j].reshape(slots, width)
        total = jnp.dot(same_ref[...], rows, preferred_element_type=F32).astype(BF16)
        out_ref[0, :, :, j * width : (j + 1) * width] = total.reshape(out_ref.shape[1:3] + (width,))


def merge(column, row, got, count):
    parts, n_from, per, width = got.shape
    slots = n_from * per
    return pl.pallas_call(
        merge_body,
        grid=(parts // count,),
        in_specs=[
            pl.BlockSpec((slots, 1), lambda i: (0, 0)),
            pl.BlockSpec((1, slots), lambda i: (0, 0)),
            pl.BlockSpec((count, n_from, per, width), lambda i: (i, 0, 0, 0)),
        ],
        out_specs=pl.BlockSpec(
            (1, slots // CAPACITY, CAPACITY, count * width), lambda i: (0, 0, 0, i)
        ),
        out_shape=jax.ShapeDtypeStruct((1, slots // CAPACITY, CAPACITY, parts * width), BF16),
        scratch_shapes=[pltpu.VMEM((slots, slots), BF16)],
        compiler_params=params(),
        name="merge",
    )(column, row, got)


def slots_of(owners, block_ids):
    blocks, width = owners.shape
    same_owner = owners[:, :, None] == owners[:, None, :]
    lower = jnp.arange(width, dtype=jnp.int32)
    earlier = lower[None, :] < lower[:, None]
    rank = jnp.sum((same_owner & earlier[None]).astype(jnp.int32), axis=2)
    return ((owners * blocks + block_ids[:, None]) * CAPACITY + rank).reshape(blocks * width)


def shift(size, step):
    return [(i, (i + step) % size) for i in range(size)]


def per_device(
    queries,
    key_vectors,
    output_grad,
    value_weight,
    decay_rate,
    doc_lengths,
    owner_block,
    row_offset,
):
    n_z = lax.axis_size("z")
    n_seq = lax.axis_size(SEQ)
    n_head = lax.axis_size("head")
    devices_all = n_seq * n_head
    tok_rows = queries.shape[0]
    head_local = decay_rate.shape[0]
    head_dim = queries.shape[1] // head_local
    seq_rank = lax.axis_index(SEQ)
    head_rank = lax.axis_index("head")
    z_rank = lax.axis_index("z")
    plane = n_seq // n_z
    turns = jnp.array(TURNS, jnp.int32)

    weight = lax.all_gather(value_weight, ("head", "y", "core"), axis=0, tiled=True)
    weight = weight.reshape(n_head, -1, value_weight.shape[1])

    queries, key_vectors, output_grad = (
        pltpu.with_memory_space_constraint(array, pltpu.HBM)
        for array in (queries, key_vectors, output_grad)
    )
    state = local_states(decay_rate, doc_lengths, queries, output_grad, head_local // 2)
    blocks = tok_rows // ROWS_BLK
    per = blocks * CAPACITY
    owners = owner_block[:, 0].reshape(blocks, ROWS_BLK)
    slot_index = slots_of(owners, jnp.arange(blocks, dtype=jnp.int32))
    my_slots = (
        (jnp.arange(n_seq, dtype=jnp.int32)[:, None] * n_head + head_rank) * per
        + jnp.arange(per, dtype=jnp.int32)[None, :]
    )
    hit = my_slots[:, :, None] == slot_index[None, None, :]
    named = jnp.sum(jnp.where(hit, row_offset[None, None, :] + 1, 0), axis=2)
    note = jnp.concatenate([(named // 32).astype(BF16), (named % 32).astype(BF16)], axis=1)
    note = jnp.pad(note[:, None, :], ((0, 0), (0, 0), (0, head_dim - 2 * per)))
    names = lax.dynamic_slice_in_dim(owners, head_rank, 1, 0).astype(BF16)
    names = jnp.broadcast_to(names[None], (n_seq, 1, ROWS_BLK))
    note = jnp.pad(jnp.concatenate([note, names], axis=1), ((0, 0), (0, 6), (0, 0)))

    share = head_local * head_dim // n_seq
    state_in = lax.all_to_all(
        state.reshape(n_seq, share, head_dim), SEQ, split_axis=0, concat_axis=0, tiled=True
    )
    intra = within(
        decay_rate, doc_lengths, queries, key_vectors, output_grad, head_local // 2
    )

    state_in, intra = lax.optimization_barrier((state_in, intra))
    doc_ends = jnp.cumsum(doc_lengths)
    ranks = jnp.arange(n_seq, dtype=jnp.int32)
    doc_last = doc_of((ranks + 1) * tok_rows - 1, doc_ends)
    doc_prior = doc_of(jnp.maximum(ranks * tok_rows - 1, 0), doc_ends)
    my_rate = decay_rate[seq_rank // (n_seq // head_local)]
    ahead = ranks[None, :] - ranks[:, None] - 1
    reach = (ahead >= 0) & (doc_last[:, None] == doc_prior[None, :])
    chain = jnp.where(
        reach, jnp.exp(-my_rate * (jnp.maximum(ahead, 0) * tok_rows).astype(F32)), 0.0
    )
    carried_all = jnp.einsum(
        "bc,cxy->bxy",
        chain,
        state_in.astype(F32),
        precision=lax.Precision.HIGHEST,
        preferred_element_type=F32,
    ).astype(BF16)
    carried = lax.all_to_all(
        jnp.concatenate([carried_all, note], axis=1),
        SEQ,
        split_axis=0,
        concat_axis=0,
        tiled=True,
    )
    offsets = (
        carried[:, share, :per].astype(jnp.int32) * 32
        + carried[:, share, per : 2 * per].astype(jnp.int32)
        - 1
    )
    column = offsets.reshape(-1, 1)
    row = offsets.reshape(n_z, plane, blocks, CAPACITY).transpose(1, 2, 0, 3).reshape(1, -1)
    near_z = (z_rank - jnp.array((0,) + ZTURNS, jnp.int32)) % n_z
    theirs = carried[:, share + 1].reshape(n_z, plane, ROWS_BLK)
    theirs = lax.dynamic_slice_in_dim(theirs, seq_rank % plane, 1, 1)[:, 0]
    theirs = theirs[near_z].astype(jnp.int32)
    their_slots = slots_of(theirs, near_z)
    all_slots = jnp.arange(devices_all * per, dtype=jnp.int32)
    pick = (all_slots[:, None] == their_slots[None, :]).astype(BF16)
    carried = carried[:, :share].reshape(head_local, head_dim, head_dim)

    own = across(decay_rate, doc_lengths, key_vectors, carried, intra)
    mine = [own[0]]
    for turn in range(1, len(TURNS)):
        mine.append(lax.ppermute(own[turn], "head", shift(n_head, TURNS[turn])))
    place = (head_rank - turns) % n_head

    def spread(rows, flip):
        below = lax.ppermute(rows, "z", shift(n_z, 1))
        above = lax.ppermute(rows, "z", shift(n_z, -1))
        relay = lax.ppermute(above if flip else below, "z", shift(n_z, -1 if flip else 1))
        return rows, below, above, relay

    groups = [spread(mine[0], False)]
    mine[1], *_ = lax.optimization_barrier((mine[1],) + groups[0][1:3])
    groups.append(spread(mine[1], True))
    mine[2], mine[3], _ = lax.optimization_barrier((mine[2], mine[3], groups[0][3]))
    groups.append(spread(mine[2], False))
    groups.append(spread(mine[3], True))
    pieces = [
        [pltpu.with_memory_space_constraint(q, pltpu.HBM) for q in group] for group in groups
    ]

    near = project_near(place, pieces[:2], (0, 1), weight, (), 512)
    near = project_near(place, pieces[2:3], (2,), weight, (near,), 512)
    send = project_far(place, pick, pieces[3], 3, weight, near, 512)
    send = send.reshape(devices_all, per, -1)
    got = lax.all_to_all(send, ALL, split_axis=0, concat_axis=0, tiled=True)
    got = got.reshape(n_z, plane * n_head, per, -1)
    return merge(column, row, got, 2)


def solution(mesh):
    planes = mesh.shape["head"]
    devices = mesh.devices.reshape(planes, -1, 2, planes)
    return jax.shard_map(
        per_device,
        mesh=Mesh(devices, ALL),
        in_specs=(
            P(SEQ, "head"),
            P(SEQ, "head"),
            P(SEQ, "head"),
            P(SEQ, "head"),
            P("head"),
            P(),
            P(SEQ, None),
            P(SEQ),
        ),
        out_specs=P(ALL, None, None, None),
        check_vma=False,
    )
```

```python
import functools

import jax
import jax.numpy as jnp
from jax import lax
from jax.experimental import pallas as pl
from jax.experimental.pallas import tpu as pltpu
from jax.sharding import Mesh, PartitionSpec as P

BF16 = jnp.bfloat16
F32 = jnp.float32
CAPACITY = 2
ROWS_BLK = 128
BIG = 1 << 30
SEQ = ("z", "y", "core")
ALL = ("z", "y", "core", "head")
TURNS = (0, 3, 1, 2)
ZTURNS = (1, 3, 2)


def doc_of(positions, doc_ends):
    return jnp.sum((positions[:, None] >= doc_ends[None, :]).astype(jnp.int32), axis=1)


def doc_limit(positions, lengths_ref):
    end = lengths_ref[0]
    limit = jnp.where(positions < end, end, BIG)
    for doc in range(1, lengths_ref.shape[0]):
        end = end + lengths_ref[doc]
        limit = jnp.minimum(limit, jnp.where(positions < end, end, BIG))
    return limit


def params(mib=48):
    return pltpu.CompilerParams(
        dimension_semantics=("arbitrary",), vmem_limit_bytes=mib << 20
    )


SCALARS = pl.BlockSpec(memory_space=pltpu.SMEM)


def local_state_body(rate_ref, lengths_ref, query_ref, grad_ref, out_ref):
    count, dim = out_ref.shape[:2]
    toks = query_ref.shape[0]
    first = lax.axis_index(SEQ) * toks
    limit = doc_limit(jnp.maximum(first - 1, 0), lengths_ref)
    step = lax.broadcasted_iota(jnp.int32, (toks, dim), 0)
    inside = first + step < limit
    span = (step + 1).astype(F32)
    for h in range(count):
        rate = rate_ref[pl.program_id(0) * count + h]
        cols = slice(h * dim, (h + 1) * dim)
        lead = jnp.where(inside, jnp.exp(-rate * span), 0.0)
        scaled = (query_ref[:, cols].astype(F32) * lead).astype(BF16)
        out_ref[h] = lax.dot_general(
            scaled, grad_ref[:, cols], (((0,), (0,)), ((), ())), preferred_element_type=F32
        ).astype(out_ref.dtype)


def local_states(rates, lengths, queries, grads, count):
    heads = rates.shape[0]
    toks, dim = queries.shape[0], queries.shape[1] // heads
    blk = pl.BlockSpec((toks, count * dim), lambda h: (0, h))
    return pl.pallas_call(
        local_state_body,
        grid=(heads // count,),
        in_specs=[SCALARS, SCALARS, blk, blk],
        out_specs=pl.BlockSpec((count, dim, dim), lambda h: (h, 0, 0)),
        out_shape=jax.ShapeDtypeStruct((heads, dim, dim), BF16),
        compiler_params=params(),
        name="local_states",
    )(rates, lengths, queries, grads)


def within_body(count, rate_ref, lengths_ref, query_ref, key_ref, grad_ref, out_ref):
    toks = query_ref.shape[0]
    dim = query_ref.shape[1] // count
    first = lax.axis_index(SEQ) * toks
    half = toks // 2
    for lo in (0, half):
        src = lax.broadcasted_iota(jnp.int32, (half, 1), 0) + lo
        dst = lax.broadcasted_iota(jnp.int32, (1, toks - lo), 1) + lo
        limit = doc_limit(src + first, lengths_ref) - first
        seen = (dst >= src) & (dst < limit)
        for h in range(count):
            rate = rate_ref[pl.program_id(0) * count + h]
            cols = slice(h * dim, (h + 1) * dim)
            rise = jnp.exp(rate * src.astype(F32)) * (1.0 / dim)
            fall = jnp.exp(-rate * dst.astype(F32))
            scores = lax.dot_general(
                key_ref[lo : lo + half, cols],
                query_ref[lo:, cols],
                (((1,), (1,)), ((), ())),
                preferred_element_type=F32,
            )
            weights = jnp.where(seen, scores * rise * fall, 0.0).astype(BF16)
            out_ref[lo : lo + half, cols] = jnp.dot(
                weights, grad_ref[lo:, cols], preferred_element_type=F32
            )


def within(rates, lengths, queries, keys, grads, count):
    heads = rates.shape[0]
    toks, dim = queries.shape[0], queries.shape[1] // heads
    blk = pl.BlockSpec((toks, count * dim), lambda h: (0, h))
    return pl.pallas_call(
        functools.partial(within_body, count),
        grid=(heads // count,),
        in_specs=[SCALARS, SCALARS, blk, blk, blk],
        out_specs=blk,
        out_shape=jax.ShapeDtypeStruct((toks, heads * dim), F32),
        compiler_params=params(),
        name="within",
    )(rates, lengths, queries, keys, grads)


def across_body(rate_ref, lengths_ref, key_ref, state_ref, intra_ref, *outs):
    heads, dim = state_ref.shape[:2]
    toks = key_ref.shape[0]
    rows = toks // len(outs)
    first = lax.axis_index(SEQ) * toks
    last = first + toks - 1
    here = lax.axis_index("head")
    for turn, out_ref in enumerate(outs):
        start = pl.multiple_of(lax.rem(here + TURNS[turn], len(outs)) * rows, rows)
        src = lax.broadcasted_iota(jnp.int32, (rows, dim), 0) + start
        inside = last < doc_limit(src + first, lengths_ref)
        span = (toks - 1 - src).astype(F32)
        for h in range(heads):
            cols = slice(h * dim, (h + 1) * dim)
            tail = jnp.where(inside, jnp.exp(-rate_ref[h] * span) * (1.0 / dim), 0.0)
            product = jnp.dot(
                key_ref[pl.ds(start, rows), cols], state_ref[h], preferred_element_type=F32
            )
            out_ref[:, cols] = (intra_ref[pl.ds(start, rows), cols] + product * tail).astype(
                BF16
            )


def across(rates, lengths, keys, states, intra):
    heads, dim = states.shape[:2]
    toks, width = keys.shape
    rows = toks // len(TURNS)
    return pl.pallas_call(
        across_body,
        grid=(1,),
        in_specs=[
            SCALARS,
            SCALARS,
            pl.BlockSpec((toks, width), lambda i: (0, 0)),
            pl.BlockSpec((heads, dim, dim), lambda i: (0, 0, 0)),
            pl.BlockSpec((toks, width), lambda i: (0, 0)),
        ],
        out_specs=[pl.BlockSpec((rows, width), lambda i: (0, 0))] * len(TURNS),
        out_shape=[jax.ShapeDtypeStruct((rows, width), BF16)] * len(TURNS),
        compiler_params=params(),
        name="across",
    )(rates, lengths, keys, states, intra)


def times(groups, weights):
    total = None
    for rows, weight in zip(groups, weights):
        rows = rows[0][...] if len(rows) == 1 else jnp.concatenate([q[...] for q in rows], 0)
        part = lax.dot_general(
            rows, weight[0], (((1,), (1,)), ((), ())), preferred_element_type=F32
        )
        total = part if total is None else total + part
    return total.astype(BF16)


def direct_body(turns, place, *refs):
    each = (len(refs) - 1 - turns) // turns
    groups = [refs[k * each : (k + 1) * each] for k in range(turns)]
    refs[-1][...] = times(groups, refs[turns * each : -1])


def project_direct(place, pieces, weight, tile):
    turns, each = len(pieces), len(pieces[0])
    rows, depth = pieces[0][0].shape
    width = weight.shape[1]
    return pl.pallas_call(
        functools.partial(direct_body, turns),
        grid_spec=pltpu.PrefetchScalarGridSpec(
            num_scalar_prefetch=1,
            grid=(width // tile,),
            in_specs=[pl.BlockSpec((rows, depth), lambda i, p: (0, 0))] * (turns * each)
            + [
                pl.BlockSpec((1, tile, depth), lambda i, p, k=k: (p[k], i, 0))
                for k in range(turns)
            ],
            out_specs=pl.BlockSpec((rows * each, tile), lambda i, p: (0, i)),
        ),
        out_shape=pltpu.HBM((rows * each, width), BF16),
        compiler_params=params(),
        name="project_direct",
    )(place, *[q for piece in pieces for q in piece], *[weight] * turns)


def relayed_body(turns, place, pick, direct, *refs):
    last = times([(q,) for q in refs[:turns]], refs[turns:-1])
    rows = jnp.concatenate([direct[...], last], axis=0)
    refs[-1][...] = jnp.dot(pick[...], rows, preferred_element_type=F32).astype(BF16)


def project_relayed(place, pick, direct, pieces, weight, tile):
    turns = len(pieces)
    rows, depth = pieces[0].shape
    slots, toks = pick.shape
    width = weight.shape[1]
    return pl.pallas_call(
        functools.partial(relayed_body, turns),
        grid_spec=pltpu.PrefetchScalarGridSpec(
            num_scalar_prefetch=1,
            grid=(width // tile,),
            in_specs=[
                pl.BlockSpec((slots, toks), lambda i, p: (0, 0)),
                pl.BlockSpec((direct.shape[0], tile), lambda i, p: (0, i)),
            ]
            + [pl.BlockSpec((rows, depth), lambda i, p: (0, 0))] * turns
            + [
                pl.BlockSpec((1, tile, depth), lambda i, p, k=k: (p[k], i, 0))
                for k in range(turns)
            ],
            out_specs=pl.BlockSpec((slots, tile), lambda i, p: (0, i)),
        ),
        out_shape=pltpu.HBM((slots, width), BF16),
        compiler_params=params(),
        name="project_relayed",
    )(place, pick, direct, *pieces, *[weight] * turns)


def merge_body(column_ref, row_ref, rows_ref, out_ref, same_ref):
    slots = column_ref.shape[0]
    count, width = rows_ref.shape[0], rows_ref.shape[-1]

    @pl.when(pl.program_id(0) == 0)
    def _():
        same = (column_ref[...] == row_ref[...]) & (column_ref[...] >= 0)
        same_ref[...] = same.astype(F32).astype(BF16)

    for j in range(count):
        rows = rows_ref[j].reshape(slots, width)
        total = jnp.dot(same_ref[...], rows, preferred_element_type=F32).astype(BF16)
        out_ref[0, :, :, j * width : (j + 1) * width] = total.reshape(out_ref.shape[1:3] + (width,))


def merge(column, row, got, count):
    parts, n_from, per, width = got.shape
    slots = n_from * per
    return pl.pallas_call(
        merge_body,
        grid=(parts // count,),
        in_specs=[
            pl.BlockSpec((slots, 1), lambda i: (0, 0)),
            pl.BlockSpec((1, slots), lambda i: (0, 0)),
            pl.BlockSpec((count, n_from, per, width), lambda i: (i, 0, 0, 0)),
        ],
        out_specs=pl.BlockSpec(
            (1, slots // CAPACITY, CAPACITY, count * width), lambda i: (0, 0, 0, i)
        ),
        out_shape=jax.ShapeDtypeStruct((1, slots // CAPACITY, CAPACITY, parts * width), BF16),
        scratch_shapes=[pltpu.VMEM((slots, slots), BF16)],
        compiler_params=params(),
        name="merge",
    )(column, row, got)


def slots_of(owners, block_ids):
    blocks, width = owners.shape
    same_owner = owners[:, :, None] == owners[:, None, :]
    lower = jnp.arange(width, dtype=jnp.int32)
    earlier = lower[None, :] < lower[:, None]
    rank = jnp.sum((same_owner & earlier[None]).astype(jnp.int32), axis=2)
    return ((owners * blocks + block_ids[:, None]) * CAPACITY + rank).reshape(blocks * width)


def shift(size, step):
    return [(i, (i + step) % size) for i in range(size)]


def per_device(
    queries,
    key_vectors,
    output_grad,
    value_weight,
    decay_rate,
    doc_lengths,
    owner_block,
    row_offset,
):
    n_z = lax.axis_size("z")
    n_seq = lax.axis_size(SEQ)
    n_head = lax.axis_size("head")
    devices_all = n_seq * n_head
    tok_rows = queries.shape[0]
    head_local = decay_rate.shape[0]
    head_dim = queries.shape[1] // head_local
    seq_rank = lax.axis_index(SEQ)
    head_rank = lax.axis_index("head")
    z_rank = lax.axis_index("z")
    plane = n_seq // n_z
    turns = jnp.array(TURNS, jnp.int32)

    weight = lax.all_gather(value_weight, ("head", "y", "core"), axis=0, tiled=True)
    weight = weight.reshape(n_head, -1, value_weight.shape[1])

    queries, key_vectors, output_grad = (
        pltpu.with_memory_space_constraint(array, pltpu.HBM)
        for array in (queries, key_vectors, output_grad)
    )
    state = local_states(decay_rate, doc_lengths, queries, output_grad, head_local // 2)
    blocks = tok_rows // ROWS_BLK
    per = blocks * CAPACITY
    owners = owner_block[:, 0].reshape(blocks, ROWS_BLK)
    slot_index = slots_of(owners, jnp.arange(blocks, dtype=jnp.int32))
    my_slots = (
        (jnp.arange(n_seq, dtype=jnp.int32)[:, None] * n_head + head_rank) * per
        + jnp.arange(per, dtype=jnp.int32)[None, :]
    )
    hit = my_slots[:, :, None] == slot_index[None, None, :]
    named = jnp.sum(jnp.where(hit, row_offset[None, None, :] + 1, 0), axis=2)
    note = jnp.concatenate([(named // 32).astype(BF16), (named % 32).astype(BF16)], axis=1)
    note = jnp.pad(note[:, None, :], ((0, 0), (0, 0), (0, head_dim - 2 * per)))
    names = lax.dynamic_slice_in_dim(owners, head_rank, 1, 0).astype(BF16)
    names = jnp.broadcast_to(names[None], (n_seq, 1, ROWS_BLK))
    note = jnp.pad(jnp.concatenate([note, names], axis=1), ((0, 0), (0, 6), (0, 0)))

    share = head_local * head_dim // n_seq
    state_in = lax.all_to_all(
        state.reshape(n_seq, share, head_dim), SEQ, split_axis=0, concat_axis=0, tiled=True
    )
    intra = within(
        decay_rate, doc_lengths, queries, key_vectors, output_grad, head_local // 2
    )

    state_in, intra = lax.optimization_barrier((state_in, intra))
    doc_ends = jnp.cumsum(doc_lengths)
    ranks = jnp.arange(n_seq, dtype=jnp.int32)
    doc_last = doc_of((ranks + 1) * tok_rows - 1, doc_ends)
    doc_prior = doc_of(jnp.maximum(ranks * tok_rows - 1, 0), doc_ends)
    my_rate = decay_rate[seq_rank // (n_seq // head_local)]
    ahead = ranks[None, :] - ranks[:, None] - 1
    reach = (ahead >= 0) & (doc_last[:, None] == doc_prior[None, :])
    chain = jnp.where(
        reach, jnp.exp(-my_rate * (jnp.maximum(ahead, 0) * tok_rows).astype(F32)), 0.0
    )
    carried_all = jnp.einsum(
        "bc,cxy->bxy",
        chain,
        state_in.astype(F32),
        precision=lax.Precision.HIGHEST,
        preferred_element_type=F32,
    ).astype(BF16)
    carried = lax.all_to_all(
        jnp.concatenate([carried_all, note], axis=1),
        SEQ,
        split_axis=0,
        concat_axis=0,
        tiled=True,
    )
    offsets = (
        carried[:, share, :per].astype(jnp.int32) * 32
        + carried[:, share, per : 2 * per].astype(jnp.int32)
        - 1
    )
    column = offsets.reshape(-1, 1)
    row = offsets.reshape(n_z, plane, blocks, CAPACITY).transpose(1, 2, 0, 3).reshape(1, -1)
    near_z = (z_rank - jnp.array((0,) + ZTURNS, jnp.int32)) % n_z
    theirs = carried[:, share + 1].reshape(n_z, plane, ROWS_BLK)
    theirs = lax.dynamic_slice_in_dim(theirs, seq_rank % plane, 1, 1)[:, 0]
    theirs = theirs[near_z].astype(jnp.int32)
    their_slots = slots_of(theirs, near_z)
    all_slots = jnp.arange(devices_all * per, dtype=jnp.int32)
    pick = (all_slots[:, None] == their_slots[None, :]).astype(BF16)
    carried = carried[:, :share].reshape(head_local, head_dim, head_dim)

    own = across(decay_rate, doc_lengths, key_vectors, carried, intra)
    mine = [own[0]]
    for turn in range(1, len(TURNS)):
        mine.append(lax.ppermute(own[turn], "head", shift(n_head, TURNS[turn])))
    place = (head_rank - turns) % n_head

    def spread(rows, flip):
        below = lax.ppermute(rows, "z", shift(n_z, 1))
        above = lax.ppermute(rows, "z", shift(n_z, -1))
        relay = lax.ppermute(above if flip else below, "z", shift(n_z, -1 if flip else 1))
        return rows, below, above, relay

    groups = [spread(mine[0], False)]
    mine[1], *_ = lax.optimization_barrier((mine[1],) + groups[0][1:3])
    groups.append(spread(mine[1], True))
    mine[2], mine[3], _ = lax.optimization_barrier((mine[2], mine[3], groups[0][3]))
    groups.append(spread(mine[2], False))
    groups.append(spread(mine[3], True))
    pieces = [
        [pltpu.with_memory_space_constraint(q, pltpu.HBM) for q in group] for group in groups
    ]

    direct = project_direct(place, [piece[:3] for piece in pieces], weight, 512)
    direct = pltpu.with_memory_space_constraint(direct, pltpu.HBM)
    send = project_relayed(place, pick, direct, [piece[3] for piece in pieces], weight, 512)
    send = send.reshape(devices_all, per, -1)
    got = lax.all_to_all(send, ALL, split_axis=0, concat_axis=0, tiled=True)
    got = got.reshape(n_z, plane * n_head, per, -1)
    return merge(column, row, got, 2)


def solution(mesh):
    planes = mesh.shape["head"]
    devices = mesh.devices.reshape(planes, -1, 2, planes)
    return jax.shard_map(
        per_device,
        mesh=Mesh(devices, ALL),
        in_specs=(
            P(SEQ, "head"),
            P(SEQ, "head"),
            P(SEQ, "head"),
            P(SEQ, "head"),
            P("head"),
            P(),
            P(SEQ, None),
            P(SEQ),
        ),
        out_specs=P(ALL, None, None, None),
        check_vma=False,
    )
```

```python
import functools

import jax
import jax.numpy as jnp
from jax import lax
from jax.experimental import pallas as pl
from jax.experimental.pallas import tpu as pltpu
from jax.sharding import Mesh, PartitionSpec as P

BF16 = jnp.bfloat16
F32 = jnp.float32
CAPACITY = 2
ROWS_BLK = 128
BIG = 1 << 30
SEQ = ("z", "y", "core")
ALL = ("z", "y", "core", "head")
TURNS = (0, 3, 1, 2)
ZTURNS = (1, 3, 2)


def doc_of(positions, doc_ends):
    return jnp.sum((positions[:, None] >= doc_ends[None, :]).astype(jnp.int32), axis=1)


def doc_limit(positions, lengths_ref):
    end = lengths_ref[0]
    limit = jnp.where(positions < end, end, BIG)
    for doc in range(1, lengths_ref.shape[0]):
        end = end + lengths_ref[doc]
        limit = jnp.minimum(limit, jnp.where(positions < end, end, BIG))
    return limit


def params(mib=48):
    return pltpu.CompilerParams(
        dimension_semantics=("arbitrary",), vmem_limit_bytes=mib << 20
    )


SCALARS = pl.BlockSpec(memory_space=pltpu.SMEM)


def local_state_body(rate_ref, lengths_ref, query_ref, grad_ref, out_ref):
    count, dim = out_ref.shape[:2]
    toks = query_ref.shape[0]
    first = lax.axis_index(SEQ) * toks
    limit = doc_limit(jnp.maximum(first - 1, 0), lengths_ref)
    step = lax.broadcasted_iota(jnp.int32, (toks, dim), 0)
    inside = first + step < limit
    span = (step + 1).astype(F32)
    for h in range(count):
        rate = rate_ref[pl.program_id(0) * count + h]
        cols = slice(h * dim, (h + 1) * dim)
        lead = jnp.where(inside, jnp.exp(-rate * span), 0.0)
        scaled = (query_ref[:, cols].astype(F32) * lead).astype(BF16)
        out_ref[h] = lax.dot_general(
            scaled, grad_ref[:, cols], (((0,), (0,)), ((), ())), preferred_element_type=F32
        ).astype(out_ref.dtype)


def local_states(rates, lengths, queries, grads, count):
    heads = rates.shape[0]
    toks, dim = queries.shape[0], queries.shape[1] // heads
    blk = pl.BlockSpec((toks, count * dim), lambda h: (0, h))
    return pl.pallas_call(
        local_state_body,
        grid=(heads // count,),
        in_specs=[SCALARS, SCALARS, blk, blk],
        out_specs=pl.BlockSpec((count, dim, dim), lambda h: (h, 0, 0)),
        out_shape=jax.ShapeDtypeStruct((heads, dim, dim), BF16),
        compiler_params=params(),
        name="local_states",
    )(rates, lengths, queries, grads)


def within_body(count, rate_ref, lengths_ref, query_ref, key_ref, grad_ref, out_ref):
    toks = query_ref.shape[0]
    dim = query_ref.shape[1] // count
    first = lax.axis_index(SEQ) * toks
    half = toks // 2
    for lo in (0, half):
        src = lax.broadcasted_iota(jnp.int32, (half, 1), 0) + lo
        dst = lax.broadcasted_iota(jnp.int32, (1, toks - lo), 1) + lo
        limit = doc_limit(src + first, lengths_ref) - first
        seen = (dst >= src) & (dst < limit)
        for h in range(count):
            rate = rate_ref[pl.program_id(0) * count + h]
            cols = slice(h * dim, (h + 1) * dim)
            rise = jnp.exp(rate * src.astype(F32)) * (1.0 / dim)
            fall = jnp.exp(-rate * dst.astype(F32))
            scores = lax.dot_general(
                key_ref[lo : lo + half, cols],
                query_ref[lo:, cols],
                (((1,), (1,)), ((), ())),
                preferred_element_type=F32,
            )
            weights = jnp.where(seen, scores * rise * fall, 0.0).astype(BF16)
            out_ref[lo : lo + half, cols] = jnp.dot(
                weights, grad_ref[lo:, cols], preferred_element_type=F32
            )


def within(rates, lengths, queries, keys, grads, count):
    heads = rates.shape[0]
    toks, dim = queries.shape[0], queries.shape[1] // heads
    blk = pl.BlockSpec((toks, count * dim), lambda h: (0, h))
    return pl.pallas_call(
        functools.partial(within_body, count),
        grid=(heads // count,),
        in_specs=[SCALARS, SCALARS, blk, blk, blk],
        out_specs=blk,
        out_shape=jax.ShapeDtypeStruct((toks, heads * dim), F32),
        compiler_params=params(),
        name="within",
    )(rates, lengths, queries, keys, grads)


def across_body(rate_ref, lengths_ref, key_ref, state_ref, intra_ref, *outs):
    heads, dim = state_ref.shape[:2]
    toks = key_ref.shape[0]
    rows = toks // len(outs)
    first = lax.axis_index(SEQ) * toks
    last = first + toks - 1
    here = lax.axis_index("head")
    for turn, out_ref in enumerate(outs):
        start = pl.multiple_of(lax.rem(here + TURNS[turn], len(outs)) * rows, rows)
        src = lax.broadcasted_iota(jnp.int32, (rows, dim), 0) + start
        inside = last < doc_limit(src + first, lengths_ref)
        span = (toks - 1 - src).astype(F32)
        for h in range(heads):
            cols = slice(h * dim, (h + 1) * dim)
            tail = jnp.where(inside, jnp.exp(-rate_ref[h] * span) * (1.0 / dim), 0.0)
            product = jnp.dot(
                key_ref[pl.ds(start, rows), cols], state_ref[h], preferred_element_type=F32
            )
            out_ref[:, cols] = (intra_ref[pl.ds(start, rows), cols] + product * tail).astype(
                BF16
            )


def across(rates, lengths, keys, states, intra):
    heads, dim = states.shape[:2]
    toks, width = keys.shape
    rows = toks // len(TURNS)
    return pl.pallas_call(
        across_body,
        grid=(1,),
        in_specs=[
            SCALARS,
            SCALARS,
            pl.BlockSpec((toks, width), lambda i: (0, 0)),
            pl.BlockSpec((heads, dim, dim), lambda i: (0, 0, 0)),
            pl.BlockSpec((toks, width), lambda i: (0, 0)),
        ],
        out_specs=[pl.BlockSpec((rows, width), lambda i: (0, 0))] * len(TURNS),
        out_shape=[jax.ShapeDtypeStruct((rows, width), BF16)] * len(TURNS),
        compiler_params=params(),
        name="across",
    )(rates, lengths, keys, states, intra)


def times(rows, weight):
    rows = jnp.concatenate([part[...] for part in rows], axis=0)
    return lax.dot_general(
        rows, weight[0], (((1,), (1,)), ((), ())), preferred_element_type=F32
    )


def project_body(turns, place, pick, *refs):
    out_ref = refs[-1]
    total = None
    for k in range(turns):
        part = times(refs[k * turns : (k + 1) * turns], refs[turns * turns + k])
        total = part if total is None else total + part
    out_ref[...] = jnp.dot(
        pick[...], total.astype(BF16), preferred_element_type=F32
    ).astype(BF16)


def project(place, pick, pieces, weight, tile):
    turns = len(pieces)
    rows, depth = pieces[0][0].shape
    slots, toks = pick.shape
    width = weight.shape[1]
    whole = pl.BlockSpec((rows, depth), lambda i, p: (0, 0))
    return pl.pallas_call(
        functools.partial(project_body, turns),
        grid_spec=pltpu.PrefetchScalarGridSpec(
            num_scalar_prefetch=1,
            grid=(width // tile,),
            in_specs=[pl.BlockSpec((slots, toks), lambda i, p: (0, 0))]
            + [whole] * (turns * turns)
            + [
                pl.BlockSpec((1, tile, depth), lambda i, p, k=k: (p[k], i, 0))
                for k in range(turns)
            ],
            out_specs=pl.BlockSpec((slots, tile), lambda i, p: (0, i)),
        ),
        out_shape=pltpu.HBM((slots, width), BF16),
        compiler_params=params(),
        name="project",
    )(place, pick, *[q for piece in pieces for q in piece], *[weight] * turns)


def merge_body(column_ref, row_ref, rows_ref, out_ref, same_ref):
    slots = column_ref.shape[0]
    count, width = rows_ref.shape[0], rows_ref.shape[-1]

    @pl.when(pl.program_id(0) == 0)
    def _():
        same = (column_ref[...] == row_ref[...]) & (column_ref[...] >= 0)
        same_ref[...] = same.astype(F32).astype(BF16)

    for j in range(count):
        rows = rows_ref[j].reshape(slots, width)
        total = jnp.dot(same_ref[...], rows, preferred_element_type=F32).astype(BF16)
        out_ref[0, :, :, j * width : (j + 1) * width] = total.reshape(out_ref.shape[1:3] + (width,))


def merge(column, row, got, count):
    parts, n_from, per, width = got.shape
    slots = n_from * per
    return pl.pallas_call(
        merge_body,
        grid=(parts // count,),
        in_specs=[
            pl.BlockSpec((slots, 1), lambda i: (0, 0)),
            pl.BlockSpec((1, slots), lambda i: (0, 0)),
            pl.BlockSpec((count, n_from, per, width), lambda i: (i, 0, 0, 0)),
        ],
        out_specs=pl.BlockSpec(
            (1, slots // CAPACITY, CAPACITY, count * width), lambda i: (0, 0, 0, i)
        ),
        out_shape=jax.ShapeDtypeStruct((1, slots // CAPACITY, CAPACITY, parts * width), BF16),
        scratch_shapes=[pltpu.VMEM((slots, slots), BF16)],
        compiler_params=params(),
        name="merge",
    )(column, row, got)


def slots_of(owners, block_ids):
    blocks, width = owners.shape
    same_owner = owners[:, :, None] == owners[:, None, :]
    lower = jnp.arange(width, dtype=jnp.int32)
    earlier = lower[None, :] < lower[:, None]
    rank = jnp.sum((same_owner & earlier[None]).astype(jnp.int32), axis=2)
    return ((owners * blocks + block_ids[:, None]) * CAPACITY + rank).reshape(blocks * width)


def shift(size, step):
    return [(i, (i + step) % size) for i in range(size)]


def per_device(
    queries,
    key_vectors,
    output_grad,
    value_weight,
    decay_rate,
    doc_lengths,
    owner_block,
    row_offset,
):
    n_z = lax.axis_size("z")
    n_seq = lax.axis_size(SEQ)
    n_head = lax.axis_size("head")
    devices_all = n_seq * n_head
    tok_rows = queries.shape[0]
    head_local = decay_rate.shape[0]
    head_dim = queries.shape[1] // head_local
    seq_rank = lax.axis_index(SEQ)
    head_rank = lax.axis_index("head")
    z_rank = lax.axis_index("z")
    plane = n_seq // n_z
    turns = jnp.array(TURNS, jnp.int32)

    weight = lax.all_gather(value_weight, ("head", "y", "core"), axis=0, tiled=True)
    weight = weight.reshape(n_head, -1, value_weight.shape[1])

    queries, key_vectors, output_grad = (
        pltpu.with_memory_space_constraint(array, pltpu.HBM)
        for array in (queries, key_vectors, output_grad)
    )
    state = local_states(decay_rate, doc_lengths, queries, output_grad, head_local // 2)
    blocks = tok_rows // ROWS_BLK
    per = blocks * CAPACITY
    owners = owner_block[:, 0].reshape(blocks, ROWS_BLK)
    names = lax.dynamic_slice_in_dim(owners, head_rank, 1, 0).astype(BF16)

    heads_in = ("y", "core")
    state_in = lax.all_to_all(state, heads_in, split_axis=0, concat_axis=0, tiled=True)
    intra = within(
        decay_rate, doc_lengths, queries, key_vectors, output_grad, head_local // 2
    )

    doc_ends = jnp.cumsum(doc_lengths)
    ranks = z_rank * plane + jnp.arange(plane, dtype=jnp.int32)
    doc_last = doc_of((ranks + 1) * tok_rows - 1, doc_ends)
    doc_prior = doc_of(jnp.maximum(ranks * tok_rows - 1, 0), doc_ends)
    my_rate = decay_rate[seq_rank % plane] * tok_rows

    def links(ahead, same):
        return jnp.where(
            same & (ahead >= 0), jnp.exp(-my_rate * jnp.maximum(ahead, 0).astype(F32)), 0.0
        )

    chain = links(ranks[None, :] - ranks[:, None] - 1, doc_last[:, None] == doc_prior[None, :])
    entry = links(ranks - ranks[0], doc_prior == doc_prior[0])
    mixed = jnp.einsum(
        "bc,cxy->bxy",
        jnp.concatenate([chain, entry[None]], axis=0),
        state_in.astype(F32),
        precision=lax.Precision.HIGHEST,
        preferred_element_type=F32,
    )
    total = jnp.concatenate([mixed[plane].astype(BF16), jnp.pad(names, ((0, 7), (0, 0)))], axis=0)
    later = [lax.ppermute(total, "z", shift(n_z, -step)) for step in range(1, n_z)]
    *later, intra = lax.optimization_barrier((*later, intra))
    carried_all = mixed[:plane]
    for step in range(1, n_z):
        first = (z_rank + step) * plane
        prior = doc_of(first[None] * tok_rows - 1, doc_ends)
        weigh = links(first - ranks - 1, (doc_last == prior) & (first < n_seq))
        carried_all += weigh[:, None, None] * later[step - 1][:head_dim].astype(F32)
    carried = lax.all_to_all(
        carried_all.astype(BF16), heads_in, split_axis=0, concat_axis=0, tiled=True
    )

    near_z = (z_rank - jnp.array((0,) + ZTURNS, jnp.int32)) % n_z
    theirs = jnp.concatenate(
        [names] + [later[n_z - 1 - step][head_dim : head_dim + 1] for step in ZTURNS], axis=0
    )
    their_slots = slots_of(theirs.astype(jnp.int32), near_z)
    all_slots = jnp.arange(devices_all * per, dtype=jnp.int32)
    pick = (all_slots[:, None] == their_slots[None, :]).astype(BF16)

    own = across(decay_rate, doc_lengths, key_vectors, carried, intra)
    mine = [own[0]]
    for turn in range(1, len(TURNS)):
        mine.append(lax.ppermute(own[turn], "head", shift(n_head, TURNS[turn])))
    place = (head_rank - turns) % n_head

    def spread(rows, flip):
        below = lax.ppermute(rows, "z", shift(n_z, 1))
        above = lax.ppermute(rows, "z", shift(n_z, -1))
        relay = lax.ppermute(above if flip else below, "z", shift(n_z, -1 if flip else 1))
        return rows, below, above, relay

    groups = [spread(mine[0], False)]
    mine[1], *_ = lax.optimization_barrier((mine[1],) + groups[0][1:3])
    groups.append(spread(mine[1], True))
    mine[2], mine[3], _ = lax.optimization_barrier((mine[2], mine[3], groups[0][3]))
    groups.append(spread(mine[2], False))
    groups.append(spread(mine[3], True))
    pieces = [
        [pltpu.with_memory_space_constraint(q, pltpu.HBM) for q in group] for group in groups
    ]

    send = project(place, pick, pieces, weight, 512)
    ids = owners * 1024 + row_offset.reshape(blocks, ROWS_BLK)
    ids, _ = lax.optimization_barrier((ids, weight))
    ids = lax.all_gather(ids, SEQ, axis=0, tiled=True)
    at = jnp.arange(ROWS_BLK, dtype=jnp.int32)[None, :]
    hit = ids // 1024 == seq_rank * n_head + head_rank
    lead = at == jnp.min(jnp.where(hit, at, ROWS_BLK), axis=1, keepdims=True)
    slot_hits = jnp.stack([hit & lead, hit & ~lead], axis=1)
    offsets = jnp.sum(jnp.where(slot_hits, (ids % 1024)[:, None, :] + 1, 0), axis=2) - 1
    column = offsets.reshape(-1, 1)
    row = offsets.reshape(n_z, plane, blocks, CAPACITY).transpose(1, 2, 0, 3).reshape(1, -1)
    send = send.reshape(devices_all, per, -1)
    got = lax.all_to_all(send, ALL, split_axis=0, concat_axis=0, tiled=True)
    got = got.reshape(n_z, plane * n_head, per, -1)
    return merge(column, row, got, 2)


def solution(mesh):
    planes = mesh.shape["head"]
    devices = mesh.devices.reshape(planes, -1, 2, planes)
    return jax.shard_map(
        per_device,
        mesh=Mesh(devices, ALL),
        in_specs=(
            P(SEQ, "head"),
            P(SEQ, "head"),
            P(SEQ, "head"),
            P(SEQ, "head"),
            P("head"),
            P(),
            P(SEQ, None),
            P(SEQ),
        ),
        out_specs=P(ALL, None, None, None),
        check_vma=False,
    )
```

```python
import functools

import jax
import jax.numpy as jnp
from jax import lax
from jax.experimental import pallas as pl
from jax.experimental.pallas import tpu as pltpu
from jax.sharding import Mesh, PartitionSpec as P

BF16 = jnp.bfloat16
F32 = jnp.float32
CAPACITY = 2
ROWS_BLK = 128
BIG = 1 << 30
SEQ = ("z", "y", "core")
ALL = ("z", "y", "core", "head")
TURNS = (0, 3, 1, 2)
ZTURNS = (1, 3, 2)


def doc_of(positions, doc_ends):
    return jnp.sum((positions[:, None] >= doc_ends[None, :]).astype(jnp.int32), axis=1)


def doc_limit(positions, lengths_ref):
    end = lengths_ref[0]
    limit = jnp.where(positions < end, end, BIG)
    for doc in range(1, lengths_ref.shape[0]):
        end = end + lengths_ref[doc]
        limit = jnp.minimum(limit, jnp.where(positions < end, end, BIG))
    return limit


def params(mib=48):
    return pltpu.CompilerParams(
        dimension_semantics=("arbitrary",), vmem_limit_bytes=mib << 20
    )


SCALARS = pl.BlockSpec(memory_space=pltpu.SMEM)


def local_state_body(rate_ref, lengths_ref, query_ref, grad_ref, out_ref):
    count, dim = out_ref.shape[:2]
    toks = query_ref.shape[0]
    first = lax.axis_index(SEQ) * toks
    limit = doc_limit(jnp.maximum(first - 1, 0), lengths_ref)
    step = lax.broadcasted_iota(jnp.int32, (toks, dim), 0)
    inside = first + step < limit
    span = (step + 1).astype(F32)
    for h in range(count):
        rate = rate_ref[pl.program_id(0) * count + h]
        cols = slice(h * dim, (h + 1) * dim)
        lead = jnp.where(inside, jnp.exp(-rate * span), 0.0)
        scaled = (query_ref[:, cols].astype(F32) * lead).astype(BF16)
        out_ref[h] = lax.dot_general(
            scaled, grad_ref[:, cols], (((0,), (0,)), ((), ())), preferred_element_type=F32
        ).astype(out_ref.dtype)


def local_states(rates, lengths, queries, grads, count):
    heads = rates.shape[0]
    toks, dim = queries.shape[0], queries.shape[1] // heads
    blk = pl.BlockSpec((toks, count * dim), lambda h: (0, h))
    return pl.pallas_call(
        local_state_body,
        grid=(heads // count,),
        in_specs=[SCALARS, SCALARS, blk, blk],
        out_specs=pl.BlockSpec((count, dim, dim), lambda h: (h, 0, 0)),
        out_shape=jax.ShapeDtypeStruct((heads, dim, dim), BF16),
        compiler_params=params(),
        name="local_states",
    )(rates, lengths, queries, grads)


def within_body(count, rate_ref, lengths_ref, query_ref, key_ref, grad_ref, out_ref):
    toks = query_ref.shape[0]
    dim = query_ref.shape[1] // count
    first = lax.axis_index(SEQ) * toks
    half = toks // 2
    for lo in (0, half):
        src = lax.broadcasted_iota(jnp.int32, (half, 1), 0) + lo
        dst = lax.broadcasted_iota(jnp.int32, (1, toks - lo), 1) + lo
        limit = doc_limit(src + first, lengths_ref) - first
        seen = (dst >= src) & (dst < limit)
        for h in range(count):
            rate = rate_ref[pl.program_id(0) * count + h]
            cols = slice(h * dim, (h + 1) * dim)
            rise = jnp.exp(rate * src.astype(F32)) * (1.0 / dim)
            fall = jnp.exp(-rate * dst.astype(F32))
            scores = lax.dot_general(
                key_ref[lo : lo + half, cols],
                query_ref[lo:, cols],
                (((1,), (1,)), ((), ())),
                preferred_element_type=F32,
            )
            weights = jnp.where(seen, scores * rise * fall, 0.0).astype(BF16)
            out_ref[lo : lo + half, cols] = jnp.dot(
                weights, grad_ref[lo:, cols], preferred_element_type=F32
            )


def within(rates, lengths, queries, keys, grads, count):
    heads = rates.shape[0]
    toks, dim = queries.shape[0], queries.shape[1] // heads
    blk = pl.BlockSpec((toks, count * dim), lambda h: (0, h))
    return pl.pallas_call(
        functools.partial(within_body, count),
        grid=(heads // count,),
        in_specs=[SCALARS, SCALARS, blk, blk, blk],
        out_specs=blk,
        out_shape=jax.ShapeDtypeStruct((toks, heads * dim), F32),
        compiler_params=params(),
        name="within",
    )(rates, lengths, queries, keys, grads)


def across_body(rate_ref, lengths_ref, key_ref, state_ref, intra_ref, *outs):
    heads, dim = state_ref.shape[:2]
    toks = key_ref.shape[0]
    rows = toks // len(outs)
    first = lax.axis_index(SEQ) * toks
    last = first + toks - 1
    here = lax.axis_index("head")
    for turn, out_ref in enumerate(outs):
        start = pl.multiple_of(lax.rem(here + TURNS[turn], len(outs)) * rows, rows)
        src = lax.broadcasted_iota(jnp.int32, (rows, dim), 0) + start
        inside = last < doc_limit(src + first, lengths_ref)
        span = (toks - 1 - src).astype(F32)
        for h in range(heads):
            cols = slice(h * dim, (h + 1) * dim)
            tail = jnp.where(inside, jnp.exp(-rate_ref[h] * span) * (1.0 / dim), 0.0)
            product = jnp.dot(
                key_ref[pl.ds(start, rows), cols], state_ref[h], preferred_element_type=F32
            )
            out_ref[:, cols] = (intra_ref[pl.ds(start, rows), cols] + product * tail).astype(
                BF16
            )


def across(rates, lengths, keys, states, intra):
    heads, dim = states.shape[:2]
    toks, width = keys.shape
    rows = toks // len(TURNS)
    return pl.pallas_call(
        across_body,
        grid=(1,),
        in_specs=[
            SCALARS,
            SCALARS,
            pl.BlockSpec((toks, width), lambda i: (0, 0)),
            pl.BlockSpec((heads, dim, dim), lambda i: (0, 0, 0)),
            pl.BlockSpec((toks, width), lambda i: (0, 0)),
        ],
        out_specs=[pl.BlockSpec((rows, width), lambda i: (0, 0))] * len(TURNS),
        out_shape=[jax.ShapeDtypeStruct((rows, width), BF16)] * len(TURNS),
        compiler_params=params(),
        name="across",
    )(rates, lengths, keys, states, intra)


def times(rows, weight):
    rows = jnp.concatenate([part[...] for part in rows], axis=0)
    return lax.dot_general(
        rows, weight[0], (((1,), (1,)), ((), ())), preferred_element_type=F32
    )


def project_body(turns, place, pick, *refs):
    out_ref = refs[-1]
    total = None
    for k in range(turns):
        part = times(refs[k * turns : (k + 1) * turns], refs[turns * turns + k])
        total = part if total is None else total + part
    out_ref[...] = jnp.dot(
        pick[...], total.astype(BF16), preferred_element_type=F32
    ).astype(BF16)


def project(place, pick, pieces, weight, tile):
    turns = len(pieces)
    rows, depth = pieces[0][0].shape
    slots, toks = pick.shape
    width = weight.shape[1]
    whole = pl.BlockSpec((rows, depth), lambda i, p: (0, 0))
    return pl.pallas_call(
        functools.partial(project_body, turns),
        grid_spec=pltpu.PrefetchScalarGridSpec(
            num_scalar_prefetch=1,
            grid=(width // tile,),
            in_specs=[pl.BlockSpec((slots, toks), lambda i, p: (0, 0))]
            + [whole] * (turns * turns)
            + [
                pl.BlockSpec((1, tile, depth), lambda i, p, k=k: (p[k], i, 0))
                for k in range(turns)
            ],
            out_specs=pl.BlockSpec((slots, tile), lambda i, p: (0, i)),
        ),
        out_shape=pltpu.HBM((slots, width), BF16),
        compiler_params=params(),
        name="project",
    )(place, pick, *[q for piece in pieces for q in piece], *[weight] * turns)


def merge_body(column_ref, row_ref, rows_ref, out_ref, same_ref):
    slots = column_ref.shape[0]
    count, width = rows_ref.shape[0], rows_ref.shape[-1]

    @pl.when(pl.program_id(0) == 0)
    def _():
        same = (column_ref[...] == row_ref[...]) & (column_ref[...] >= 0)
        same_ref[...] = same.astype(F32).astype(BF16)

    for j in range(count):
        rows = rows_ref[j].reshape(slots, width)
        total = jnp.dot(same_ref[...], rows, preferred_element_type=F32).astype(BF16)
        out_ref[0, :, :, j * width : (j + 1) * width] = total.reshape(out_ref.shape[1:3] + (width,))


def merge(column, row, got, count):
    parts, n_from, per, width = got.shape
    slots = n_from * per
    return pl.pallas_call(
        merge_body,
        grid=(parts // count,),
        in_specs=[
            pl.BlockSpec((slots, 1), lambda i: (0, 0)),
            pl.BlockSpec((1, slots), lambda i: (0, 0)),
            pl.BlockSpec((count, n_from, per, width), lambda i: (i, 0, 0, 0)),
        ],
        out_specs=pl.BlockSpec(
            (1, slots // CAPACITY, CAPACITY, count * width), lambda i: (0, 0, 0, i)
        ),
        out_shape=jax.ShapeDtypeStruct((1, slots // CAPACITY, CAPACITY, parts * width), BF16),
        scratch_shapes=[pltpu.VMEM((slots, slots), BF16)],
        compiler_params=params(),
        name="merge",
    )(column, row, got)


def slots_of(owners, block_ids):
    blocks, width = owners.shape
    same_owner = owners[:, :, None] == owners[:, None, :]
    lower = jnp.arange(width, dtype=jnp.int32)
    earlier = lower[None, :] < lower[:, None]
    rank = jnp.sum((same_owner & earlier[None]).astype(jnp.int32), axis=2)
    return ((owners * blocks + block_ids[:, None]) * CAPACITY + rank).reshape(blocks * width)


def shift(size, step):
    return [(i, (i + step) % size) for i in range(size)]


def per_device(
    queries,
    key_vectors,
    output_grad,
    value_weight,
    decay_rate,
    doc_lengths,
    owner_block,
    row_offset,
):
    n_z = lax.axis_size("z")
    n_seq = lax.axis_size(SEQ)
    n_head = lax.axis_size("head")
    devices_all = n_seq * n_head
    tok_rows = queries.shape[0]
    head_local = decay_rate.shape[0]
    head_dim = queries.shape[1] // head_local
    seq_rank = lax.axis_index(SEQ)
    head_rank = lax.axis_index("head")
    z_rank = lax.axis_index("z")
    plane = n_seq // n_z
    turns = jnp.array(TURNS, jnp.int32)

    weight = lax.all_gather(value_weight, ("head", "y", "core"), axis=0, tiled=True)
    weight = weight.reshape(n_head, -1, value_weight.shape[1])

    queries, key_vectors, output_grad, rates, lengths = (
        pltpu.with_memory_space_constraint(array, pltpu.HBM)
        for array in (queries, key_vectors, output_grad, decay_rate, doc_lengths)
    )
    state = local_states(rates, lengths, queries, output_grad, head_local // 2)
    blocks = tok_rows // ROWS_BLK
    per = blocks * CAPACITY
    owners = owner_block[:, 0].reshape(blocks, ROWS_BLK)
    slot_index = slots_of(owners, jnp.arange(blocks, dtype=jnp.int32))
    my_slots = (
        (jnp.arange(n_seq, dtype=jnp.int32)[:, None] * n_head + head_rank) * per
        + jnp.arange(per, dtype=jnp.int32)[None, :]
    )
    hit = my_slots[:, :, None] == slot_index[None, None, :]
    named = jnp.sum(jnp.where(hit, row_offset[None, None, :] + 1, 0), axis=2)
    note = jnp.concatenate([(named // 32).astype(BF16), (named % 32).astype(BF16)], axis=1)
    note = jnp.pad(note[:, None, :], ((0, 0), (0, 0), (0, head_dim - 2 * per)))
    names = lax.dynamic_slice_in_dim(owners, head_rank, 1, 0).astype(BF16)
    names = jnp.broadcast_to(names[None], (n_seq, 1, ROWS_BLK))
    note = jnp.pad(jnp.concatenate([note, names], axis=1), ((0, 0), (0, 6), (0, 0)))

    share = head_local * head_dim // n_seq
    state_in = lax.all_to_all(
        state.reshape(n_seq, share, head_dim), SEQ, split_axis=0, concat_axis=0, tiled=True
    )
    intra = within(
        rates, lengths, queries, key_vectors, output_grad, head_local // 2
    )

    state_in, intra = lax.optimization_barrier((state_in, intra))
    doc_ends = jnp.cumsum(doc_lengths)
    ranks = jnp.arange(n_seq, dtype=jnp.int32)
    doc_last = doc_of((ranks + 1) * tok_rows - 1, doc_ends)
    doc_prior = doc_of(jnp.maximum(ranks * tok_rows - 1, 0), doc_ends)
    my_rate = decay_rate[seq_rank // (n_seq // head_local)]
    ahead = ranks[None, :] - ranks[:, None] - 1
    reach = (ahead >= 0) & (doc_last[:, None] == doc_prior[None, :])
    chain = jnp.where(
        reach, jnp.exp(-my_rate * (jnp.maximum(ahead, 0) * tok_rows).astype(F32)), 0.0
    )
    carried_all = jnp.einsum(
        "bc,cxy->bxy",
        chain,
        state_in.astype(F32),
        precision=lax.Precision.HIGHEST,
        preferred_element_type=F32,
    ).astype(BF16)
    carried = lax.all_to_all(
        jnp.concatenate([carried_all, note], axis=1),
        SEQ,
        split_axis=0,
        concat_axis=0,
        tiled=True,
    )
    offsets = (
        carried[:, share, :per].astype(jnp.int32) * 32
        + carried[:, share, per : 2 * per].astype(jnp.int32)
        - 1
    )
    column = offsets.reshape(-1, 1)
    row = offsets.reshape(n_z, plane, blocks, CAPACITY).transpose(1, 2, 0, 3).reshape(1, -1)
    near_z = (z_rank - jnp.array((0,) + ZTURNS, jnp.int32)) % n_z
    theirs = carried[:, share + 1].reshape(n_z, plane, ROWS_BLK)
    theirs = lax.dynamic_slice_in_dim(theirs, seq_rank % plane, 1, 1)[:, 0]
    theirs = theirs[near_z].astype(jnp.int32)
    their_slots = slots_of(theirs, near_z)
    all_slots = jnp.arange(devices_all * per, dtype=jnp.int32)
    pick = (all_slots[:, None] == their_slots[None, :]).astype(BF16)
    carried = carried[:, :share].reshape(head_local, head_dim, head_dim)

    own = across(rates, lengths, key_vectors, carried, intra)
    mine = [own[0]]
    for turn in range(1, len(TURNS)):
        mine.append(lax.ppermute(own[turn], "head", shift(n_head, TURNS[turn])))
    place = (head_rank - turns) % n_head

    def spread(rows, flip):
        below = lax.ppermute(rows, "z", shift(n_z, 1))
        above = lax.ppermute(rows, "z", shift(n_z, -1))
        relay = lax.ppermute(above if flip else below, "z", shift(n_z, -1 if flip else 1))
        return rows, below, above, relay

    groups = [spread(mine[0], False)]
    mine[1], mine[2], *_ = lax.optimization_barrier((mine[1], mine[2]) + groups[0][1:3])
    groups.append(spread(mine[1], True))
    groups.append(spread(mine[2], False))
    mine[3], *_ = lax.optimization_barrier((mine[3], groups[0][3]))
    groups.append(spread(mine[3], True))
    pieces = [
        [pltpu.with_memory_space_constraint(q, pltpu.HBM) for q in group] for group in groups
    ]

    send = project(place, pick, pieces, weight, 512)
    send = send.reshape(devices_all, per, -1)
    got = lax.all_to_all(send, ALL, split_axis=0, concat_axis=0, tiled=True)
    got = got.reshape(n_z, plane * n_head, per, -1)
    return merge(column, row, got, 2)


def solution(mesh):
    planes = mesh.shape["head"]
    devices = mesh.devices.reshape(planes, -1, 2, planes)
    return jax.shard_map(
        per_device,
        mesh=Mesh(devices, ALL),
        in_specs=(
            P(SEQ, "head"),
            P(SEQ, "head"),
            P(SEQ, "head"),
            P(SEQ, "head"),
            P("head"),
            P(),
            P(SEQ, None),
            P(SEQ),
        ),
        out_specs=P(ALL, None, None, None),
        check_vma=False,
    )
```

```python
import functools

import jax
import jax.numpy as jnp
from jax import lax
from jax.experimental import pallas as pl
from jax.experimental.pallas import tpu as pltpu
from jax.sharding import Mesh, PartitionSpec as P

BF16 = jnp.bfloat16
F32 = jnp.float32
CAPACITY = 2
ROWS_BLK = 128
BIG = 1 << 30
SEQ = ("z", "y", "core")
ALL = ("z", "y", "core", "head")
TURNS = (0, 3, 1, 2)
ZTURNS = (1, 3, 2)


def doc_of(positions, doc_ends):
    return jnp.sum((positions[:, None] >= doc_ends[None, :]).astype(jnp.int32), axis=1)


def doc_limit(positions, lengths_ref):
    end = lengths_ref[0]
    limit = jnp.where(positions < end, end, BIG)
    for doc in range(1, lengths_ref.shape[0]):
        end = end + lengths_ref[doc]
        limit = jnp.minimum(limit, jnp.where(positions < end, end, BIG))
    return limit


def params(mib=48):
    return pltpu.CompilerParams(
        dimension_semantics=("arbitrary",), vmem_limit_bytes=mib << 20
    )


SCALARS = pl.BlockSpec(memory_space=pltpu.SMEM)


def local_state_body(rate_ref, lengths_ref, query_ref, grad_ref, out_ref):
    count, dim = out_ref.shape[:2]
    toks = query_ref.shape[0]
    first = lax.axis_index(SEQ) * toks
    limit = doc_limit(jnp.maximum(first - 1, 0), lengths_ref)
    step = lax.broadcasted_iota(jnp.int32, (toks, dim), 0)
    inside = first + step < limit
    span = (step + 1).astype(F32)
    for h in range(count):
        rate = rate_ref[pl.program_id(0) * count + h]
        cols = slice(h * dim, (h + 1) * dim)
        lead = jnp.where(inside, jnp.exp(-rate * span), 0.0)
        scaled = (query_ref[:, cols].astype(F32) * lead).astype(BF16)
        out_ref[h] = lax.dot_general(
            scaled, grad_ref[:, cols], (((0,), (0,)), ((), ())), preferred_element_type=F32
        ).astype(out_ref.dtype)


def local_states(rates, lengths, queries, grads, count):
    heads = rates.shape[0]
    toks, dim = queries.shape[0], queries.shape[1] // heads
    blk = pl.BlockSpec((toks, count * dim), lambda h: (0, h))
    return pl.pallas_call(
        local_state_body,
        grid=(heads // count,),
        in_specs=[SCALARS, SCALARS, blk, blk],
        out_specs=pl.BlockSpec((count, dim, dim), lambda h: (h, 0, 0)),
        out_shape=jax.ShapeDtypeStruct((heads, dim, dim), BF16),
        compiler_params=params(),
        name="local_states",
    )(rates, lengths, queries, grads)


def within_body(count, rate_ref, lengths_ref, query_ref, key_ref, grad_ref, out_ref):
    toks = query_ref.shape[0]
    dim = query_ref.shape[1] // count
    first = lax.axis_index(SEQ) * toks
    half = toks // 2
    for lo in (0, half):
        src = lax.broadcasted_iota(jnp.int32, (half, 1), 0) + lo
        dst = lax.broadcasted_iota(jnp.int32, (1, toks - lo), 1) + lo
        limit = doc_limit(src + first, lengths_ref) - first
        seen = (dst >= src) & (dst < limit)
        for h in range(count):
            rate = rate_ref[pl.program_id(0) * count + h]
            cols = slice(h * dim, (h + 1) * dim)
            rise = jnp.exp(rate * src.astype(F32)) * (1.0 / dim)
            fall = jnp.exp(-rate * dst.astype(F32))
            scores = lax.dot_general(
                key_ref[lo : lo + half, cols],
                query_ref[lo:, cols],
                (((1,), (1,)), ((), ())),
                preferred_element_type=F32,
            )
            weights = jnp.where(seen, scores * rise * fall, 0.0).astype(BF16)
            out_ref[lo : lo + half, cols] = jnp.dot(
                weights, grad_ref[lo:, cols], preferred_element_type=F32
            )


def within(rates, lengths, queries, keys, grads, count):
    heads = rates.shape[0]
    toks, dim = queries.shape[0], queries.shape[1] // heads
    blk = pl.BlockSpec((toks, count * dim), lambda h: (0, h))
    return pl.pallas_call(
        functools.partial(within_body, count),
        grid=(heads // count,),
        in_specs=[SCALARS, SCALARS, blk, blk, blk],
        out_specs=blk,
        out_shape=jax.ShapeDtypeStruct((toks, heads * dim), F32),
        compiler_params=params(),
        name="within",
    )(rates, lengths, queries, keys, grads)


def across_body(rate_ref, lengths_ref, key_ref, state_ref, intra_ref, *outs):
    heads, dim = state_ref.shape[:2]
    toks = key_ref.shape[0]
    rows = toks // len(outs)
    first = lax.axis_index(SEQ) * toks
    last = first + toks - 1
    here = lax.axis_index("head")
    for turn, out_ref in enumerate(outs):
        start = pl.multiple_of(lax.rem(here + TURNS[turn], len(outs)) * rows, rows)
        src = lax.broadcasted_iota(jnp.int32, (rows, dim), 0) + start
        inside = last < doc_limit(src + first, lengths_ref)
        span = (toks - 1 - src).astype(F32)
        for h in range(heads):
            cols = slice(h * dim, (h + 1) * dim)
            tail = jnp.where(inside, jnp.exp(-rate_ref[h] * span) * (1.0 / dim), 0.0)
            product = jnp.dot(
                key_ref[pl.ds(start, rows), cols], state_ref[h], preferred_element_type=F32
            )
            out_ref[:, cols] = (intra_ref[pl.ds(start, rows), cols] + product * tail).astype(
                BF16
            )


def across(rates, lengths, keys, states, intra):
    heads, dim = states.shape[:2]
    toks, width = keys.shape
    rows = toks // len(TURNS)
    return pl.pallas_call(
        across_body,
        grid=(1,),
        in_specs=[
            SCALARS,
            SCALARS,
            pl.BlockSpec((toks, width), lambda i: (0, 0)),
            pl.BlockSpec((heads, dim, dim), lambda i: (0, 0, 0)),
            pl.BlockSpec((toks, width), lambda i: (0, 0)),
        ],
        out_specs=[pl.BlockSpec((rows, width), lambda i: (0, 0))] * len(TURNS),
        out_shape=[jax.ShapeDtypeStruct((rows, width), BF16)] * len(TURNS),
        compiler_params=params(),
        name="across",
    )(rates, lengths, keys, states, intra)


def times(rows, weight):
    rows = jnp.concatenate([part[...] for part in rows], axis=0)
    return lax.dot_general(
        rows, weight[0], (((1,), (1,)), ((), ())), preferred_element_type=F32
    )


def project_body(turns, place, pick, *refs):
    out_ref = refs[-1]
    total = None
    for k in range(turns):
        part = times(refs[k * turns : (k + 1) * turns], refs[turns * turns + k])
        total = part if total is None else total + part
    out_ref[...] = jnp.dot(
        pick[...], total.astype(BF16), preferred_element_type=F32
    ).astype(BF16)


def project(place, pick, pieces, weight, tile):
    turns = len(pieces)
    rows, depth = pieces[0][0].shape
    slots, toks = pick.shape
    width = weight.shape[1]
    whole = pl.BlockSpec((rows, depth), lambda i, p: (0, 0))
    return pl.pallas_call(
        functools.partial(project_body, turns),
        grid_spec=pltpu.PrefetchScalarGridSpec(
            num_scalar_prefetch=1,
            grid=(width // tile,),
            in_specs=[pl.BlockSpec((slots, toks), lambda i, p: (0, 0))]
            + [whole] * (turns * turns)
            + [
                pl.BlockSpec((1, tile, depth), lambda i, p, k=k: (p[k], i, 0))
                for k in range(turns)
            ],
            out_specs=pl.BlockSpec((slots, tile), lambda i, p: (0, i)),
        ),
        out_shape=pltpu.HBM((slots, width), BF16),
        compiler_params=params(),
        name="project",
    )(place, pick, *[q for piece in pieces for q in piece], *[weight] * turns)


def merge_body(column_ref, row_ref, rows_ref, out_ref, same_ref):
    slots = column_ref.shape[0]
    count, width = rows_ref.shape[0], rows_ref.shape[-1]

    @pl.when(pl.program_id(0) == 0)
    def _():
        same = (column_ref[...] == row_ref[...]) & (column_ref[...] >= 0)
        same_ref[...] = same.astype(F32).astype(BF16)

    for j in range(count):
        rows = rows_ref[j].reshape(slots, width)
        total = jnp.dot(same_ref[...], rows, preferred_element_type=F32).astype(BF16)
        out_ref[0, :, :, j * width : (j + 1) * width] = total.reshape(out_ref.shape[1:3] + (width,))


def merge(column, row, got, count):
    parts, n_from, per, width = got.shape
    slots = n_from * per
    return pl.pallas_call(
        merge_body,
        grid=(parts // count,),
        in_specs=[
            pl.BlockSpec((slots, 1), lambda i: (0, 0)),
            pl.BlockSpec((1, slots), lambda i: (0, 0)),
            pl.BlockSpec((count, n_from, per, width), lambda i: (i, 0, 0, 0)),
        ],
        out_specs=pl.BlockSpec(
            (1, slots // CAPACITY, CAPACITY, count * width), lambda i: (0, 0, 0, i)
        ),
        out_shape=jax.ShapeDtypeStruct((1, slots // CAPACITY, CAPACITY, parts * width), BF16),
        scratch_shapes=[pltpu.VMEM((slots, slots), BF16)],
        compiler_params=params(),
        name="merge",
    )(column, row, got)


def slots_of(owners, block_ids):
    blocks, width = owners.shape
    same_owner = owners[:, :, None] == owners[:, None, :]
    lower = jnp.arange(width, dtype=jnp.int32)
    earlier = lower[None, :] < lower[:, None]
    rank = jnp.sum((same_owner & earlier[None]).astype(jnp.int32), axis=2)
    return ((owners * blocks + block_ids[:, None]) * CAPACITY + rank).reshape(blocks * width)


def shift(size, step):
    return [(i, (i + step) % size) for i in range(size)]


def per_device(
    queries,
    key_vectors,
    output_grad,
    value_weight,
    decay_rate,
    doc_lengths,
    owner_block,
    row_offset,
):
    n_z = lax.axis_size("z")
    n_seq = lax.axis_size(SEQ)
    n_head = lax.axis_size("head")
    devices_all = n_seq * n_head
    tok_rows = queries.shape[0]
    head_local = decay_rate.shape[0]
    head_dim = queries.shape[1] // head_local
    seq_rank = lax.axis_index(SEQ)
    head_rank = lax.axis_index("head")
    z_rank = lax.axis_index("z")
    plane = n_seq // n_z
    turns = jnp.array(TURNS, jnp.int32)

    weight = lax.all_gather(value_weight, ("head", "y", "core"), axis=0, tiled=True)
    weight = weight.reshape(n_head, -1, value_weight.shape[1])

    queries, key_vectors, output_grad, rates, lengths = (
        pltpu.with_memory_space_constraint(array, pltpu.HBM)
        for array in (queries, key_vectors, output_grad, decay_rate, doc_lengths)
    )
    state = local_states(rates, lengths, queries, output_grad, head_local // 2)
    blocks = tok_rows // ROWS_BLK
    per = blocks * CAPACITY
    owners = owner_block[:, 0].reshape(blocks, ROWS_BLK)
    slot_index = slots_of(owners, jnp.arange(blocks, dtype=jnp.int32))
    my_slots = (
        (jnp.arange(n_seq, dtype=jnp.int32)[:, None] * n_head + head_rank) * per
        + jnp.arange(per, dtype=jnp.int32)[None, :]
    )
    hit = my_slots[:, :, None] == slot_index[None, None, :]
    named = jnp.sum(jnp.where(hit, row_offset[None, None, :] + 1, 0), axis=2)
    note = jnp.concatenate([(named // 32).astype(BF16), (named % 32).astype(BF16)], axis=1)
    note = jnp.pad(note[:, None, :], ((0, 0), (0, 0), (0, head_dim - 2 * per)))
    names = lax.dynamic_slice_in_dim(owners, head_rank, 1, 0).astype(BF16)
    names = jnp.broadcast_to(names[None], (n_seq, 1, ROWS_BLK))
    note = jnp.pad(jnp.concatenate([note, names], axis=1), ((0, 0), (0, 6), (0, 0)))

    share = head_local * head_dim // n_seq
    state_in = lax.all_to_all(
        state.reshape(n_seq, share, head_dim), SEQ, split_axis=0, concat_axis=0, tiled=True
    )
    intra = within(
        rates, lengths, queries, key_vectors, output_grad, head_local // 2
    )

    state_in, intra = lax.optimization_barrier((state_in, intra))
    doc_ends = jnp.cumsum(doc_lengths)
    ranks = jnp.arange(n_seq, dtype=jnp.int32)
    doc_last = doc_of((ranks + 1) * tok_rows - 1, doc_ends)
    doc_prior = doc_of(jnp.maximum(ranks * tok_rows - 1, 0), doc_ends)
    my_rate = decay_rate[seq_rank // (n_seq // head_local)]
    ahead = ranks[None, :] - ranks[:, None] - 1
    reach = (ahead >= 0) & (doc_last[:, None] == doc_prior[None, :])
    chain = jnp.where(
        reach, jnp.exp(-my_rate * (jnp.maximum(ahead, 0) * tok_rows).astype(F32)), 0.0
    )
    carried_all = jnp.einsum(
        "bc,cxy->bxy",
        chain,
        state_in.astype(F32),
        precision=lax.Precision.HIGHEST,
        preferred_element_type=F32,
    ).astype(BF16)
    carried = lax.all_to_all(
        jnp.concatenate([carried_all, note], axis=1),
        SEQ,
        split_axis=0,
        concat_axis=0,
        tiled=True,
    )
    offsets = (
        carried[:, share, :per].astype(jnp.int32) * 32
        + carried[:, share, per : 2 * per].astype(jnp.int32)
        - 1
    )
    column = offsets.reshape(-1, 1)
    row = offsets.reshape(n_z, plane, blocks, CAPACITY).transpose(1, 2, 0, 3).reshape(1, -1)
    near_z = (z_rank - jnp.array((0,) + ZTURNS, jnp.int32)) % n_z
    theirs = carried[:, share + 1].reshape(n_z, plane, ROWS_BLK)
    theirs = lax.dynamic_slice_in_dim(theirs, seq_rank % plane, 1, 1)[:, 0]
    theirs = theirs[near_z].astype(jnp.int32)
    their_slots = slots_of(theirs, near_z)
    all_slots = jnp.arange(devices_all * per, dtype=jnp.int32)
    pick = (all_slots[:, None] == their_slots[None, :]).astype(BF16)
    carried = carried[:, :share].reshape(head_local, head_dim, head_dim)

    own = across(rates, lengths, key_vectors, carried, intra)
    mine = [own[0]]
    for turn in range(1, len(TURNS)):
        mine.append(lax.ppermute(own[turn], "head", shift(n_head, TURNS[turn])))
    place = (head_rank - turns) % n_head

    def spread(rows, flip):
        below = lax.ppermute(rows, "z", shift(n_z, 1))
        above = lax.ppermute(rows, "z", shift(n_z, -1))
        relay = lax.ppermute(above if flip else below, "z", shift(n_z, -1 if flip else 1))
        return rows, below, above, relay

    groups = [spread(mine[0], False)]
    mine[1], mine[2], *_ = lax.optimization_barrier((mine[1], mine[2]) + groups[0][1:3])
    groups.append(spread(mine[1], False))
    groups.append(spread(mine[2], False))
    mine[3], *_ = lax.optimization_barrier((mine[3], groups[0][3]))
    groups.append(spread(mine[3], True))
    pieces = [
        [pltpu.with_memory_space_constraint(q, pltpu.HBM) for q in group] for group in groups
    ]

    send = project(place, pick, pieces, weight, 512)
    send = send.reshape(devices_all, per, -1)
    got = lax.all_to_all(send, ALL, split_axis=0, concat_axis=0, tiled=True)
    got = got.reshape(n_z, plane * n_head, per, -1)
    return merge(column, row, got, 2)


def solution(mesh):
    planes = mesh.shape["head"]
    devices = mesh.devices.reshape(planes, -1, 2, planes)
    return jax.shard_map(
        per_device,
        mesh=Mesh(devices, ALL),
        in_specs=(
            P(SEQ, "head"),
            P(SEQ, "head"),
            P(SEQ, "head"),
            P(SEQ, "head"),
            P("head"),
            P(),
            P(SEQ, None),
            P(SEQ),
        ),
        out_specs=P(ALL, None, None, None),
        check_vma=False,
    )
```

```python
import functools

import jax
import jax.numpy as jnp
from jax import lax
from jax.experimental import pallas as pl
from jax.experimental.pallas import tpu as pltpu
from jax.sharding import Mesh, PartitionSpec as P

BF16 = jnp.bfloat16
F32 = jnp.float32
CAPACITY = 2
ROWS_BLK = 128
BIG = 1 << 30
SEQ = ("z", "y", "core")
ALL = ("z", "y", "core", "head")
TURNS = (0, 3, 1, 2)
ZTURNS = (1, 3, 2)


def doc_of(positions, doc_ends):
    return jnp.sum((positions[:, None] >= doc_ends[None, :]).astype(jnp.int32), axis=1)


def doc_limit(positions, lengths_ref):
    end = lengths_ref[0]
    limit = jnp.where(positions < end, end, BIG)
    for doc in range(1, lengths_ref.shape[0]):
        end = end + lengths_ref[doc]
        limit = jnp.minimum(limit, jnp.where(positions < end, end, BIG))
    return limit


def params(mib=48):
    return pltpu.CompilerParams(
        dimension_semantics=("arbitrary",), vmem_limit_bytes=mib << 20
    )


SCALARS = pl.BlockSpec(memory_space=pltpu.SMEM)


def local_state_body(rate_ref, lengths_ref, query_ref, grad_ref, out_ref):
    count, dim = out_ref.shape[:2]
    toks = query_ref.shape[0]
    first = lax.axis_index(SEQ) * toks
    limit = doc_limit(jnp.maximum(first - 1, 0), lengths_ref)
    step = lax.broadcasted_iota(jnp.int32, (toks, dim), 0)
    inside = first + step < limit
    span = (step + 1).astype(F32)
    for h in range(count):
        rate = rate_ref[pl.program_id(0) * count + h]
        cols = slice(h * dim, (h + 1) * dim)
        lead = jnp.where(inside, jnp.exp(-rate * span), 0.0)
        scaled = (query_ref[:, cols].astype(F32) * lead).astype(BF16)
        out_ref[h] = lax.dot_general(
            scaled, grad_ref[:, cols], (((0,), (0,)), ((), ())), preferred_element_type=F32
        ).astype(out_ref.dtype)


def local_states(rates, lengths, queries, grads, count):
    heads = rates.shape[0]
    toks, dim = queries.shape[0], queries.shape[1] // heads
    blk = pl.BlockSpec((toks, count * dim), lambda h: (0, h))
    return pl.pallas_call(
        local_state_body,
        grid=(heads // count,),
        in_specs=[SCALARS, SCALARS, blk, blk],
        out_specs=pl.BlockSpec((count, dim, dim), lambda h: (h, 0, 0)),
        out_shape=jax.ShapeDtypeStruct((heads, dim, dim), BF16),
        compiler_params=params(),
        name="local_states",
    )(rates, lengths, queries, grads)


def within_body(count, rate_ref, lengths_ref, query_ref, key_ref, grad_ref, out_ref):
    toks = query_ref.shape[0]
    dim = query_ref.shape[1] // count
    first = lax.axis_index(SEQ) * toks
    half = toks // 2
    for lo in (0, half):
        src = lax.broadcasted_iota(jnp.int32, (half, 1), 0) + lo
        dst = lax.broadcasted_iota(jnp.int32, (1, toks - lo), 1) + lo
        limit = doc_limit(src + first, lengths_ref) - first
        seen = (dst >= src) & (dst < limit)
        for h in range(count):
            rate = rate_ref[pl.program_id(0) * count + h]
            cols = slice(h * dim, (h + 1) * dim)
            rise = jnp.exp(rate * src.astype(F32)) * (1.0 / dim)
            fall = jnp.exp(-rate * dst.astype(F32))
            scores = lax.dot_general(
                key_ref[lo : lo + half, cols],
                query_ref[lo:, cols],
                (((1,), (1,)), ((), ())),
                preferred_element_type=F32,
            )
            weights = jnp.where(seen, scores * rise * fall, 0.0).astype(BF16)
            out_ref[lo : lo + half, cols] = jnp.dot(
                weights, grad_ref[lo:, cols], preferred_element_type=F32
            )


def within(rates, lengths, queries, keys, grads, count):
    heads = rates.shape[0]
    toks, dim = queries.shape[0], queries.shape[1] // heads
    blk = pl.BlockSpec((toks, count * dim), lambda h: (0, h))
    return pl.pallas_call(
        functools.partial(within_body, count),
        grid=(heads // count,),
        in_specs=[SCALARS, SCALARS, blk, blk, blk],
        out_specs=blk,
        out_shape=jax.ShapeDtypeStruct((toks, heads * dim), F32),
        compiler_params=params(),
        name="within",
    )(rates, lengths, queries, keys, grads)


def across_body(rate_ref, lengths_ref, key_ref, state_ref, intra_ref, *outs):
    heads, dim = state_ref.shape[:2]
    toks = key_ref.shape[0]
    rows = toks // len(outs)
    first = lax.axis_index(SEQ) * toks
    last = first + toks - 1
    here = lax.axis_index("head")
    for turn, out_ref in enumerate(outs):
        start = pl.multiple_of(lax.rem(here + TURNS[turn], len(outs)) * rows, rows)
        src = lax.broadcasted_iota(jnp.int32, (rows, dim), 0) + start
        inside = last < doc_limit(src + first, lengths_ref)
        span = (toks - 1 - src).astype(F32)
        for h in range(heads):
            cols = slice(h * dim, (h + 1) * dim)
            tail = jnp.where(inside, jnp.exp(-rate_ref[h] * span) * (1.0 / dim), 0.0)
            product = jnp.dot(
                key_ref[pl.ds(start, rows), cols], state_ref[h], preferred_element_type=F32
            )
            out_ref[:, cols] = (intra_ref[pl.ds(start, rows), cols] + product * tail).astype(
                BF16
            )


def across(rates, lengths, keys, states, intra):
    heads, dim = states.shape[:2]
    toks, width = keys.shape
    rows = toks // len(TURNS)
    return pl.pallas_call(
        across_body,
        grid=(1,),
        in_specs=[
            SCALARS,
            SCALARS,
            pl.BlockSpec((toks, width), lambda i: (0, 0)),
            pl.BlockSpec((heads, dim, dim), lambda i: (0, 0, 0)),
            pl.BlockSpec((toks, width), lambda i: (0, 0)),
        ],
        out_specs=[pl.BlockSpec((rows, width), lambda i: (0, 0))] * len(TURNS),
        out_shape=[jax.ShapeDtypeStruct((rows, width), BF16)] * len(TURNS),
        compiler_params=params(),
        name="across",
    )(rates, lengths, keys, states, intra)


def times(rows, weight):
    rows = jnp.concatenate([part[...] for part in rows], axis=0)
    return lax.dot_general(
        rows, weight[0], (((1,), (1,)), ((), ())), preferred_element_type=F32
    )


def project_body(turns, place, pick, *refs):
    out_ref = refs[-1]
    total = None
    for k in range(turns):
        part = times(refs[k * turns : (k + 1) * turns], refs[turns * turns + k])
        total = part if total is None else total + part
    out_ref[...] = jnp.dot(
        pick[...], total.astype(BF16), preferred_element_type=F32
    ).astype(BF16)


def project(place, pick, pieces, weight, tile):
    turns = len(pieces)
    rows, depth = pieces[0][0].shape
    slots, toks = pick.shape
    width = weight.shape[1]
    whole = pl.BlockSpec((rows, depth), lambda i, p: (0, 0))
    return pl.pallas_call(
        functools.partial(project_body, turns),
        grid_spec=pltpu.PrefetchScalarGridSpec(
            num_scalar_prefetch=1,
            grid=(width // tile,),
            in_specs=[pl.BlockSpec((slots, toks), lambda i, p: (0, 0))]
            + [whole] * (turns * turns)
            + [
                pl.BlockSpec((1, tile, depth), lambda i, p, k=k: (p[k], i, 0))
                for k in range(turns)
            ],
            out_specs=pl.BlockSpec((slots, tile), lambda i, p: (0, i)),
        ),
        out_shape=pltpu.HBM((slots, width), BF16),
        compiler_params=params(),
        name="project",
    )(place, pick, *[q for piece in pieces for q in piece], *[weight] * turns)


def merge_body(column_ref, row_ref, rows_ref, out_ref, same_ref):
    slots = column_ref.shape[0]
    count, width = rows_ref.shape[0], rows_ref.shape[-1]

    @pl.when(pl.program_id(0) == 0)
    def _():
        same = (column_ref[...] == row_ref[...]) & (column_ref[...] >= 0)
        same_ref[...] = same.astype(F32).astype(BF16)

    for j in range(count):
        rows = rows_ref[j].reshape(slots, width)
        total = jnp.dot(same_ref[...], rows, preferred_element_type=F32).astype(BF16)
        out_ref[0, :, :, j * width : (j + 1) * width] = total.reshape(out_ref.shape[1:3] + (width,))


def merge(column, row, got, count):
    parts, n_from, per, width = got.shape
    slots = n_from * per
    return pl.pallas_call(
        merge_body,
        grid=(parts // count,),
        in_specs=[
            pl.BlockSpec((slots, 1), lambda i: (0, 0)),
            pl.BlockSpec((1, slots), lambda i: (0, 0)),
            pl.BlockSpec((count, n_from, per, width), lambda i: (i, 0, 0, 0)),
        ],
        out_specs=pl.BlockSpec(
            (1, slots // CAPACITY, CAPACITY, count * width), lambda i: (0, 0, 0, i)
        ),
        out_shape=jax.ShapeDtypeStruct((1, slots // CAPACITY, CAPACITY, parts * width), BF16),
        scratch_shapes=[pltpu.VMEM((slots, slots), BF16)],
        compiler_params=params(),
        name="merge",
    )(column, row, got)


def slots_of(owners, block_ids):
    blocks, width = owners.shape
    same_owner = owners[:, :, None] == owners[:, None, :]
    lower = jnp.arange(width, dtype=jnp.int32)
    earlier = lower[None, :] < lower[:, None]
    rank = jnp.sum((same_owner & earlier[None]).astype(jnp.int32), axis=2)
    return ((owners * blocks + block_ids[:, None]) * CAPACITY + rank).reshape(blocks * width)


def shift(size, step):
    return [(i, (i + step) % size) for i in range(size)]


def per_device(
    queries,
    key_vectors,
    output_grad,
    value_weight,
    decay_rate,
    doc_lengths,
    owner_block,
    row_offset,
):
    n_z = lax.axis_size("z")
    n_seq = lax.axis_size(SEQ)
    n_head = lax.axis_size("head")
    devices_all = n_seq * n_head
    tok_rows = queries.shape[0]
    head_local = decay_rate.shape[0]
    head_dim = queries.shape[1] // head_local
    seq_rank = lax.axis_index(SEQ)
    head_rank = lax.axis_index("head")
    z_rank = lax.axis_index("z")
    plane = n_seq // n_z
    turns = jnp.array(TURNS, jnp.int32)

    weight = lax.all_gather(value_weight, ("head", "y", "core"), axis=0, tiled=True)
    weight = weight.reshape(n_head, -1, value_weight.shape[1])

    queries, key_vectors, output_grad, rates, lengths = (
        pltpu.with_memory_space_constraint(array, pltpu.HBM)
        for array in (queries, key_vectors, output_grad, decay_rate, doc_lengths)
    )
    state = local_states(rates, lengths, queries, output_grad, head_local // 2)
    blocks = tok_rows // ROWS_BLK
    per = blocks * CAPACITY
    owners = owner_block[:, 0].reshape(blocks, ROWS_BLK)
    slot_index = slots_of(owners, jnp.arange(blocks, dtype=jnp.int32))
    my_slots = (
        (jnp.arange(n_seq, dtype=jnp.int32)[:, None] * n_head + head_rank) * per
        + jnp.arange(per, dtype=jnp.int32)[None, :]
    )
    hit = my_slots[:, :, None] == slot_index[None, None, :]
    named = jnp.sum(jnp.where(hit, row_offset[None, None, :] + 1, 0), axis=2)
    note = jnp.concatenate([(named // 32).astype(BF16), (named % 32).astype(BF16)], axis=1)
    note = jnp.pad(note[:, None, :], ((0, 0), (0, 0), (0, head_dim - 2 * per)))
    names = lax.dynamic_slice_in_dim(owners, head_rank, 1, 0).astype(BF16)
    names = jnp.broadcast_to(names[None], (n_seq, 1, ROWS_BLK))
    note = jnp.pad(jnp.concatenate([note, names], axis=1), ((0, 0), (0, 6), (0, 0)))

    share = head_local * head_dim // n_seq
    state_in = lax.all_to_all(
        state.reshape(n_seq, share, head_dim), SEQ, split_axis=0, concat_axis=0, tiled=True
    )
    intra = within(
        rates, lengths, queries, key_vectors, output_grad, head_local // 2
    )

    doc_ends = jnp.cumsum(doc_lengths)
    ranks = jnp.arange(n_seq, dtype=jnp.int32)
    doc_last = doc_of((ranks + 1) * tok_rows - 1, doc_ends)
    doc_prior = doc_of(jnp.maximum(ranks * tok_rows - 1, 0), doc_ends)
    my_rate = decay_rate[seq_rank // (n_seq // head_local)]
    ahead = ranks[None, :] - ranks[:, None] - 1
    reach = (ahead >= 0) & (doc_last[:, None] == doc_prior[None, :])
    chain = jnp.where(
        reach, jnp.exp(-my_rate * (jnp.maximum(ahead, 0) * tok_rows).astype(F32)), 0.0
    )
    carried_all = jnp.einsum(
        "bc,cxy->bxy",
        chain,
        state_in.astype(F32),
        precision=lax.Precision.HIGHEST,
        preferred_element_type=F32,
    ).astype(BF16)
    carried = lax.all_to_all(
        jnp.concatenate([carried_all, note], axis=1),
        SEQ,
        split_axis=0,
        concat_axis=0,
        tiled=True,
    )
    offsets = (
        carried[:, share, :per].astype(jnp.int32) * 32
        + carried[:, share, per : 2 * per].astype(jnp.int32)
        - 1
    )
    column = offsets.reshape(-1, 1)
    row = offsets.reshape(n_z, plane, blocks, CAPACITY).transpose(1, 2, 0, 3).reshape(1, -1)
    near_z = (z_rank - jnp.array((0,) + ZTURNS, jnp.int32)) % n_z
    theirs = carried[:, share + 1].reshape(n_z, plane, ROWS_BLK)
    theirs = lax.dynamic_slice_in_dim(theirs, seq_rank % plane, 1, 1)[:, 0]
    theirs = theirs[near_z].astype(jnp.int32)
    their_slots = slots_of(theirs, near_z)
    all_slots = jnp.arange(devices_all * per, dtype=jnp.int32)
    pick = (all_slots[:, None] == their_slots[None, :]).astype(BF16)
    carried = carried[:, :share].reshape(head_local, head_dim, head_dim)

    own = across(rates, lengths, key_vectors, carried, intra)
    mine = [own[0]]
    for turn in range(1, len(TURNS)):
        mine.append(lax.ppermute(own[turn], "head", shift(n_head, TURNS[turn])))
    place = (head_rank - turns) % n_head

    def spread(rows, flip):
        below = lax.ppermute(rows, "z", shift(n_z, 1))
        above = lax.ppermute(rows, "z", shift(n_z, -1))
        relay = lax.ppermute(above if flip else below, "z", shift(n_z, -1 if flip else 1))
        return rows, below, above, relay

    groups = [spread(mine[0], False)]
    mine[1], mine[2], *_ = lax.optimization_barrier((mine[1], mine[2]) + groups[0][1:3])
    groups.append(spread(mine[1], False))
    groups.append(spread(mine[2], False))
    mine[3], *_ = lax.optimization_barrier((mine[3], groups[0][3]))
    groups.append(spread(mine[3], True))
    pieces = [
        [pltpu.with_memory_space_constraint(q, pltpu.HBM) for q in group] for group in groups
    ]

    send = project(place, pick, pieces, weight, 512)
    send = send.reshape(devices_all, per, -1)
    got = lax.all_to_all(send, ALL, split_axis=0, concat_axis=0, tiled=True)
    got = got.reshape(n_z, plane * n_head, per, -1)
    return merge(column, row, got, 2)


def solution(mesh):
    planes = mesh.shape["head"]
    devices = mesh.devices.reshape(planes, -1, 2, planes)
    return jax.shard_map(
        per_device,
        mesh=Mesh(devices, ALL),
        in_specs=(
            P(SEQ, "head"),
            P(SEQ, "head"),
            P(SEQ, "head"),
            P(SEQ, "head"),
            P("head"),
            P(),
            P(SEQ, None),
            P(SEQ),
        ),
        out_specs=P(ALL, None, None, None),
        check_vma=False,
    )
```

```python
import functools

import jax
import jax.numpy as jnp
from jax import lax
from jax.experimental import pallas as pl
from jax.experimental.pallas import tpu as pltpu
from jax.sharding import Mesh, PartitionSpec as P

BF16 = jnp.bfloat16
F32 = jnp.float32
CAPACITY = 2
ROWS_BLK = 128
BIG = 1 << 30
SEQ = ("z", "y", "core")
ALL = ("z", "y", "core", "head")
TURNS = (0, 3, 1, 2)
ZTURNS = (1, 3, 2)


def doc_of(positions, doc_ends):
    return jnp.sum((positions[:, None] >= doc_ends[None, :]).astype(jnp.int32), axis=1)


def doc_limit(positions, lengths_ref):
    end = lengths_ref[0]
    limit = jnp.where(positions < end, end, BIG)
    for doc in range(1, lengths_ref.shape[0]):
        end = end + lengths_ref[doc]
        limit = jnp.minimum(limit, jnp.where(positions < end, end, BIG))
    return limit


def params(mib=48):
    return pltpu.CompilerParams(
        dimension_semantics=("arbitrary",), vmem_limit_bytes=mib << 20
    )


SCALARS = pl.BlockSpec(memory_space=pltpu.SMEM)


def local_state_body(rate_ref, lengths_ref, query_ref, grad_ref, out_ref):
    count, dim = out_ref.shape[:2]
    toks = query_ref.shape[0]
    first = lax.axis_index(SEQ) * toks
    limit = doc_limit(jnp.maximum(first - 1, 0), lengths_ref)
    step = lax.broadcasted_iota(jnp.int32, (toks, dim), 0)
    inside = first + step < limit
    span = (step + 1).astype(F32)
    for h in range(count):
        rate = rate_ref[pl.program_id(0) * count + h]
        cols = slice(h * dim, (h + 1) * dim)
        lead = jnp.where(inside, jnp.exp(-rate * span), 0.0)
        scaled = (query_ref[:, cols].astype(F32) * lead).astype(BF16)
        out_ref[h] = lax.dot_general(
            scaled, grad_ref[:, cols], (((0,), (0,)), ((), ())), preferred_element_type=F32
        ).astype(out_ref.dtype)


def local_states(rates, lengths, queries, grads, count):
    heads = rates.shape[0]
    toks, dim = queries.shape[0], queries.shape[1] // heads
    blk = pl.BlockSpec((toks, count * dim), lambda h: (0, h))
    return pl.pallas_call(
        local_state_body,
        grid=(heads // count,),
        in_specs=[SCALARS, SCALARS, blk, blk],
        out_specs=pl.BlockSpec((count, dim, dim), lambda h: (h, 0, 0)),
        out_shape=jax.ShapeDtypeStruct((heads, dim, dim), BF16),
        compiler_params=params(),
        name="local_states",
    )(rates, lengths, queries, grads)


def within_body(count, rate_ref, lengths_ref, query_ref, key_ref, grad_ref, out_ref):
    toks = query_ref.shape[0]
    dim = query_ref.shape[1] // count
    first = lax.axis_index(SEQ) * toks
    half = toks // 2
    for lo in (0, half):
        src = lax.broadcasted_iota(jnp.int32, (half, 1), 0) + lo
        dst = lax.broadcasted_iota(jnp.int32, (1, toks - lo), 1) + lo
        limit = doc_limit(src + first, lengths_ref) - first
        seen = (dst >= src) & (dst < limit)
        for h in range(count):
            rate = rate_ref[pl.program_id(0) * count + h]
            cols = slice(h * dim, (h + 1) * dim)
            rise = jnp.exp(rate * src.astype(F32)) * (1.0 / dim)
            fall = jnp.exp(-rate * dst.astype(F32))
            scores = lax.dot_general(
                key_ref[lo : lo + half, cols],
                query_ref[lo:, cols],
                (((1,), (1,)), ((), ())),
                preferred_element_type=F32,
            )
            weights = jnp.where(seen, scores * rise * fall, 0.0).astype(BF16)
            out_ref[lo : lo + half, cols] = jnp.dot(
                weights, grad_ref[lo:, cols], preferred_element_type=F32
            )


def within(rates, lengths, queries, keys, grads, count):
    heads = rates.shape[0]
    toks, dim = queries.shape[0], queries.shape[1] // heads
    blk = pl.BlockSpec((toks, count * dim), lambda h: (0, h))
    return pl.pallas_call(
        functools.partial(within_body, count),
        grid=(heads // count,),
        in_specs=[SCALARS, SCALARS, blk, blk, blk],
        out_specs=blk,
        out_shape=jax.ShapeDtypeStruct((toks, heads * dim), F32),
        compiler_params=params(),
        name="within",
    )(rates, lengths, queries, keys, grads)


def across_body(rate_ref, lengths_ref, key_ref, state_ref, intra_ref, *outs):
    heads, dim = state_ref.shape[:2]
    toks = key_ref.shape[0]
    rows = toks // len(outs)
    first = lax.axis_index(SEQ) * toks
    last = first + toks - 1
    here = lax.axis_index("head")
    for turn, out_ref in enumerate(outs):
        start = pl.multiple_of(lax.rem(here + TURNS[turn], len(outs)) * rows, rows)
        src = lax.broadcasted_iota(jnp.int32, (rows, dim), 0) + start
        inside = last < doc_limit(src + first, lengths_ref)
        span = (toks - 1 - src).astype(F32)
        for h in range(heads):
            cols = slice(h * dim, (h + 1) * dim)
            tail = jnp.where(inside, jnp.exp(-rate_ref[h] * span) * (1.0 / dim), 0.0)
            product = jnp.dot(
                key_ref[pl.ds(start, rows), cols], state_ref[h], preferred_element_type=F32
            )
            out_ref[:, cols] = (intra_ref[pl.ds(start, rows), cols] + product * tail).astype(
                BF16
            )


def across(rates, lengths, keys, states, intra):
    heads, dim = states.shape[:2]
    toks, width = keys.shape
    rows = toks // len(TURNS)
    return pl.pallas_call(
        across_body,
        grid=(1,),
        in_specs=[
            SCALARS,
            SCALARS,
            pl.BlockSpec((toks, width), lambda i: (0, 0)),
            pl.BlockSpec((heads, dim, dim), lambda i: (0, 0, 0)),
            pl.BlockSpec((toks, width), lambda i: (0, 0)),
        ],
        out_specs=[pl.BlockSpec((rows, width), lambda i: (0, 0))] * len(TURNS),
        out_shape=[jax.ShapeDtypeStruct((rows, width), BF16)] * len(TURNS),
        compiler_params=params(),
        name="across",
    )(rates, lengths, keys, states, intra)


def times(rows, weight):
    rows = jnp.concatenate([part[...] for part in rows], axis=0)
    return lax.dot_general(
        rows, weight[0], (((1,), (1,)), ((), ())), preferred_element_type=F32
    )


def project_body(turns, place, pick, *refs):
    out_ref = refs[-1]
    total = None
    for k in range(turns):
        part = times(refs[k * turns : (k + 1) * turns], refs[turns * turns + k])
        total = part if total is None else total + part
    out_ref[...] = jnp.dot(
        pick[...], total.astype(BF16), preferred_element_type=F32
    ).astype(BF16)


def project(place, pick, pieces, weight, tile):
    turns = len(pieces)
    rows, depth = pieces[0][0].shape
    slots, toks = pick.shape
    width = weight.shape[1]
    whole = pl.BlockSpec((rows, depth), lambda i, p: (0, 0))
    return pl.pallas_call(
        functools.partial(project_body, turns),
        grid_spec=pltpu.PrefetchScalarGridSpec(
            num_scalar_prefetch=1,
            grid=(width // tile,),
            in_specs=[pl.BlockSpec((slots, toks), lambda i, p: (0, 0))]
            + [whole] * (turns * turns)
            + [
                pl.BlockSpec((1, tile, depth), lambda i, p, k=k: (p[k], i, 0))
                for k in range(turns)
            ],
            out_specs=pl.BlockSpec((slots, tile), lambda i, p: (0, i)),
        ),
        out_shape=pltpu.HBM((slots, width), BF16),
        compiler_params=params(),
        name="project",
    )(place, pick, *[q for piece in pieces for q in piece], *[weight] * turns)


def merge_body(column_ref, row_ref, rows_ref, out_ref, same_ref):
    slots = column_ref.shape[0]
    count, width = rows_ref.shape[0], rows_ref.shape[-1]

    @pl.when(pl.program_id(0) == 0)
    def _():
        same = (column_ref[...] == row_ref[...]) & (column_ref[...] >= 0)
        same_ref[...] = same.astype(F32).astype(BF16)

    for j in range(count):
        rows = rows_ref[j].reshape(slots, width)
        total = jnp.dot(same_ref[...], rows, preferred_element_type=F32).astype(BF16)
        out_ref[0, :, :, j * width : (j + 1) * width] = total.reshape(out_ref.shape[1:3] + (width,))


def merge(column, row, got, count):
    parts, n_from, per, width = got.shape
    slots = n_from * per
    return pl.pallas_call(
        merge_body,
        grid=(parts // count,),
        in_specs=[
            pl.BlockSpec((slots, 1), lambda i: (0, 0)),
            pl.BlockSpec((1, slots), lambda i: (0, 0)),
            pl.BlockSpec((count, n_from, per, width), lambda i: (i, 0, 0, 0)),
        ],
        out_specs=pl.BlockSpec(
            (1, slots // CAPACITY, CAPACITY, count * width), lambda i: (0, 0, 0, i)
        ),
        out_shape=jax.ShapeDtypeStruct((1, slots // CAPACITY, CAPACITY, parts * width), BF16),
        scratch_shapes=[pltpu.VMEM((slots, slots), BF16)],
        compiler_params=params(),
        name="merge",
    )(column, row, got)


def slots_of(owners, block_ids):
    blocks, width = owners.shape
    same_owner = owners[:, :, None] == owners[:, None, :]
    lower = jnp.arange(width, dtype=jnp.int32)
    earlier = lower[None, :] < lower[:, None]
    rank = jnp.sum((same_owner & earlier[None]).astype(jnp.int32), axis=2)
    return ((owners * blocks + block_ids[:, None]) * CAPACITY + rank).reshape(blocks * width)


def shift(size, step):
    return [(i, (i + step) % size) for i in range(size)]


def per_device(
    queries,
    key_vectors,
    output_grad,
    value_weight,
    decay_rate,
    doc_lengths,
    owner_block,
    row_offset,
):
    n_z = lax.axis_size("z")
    n_seq = lax.axis_size(SEQ)
    n_head = lax.axis_size("head")
    devices_all = n_seq * n_head
    tok_rows = queries.shape[0]
    head_local = decay_rate.shape[0]
    head_dim = queries.shape[1] // head_local
    seq_rank = lax.axis_index(SEQ)
    head_rank = lax.axis_index("head")
    z_rank = lax.axis_index("z")
    plane = n_seq // n_z
    turns = jnp.array(TURNS, jnp.int32)

    weight = lax.all_gather(value_weight, ("head", "y", "core"), axis=0, tiled=True)
    weight = weight.reshape(n_head, -1, value_weight.shape[1])

    queries, key_vectors, output_grad, rates, lengths = (
        pltpu.with_memory_space_constraint(array, pltpu.HBM)
        for array in (queries, key_vectors, output_grad, decay_rate, doc_lengths)
    )
    state = local_states(rates, lengths, queries, output_grad, head_local // 2)
    blocks = tok_rows // ROWS_BLK
    per = blocks * CAPACITY
    owners = owner_block[:, 0].reshape(blocks, ROWS_BLK)
    slot_index = slots_of(owners, jnp.arange(blocks, dtype=jnp.int32))
    my_slots = (
        (jnp.arange(n_seq, dtype=jnp.int32)[:, None] * n_head + head_rank) * per
        + jnp.arange(per, dtype=jnp.int32)[None, :]
    )
    hit = my_slots[:, :, None] == slot_index[None, None, :]
    named = jnp.sum(jnp.where(hit, row_offset[None, None, :] + 1, 0), axis=2)
    note = jnp.concatenate([(named // 32).astype(BF16), (named % 32).astype(BF16)], axis=1)
    note = jnp.pad(note[:, None, :], ((0, 0), (0, 0), (0, head_dim - 2 * per)))
    names = lax.dynamic_slice_in_dim(owners, head_rank, 1, 0).astype(BF16)
    names = jnp.broadcast_to(names[None], (n_seq, 1, ROWS_BLK))
    note = jnp.pad(jnp.concatenate([note, names], axis=1), ((0, 0), (0, 6), (0, 0)))

    share = head_local * head_dim // n_seq
    state_in = lax.all_to_all(
        state.reshape(n_seq, share, head_dim), SEQ, split_axis=0, concat_axis=0, tiled=True
    )
    intra = within(
        rates, lengths, queries, key_vectors, output_grad, head_local // 2
    )

    doc_ends = jnp.cumsum(doc_lengths)
    ranks = jnp.arange(n_seq, dtype=jnp.int32)
    doc_last = doc_of((ranks + 1) * tok_rows - 1, doc_ends)
    doc_prior = doc_of(jnp.maximum(ranks * tok_rows - 1, 0), doc_ends)
    my_rate = decay_rate[seq_rank // (n_seq // head_local)]
    ahead = ranks[None, :] - ranks[:, None] - 1
    reach = (ahead >= 0) & (doc_last[:, None] == doc_prior[None, :])
    chain = jnp.where(
        reach, jnp.exp(-my_rate * (jnp.maximum(ahead, 0) * tok_rows).astype(F32)), 0.0
    )
    carried_all = jnp.einsum(
        "bc,cxy->bxy",
        chain,
        state_in.astype(F32),
        precision=lax.Precision.HIGHEST,
        preferred_element_type=F32,
    ).astype(BF16)
    carried = lax.all_to_all(
        jnp.concatenate([carried_all, note], axis=1),
        SEQ,
        split_axis=0,
        concat_axis=0,
        tiled=True,
    )
    offsets = (
        carried[:, share, :per].astype(jnp.int32) * 32
        + carried[:, share, per : 2 * per].astype(jnp.int32)
        - 1
    )
    column = offsets.reshape(-1, 1)
    row = offsets.reshape(n_z, plane, blocks, CAPACITY).transpose(1, 2, 0, 3).reshape(1, -1)
    near_z = (z_rank - jnp.array((0,) + ZTURNS, jnp.int32)) % n_z
    theirs = carried[:, share + 1].reshape(n_z, plane, ROWS_BLK)
    theirs = lax.dynamic_slice_in_dim(theirs, seq_rank % plane, 1, 1)[:, 0]
    theirs = theirs[near_z].astype(jnp.int32)
    their_slots = slots_of(theirs, near_z)
    all_slots = jnp.arange(devices_all * per, dtype=jnp.int32)
    pick = (all_slots[:, None] == their_slots[None, :]).astype(BF16)
    carried = carried[:, :share].reshape(head_local, head_dim, head_dim)

    own = across(rates, lengths, key_vectors, carried, intra)
    mine = [own[0]]
    for turn in range(1, len(TURNS)):
        mine.append(lax.ppermute(own[turn], "head", shift(n_head, TURNS[turn])))
    place = (head_rank - turns) % n_head

    def spread(rows, flip):
        below = lax.ppermute(rows, "z", shift(n_z, 1))
        above = lax.ppermute(rows, "z", shift(n_z, -1))
        relay = lax.ppermute(above if flip else below, "z", shift(n_z, -1 if flip else 1))
        return rows, below, above, relay

    groups = [spread(mine[0], False)]
    mine[1], mine[2], *_ = lax.optimization_barrier((mine[1], mine[2]) + groups[0][1:3])
    groups.append(spread(mine[1], False))
    groups.append(spread(mine[2], False))
    mine[3], *_ = lax.optimization_barrier((mine[3], groups[0][3]))
    groups.append(spread(mine[3], True))
    pieces = [
        [
            pltpu.with_memory_space_constraint(q, pltpu.VMEM if turn < 2 else pltpu.HBM)
            for q in group
        ]
        for turn, group in enumerate(groups)
    ]

    send = project(place, pick, pieces, weight, 512)
    send = send.reshape(devices_all, per, -1)
    got = lax.all_to_all(send, ALL, split_axis=0, concat_axis=0, tiled=True)
    got = got.reshape(n_z, plane * n_head, per, -1)
    return merge(column, row, got, 2)


def solution(mesh):
    planes = mesh.shape["head"]
    devices = mesh.devices.reshape(planes, -1, 2, planes)
    return jax.shard_map(
        per_device,
        mesh=Mesh(devices, ALL),
        in_specs=(
            P(SEQ, "head"),
            P(SEQ, "head"),
            P(SEQ, "head"),
            P(SEQ, "head"),
            P("head"),
            P(),
            P(SEQ, None),
            P(SEQ),
        ),
        out_specs=P(ALL, None, None, None),
        check_vma=False,
    )
```

```python
import functools

import jax
import jax.numpy as jnp
from jax import lax
from jax.experimental import pallas as pl
from jax.experimental.pallas import tpu as pltpu
from jax.sharding import Mesh, PartitionSpec as P

BF16 = jnp.bfloat16
F32 = jnp.float32
CAPACITY = 2
ROWS_BLK = 128
BIG = 1 << 30
SEQ = ("z", "y", "core")
ALL = ("z", "y", "core", "head")
TURNS = (0, 3, 1, 2)
ZTURNS = (1, 3, 2)


def doc_of(positions, doc_ends):
    return jnp.sum((positions[:, None] >= doc_ends[None, :]).astype(jnp.int32), axis=1)


def doc_limit(positions, lengths_ref):
    end = lengths_ref[0]
    limit = jnp.where(positions < end, end, BIG)
    for doc in range(1, lengths_ref.shape[0]):
        end = end + lengths_ref[doc]
        limit = jnp.minimum(limit, jnp.where(positions < end, end, BIG))
    return limit


def params(mib=48):
    return pltpu.CompilerParams(
        dimension_semantics=("arbitrary",), vmem_limit_bytes=mib << 20
    )


SCALARS = pl.BlockSpec(memory_space=pltpu.SMEM)


def local_state_body(rate_ref, lengths_ref, query_ref, grad_ref, out_ref):
    count, dim = out_ref.shape[:2]
    toks = query_ref.shape[0]
    first = lax.axis_index(SEQ) * toks
    limit = doc_limit(jnp.maximum(first - 1, 0), lengths_ref)
    step = lax.broadcasted_iota(jnp.int32, (toks, dim), 0)
    inside = first + step < limit
    span = (step + 1).astype(F32)
    for h in range(count):
        rate = rate_ref[pl.program_id(0) * count + h]
        cols = slice(h * dim, (h + 1) * dim)
        lead = jnp.where(inside, jnp.exp(-rate * span), 0.0)
        scaled = (query_ref[:, cols].astype(F32) * lead).astype(BF16)
        out_ref[h] = lax.dot_general(
            scaled, grad_ref[:, cols], (((0,), (0,)), ((), ())), preferred_element_type=F32
        ).astype(out_ref.dtype)


def local_states(rates, lengths, queries, grads, count):
    heads = rates.shape[0]
    toks, dim = queries.shape[0], queries.shape[1] // heads
    blk = pl.BlockSpec((toks, count * dim), lambda h: (0, h))
    return pl.pallas_call(
        local_state_body,
        grid=(heads // count,),
        in_specs=[SCALARS, SCALARS, blk, blk],
        out_specs=pl.BlockSpec((count, dim, dim), lambda h: (h, 0, 0)),
        out_shape=jax.ShapeDtypeStruct((heads, dim, dim), BF16),
        compiler_params=params(),
        name="local_states",
    )(rates, lengths, queries, grads)


def within_body(count, rate_ref, lengths_ref, query_ref, key_ref, grad_ref, out_ref):
    toks = query_ref.shape[0]
    dim = query_ref.shape[1] // count
    first = lax.axis_index(SEQ) * toks
    half = toks // 2
    for lo in (0, half):
        src = lax.broadcasted_iota(jnp.int32, (half, 1), 0) + lo
        dst = lax.broadcasted_iota(jnp.int32, (1, toks - lo), 1) + lo
        limit = doc_limit(src + first, lengths_ref) - first
        seen = (dst >= src) & (dst < limit)
        for h in range(count):
            rate = rate_ref[pl.program_id(0) * count + h]
            cols = slice(h * dim, (h + 1) * dim)
            rise = jnp.exp(rate * src.astype(F32)) * (1.0 / dim)
            fall = jnp.exp(-rate * dst.astype(F32))
            scores = lax.dot_general(
                key_ref[lo : lo + half, cols],
                query_ref[lo:, cols],
                (((1,), (1,)), ((), ())),
                preferred_element_type=F32,
            )
            weights = jnp.where(seen, scores * rise * fall, 0.0).astype(BF16)
            out_ref[lo : lo + half, cols] = jnp.dot(
                weights, grad_ref[lo:, cols], preferred_element_type=F32
            )


def within(rates, lengths, queries, keys, grads, count):
    heads = rates.shape[0]
    toks, dim = queries.shape[0], queries.shape[1] // heads
    blk = pl.BlockSpec((toks, count * dim), lambda h: (0, h))
    return pl.pallas_call(
        functools.partial(within_body, count),
        grid=(heads // count,),
        in_specs=[SCALARS, SCALARS, blk, blk, blk],
        out_specs=blk,
        out_shape=jax.ShapeDtypeStruct((toks, heads * dim), F32),
        compiler_params=params(),
        name="within",
    )(rates, lengths, queries, keys, grads)


def across_body(rate_ref, lengths_ref, key_ref, state_ref, intra_ref, *outs):
    heads, dim = state_ref.shape[:2]
    toks = key_ref.shape[0]
    rows = toks // len(outs)
    first = lax.axis_index(SEQ) * toks
    last = first + toks - 1
    here = lax.axis_index("head")
    for turn, out_ref in enumerate(outs):
        start = pl.multiple_of(lax.rem(here + TURNS[turn], len(outs)) * rows, rows)
        src = lax.broadcasted_iota(jnp.int32, (rows, dim), 0) + start
        inside = last < doc_limit(src + first, lengths_ref)
        span = (toks - 1 - src).astype(F32)
        for h in range(heads):
            cols = slice(h * dim, (h + 1) * dim)
            tail = jnp.where(inside, jnp.exp(-rate_ref[h] * span) * (1.0 / dim), 0.0)
            product = jnp.dot(
                key_ref[pl.ds(start, rows), cols], state_ref[h], preferred_element_type=F32
            )
            out_ref[:, cols] = (intra_ref[pl.ds(start, rows), cols] + product * tail).astype(
                BF16
            )


def across(rates, lengths, keys, states, intra):
    heads, dim = states.shape[:2]
    toks, width = keys.shape
    rows = toks // len(TURNS)
    return pl.pallas_call(
        across_body,
        grid=(1,),
        in_specs=[
            SCALARS,
            SCALARS,
            pl.BlockSpec((toks, width), lambda i: (0, 0)),
            pl.BlockSpec((heads, dim, dim), lambda i: (0, 0, 0)),
            pl.BlockSpec((toks, width), lambda i: (0, 0)),
        ],
        out_specs=[pl.BlockSpec((rows, width), lambda i: (0, 0))] * len(TURNS),
        out_shape=[jax.ShapeDtypeStruct((rows, width), BF16)] * len(TURNS),
        compiler_params=params(),
        name="across",
    )(rates, lengths, keys, states, intra)


def times(rows, weight):
    rows = jnp.concatenate([part[...] for part in rows], axis=0)
    return lax.dot_general(
        rows, weight[0], (((1,), (1,)), ((), ())), preferred_element_type=F32
    )


def project_body(turns, place, pick, *refs):
    out_ref = refs[-1]
    total = None
    for k in range(turns):
        part = times(refs[k * turns : (k + 1) * turns], refs[turns * turns + k])
        total = part if total is None else total + part
    out_ref[...] = jnp.dot(
        pick[...], total.astype(BF16), preferred_element_type=F32
    ).astype(BF16)


def project(place, pick, pieces, weight, tile):
    turns = len(pieces)
    rows, depth = pieces[0][0].shape
    slots, toks = pick.shape
    width = weight.shape[1]
    whole = pl.BlockSpec((rows, depth), lambda i, p: (0, 0))
    return pl.pallas_call(
        functools.partial(project_body, turns),
        grid_spec=pltpu.PrefetchScalarGridSpec(
            num_scalar_prefetch=1,
            grid=(width // tile,),
            in_specs=[pl.BlockSpec((slots, toks), lambda i, p: (0, 0))]
            + [whole] * (turns * turns)
            + [
                pl.BlockSpec((1, tile, depth), lambda i, p, k=k: (p[k], i, 0))
                for k in range(turns)
            ],
            out_specs=pl.BlockSpec((slots, tile), lambda i, p: (0, i)),
        ),
        out_shape=pltpu.HBM((slots, width), BF16),
        compiler_params=params(),
        name="project",
    )(place, pick, *[q for piece in pieces for q in piece], *[weight] * turns)


def merge_body(column_ref, row_ref, rows_ref, out_ref, same_ref):
    slots = column_ref.shape[0]
    count, width = rows_ref.shape[0], rows_ref.shape[-1]

    @pl.when(pl.program_id(0) == 0)
    def _():
        same = (column_ref[...] == row_ref[...]) & (column_ref[...] >= 0)
        same_ref[...] = same.astype(F32).astype(BF16)

    for j in range(count):
        rows = rows_ref[j].reshape(slots, width)
        total = jnp.dot(same_ref[...], rows, preferred_element_type=F32).astype(BF16)
        out_ref[0, :, :, j * width : (j + 1) * width] = total.reshape(out_ref.shape[1:3] + (width,))


def merge(column, row, got, count):
    parts, n_from, per, width = got.shape
    slots = n_from * per
    return pl.pallas_call(
        merge_body,
        grid=(parts // count,),
        in_specs=[
            pl.BlockSpec((slots, 1), lambda i: (0, 0)),
            pl.BlockSpec((1, slots), lambda i: (0, 0)),
            pl.BlockSpec((count, n_from, per, width), lambda i: (i, 0, 0, 0)),
        ],
        out_specs=pl.BlockSpec(
            (1, slots // CAPACITY, CAPACITY, count * width), lambda i: (0, 0, 0, i)
        ),
        out_shape=jax.ShapeDtypeStruct((1, slots // CAPACITY, CAPACITY, parts * width), BF16),
        scratch_shapes=[pltpu.VMEM((slots, slots), BF16)],
        compiler_params=params(),
        name="merge",
    )(column, row, got)


def slots_of(owners, block_ids):
    blocks, width = owners.shape
    same_owner = owners[:, :, None] == owners[:, None, :]
    lower = jnp.arange(width, dtype=jnp.int32)
    earlier = lower[None, :] < lower[:, None]
    rank = jnp.sum((same_owner & earlier[None]).astype(jnp.int32), axis=2)
    return ((owners * blocks + block_ids[:, None]) * CAPACITY + rank).reshape(blocks * width)


def shift(size, step):
    return [(i, (i + step) % size) for i in range(size)]


def per_device(
    queries,
    key_vectors,
    output_grad,
    value_weight,
    decay_rate,
    doc_lengths,
    owner_block,
    row_offset,
):
    n_z = lax.axis_size("z")
    n_seq = lax.axis_size(SEQ)
    n_head = lax.axis_size("head")
    devices_all = n_seq * n_head
    tok_rows = queries.shape[0]
    head_local = decay_rate.shape[0]
    head_dim = queries.shape[1] // head_local
    seq_rank = lax.axis_index(SEQ)
    head_rank = lax.axis_index("head")
    z_rank = lax.axis_index("z")
    plane = n_seq // n_z
    turns = jnp.array(TURNS, jnp.int32)

    weight = lax.all_gather(value_weight, ("head", "y", "core"), axis=0, tiled=True)
    weight = weight.reshape(n_head, -1, value_weight.shape[1])

    queries, key_vectors, output_grad, rates, lengths = (
        pltpu.with_memory_space_constraint(array, pltpu.HBM)
        for array in (queries, key_vectors, output_grad, decay_rate, doc_lengths)
    )
    state = local_states(rates, lengths, queries, output_grad, head_local // 4)
    blocks = tok_rows // ROWS_BLK
    per = blocks * CAPACITY
    owners = owner_block[:, 0].reshape(blocks, ROWS_BLK)
    slot_index = slots_of(owners, jnp.arange(blocks, dtype=jnp.int32))
    my_slots = (
        (jnp.arange(n_seq, dtype=jnp.int32)[:, None] * n_head + head_rank) * per
        + jnp.arange(per, dtype=jnp.int32)[None, :]
    )
    hit = my_slots[:, :, None] == slot_index[None, None, :]
    named = jnp.sum(jnp.where(hit, row_offset[None, None, :] + 1, 0), axis=2)
    note = jnp.concatenate([(named // 32).astype(BF16), (named % 32).astype(BF16)], axis=1)
    note = jnp.pad(note[:, None, :], ((0, 0), (0, 0), (0, head_dim - 2 * per)))
    names = lax.dynamic_slice_in_dim(owners, head_rank, 1, 0).astype(BF16)
    names = jnp.broadcast_to(names[None], (n_seq, 1, ROWS_BLK))
    note = jnp.pad(jnp.concatenate([note, names], axis=1), ((0, 0), (0, 6), (0, 0)))

    share = head_local * head_dim // n_seq
    state_in = lax.all_to_all(
        state.reshape(n_seq, share, head_dim), SEQ, split_axis=0, concat_axis=0, tiled=True
    )
    intra = within(
        rates, lengths, queries, key_vectors, output_grad, head_local // 2
    )

    doc_ends = jnp.cumsum(doc_lengths)
    ranks = jnp.arange(n_seq, dtype=jnp.int32)
    doc_last = doc_of((ranks + 1) * tok_rows - 1, doc_ends)
    doc_prior = doc_of(jnp.maximum(ranks * tok_rows - 1, 0), doc_ends)
    my_rate = decay_rate[seq_rank // (n_seq // head_local)]
    ahead = ranks[None, :] - ranks[:, None] - 1
    reach = (ahead >= 0) & (doc_last[:, None] == doc_prior[None, :])
    chain = jnp.where(
        reach, jnp.exp(-my_rate * (jnp.maximum(ahead, 0) * tok_rows).astype(F32)), 0.0
    )
    carried_all = jnp.einsum(
        "bc,cxy->bxy",
        chain,
        state_in.astype(F32),
        precision=lax.Precision.HIGHEST,
        preferred_element_type=F32,
    ).astype(BF16)
    carried = lax.all_to_all(
        jnp.concatenate([carried_all, note], axis=1),
        SEQ,
        split_axis=0,
        concat_axis=0,
        tiled=True,
    )
    offsets = (
        carried[:, share, :per].astype(jnp.int32) * 32
        + carried[:, share, per : 2 * per].astype(jnp.int32)
        - 1
    )
    column = offsets.reshape(-1, 1)
    row = offsets.reshape(n_z, plane, blocks, CAPACITY).transpose(1, 2, 0, 3).reshape(1, -1)
    near_z = (z_rank - jnp.array((0,) + ZTURNS, jnp.int32)) % n_z
    theirs = carried[:, share + 1].reshape(n_z, plane, ROWS_BLK)
    theirs = lax.dynamic_slice_in_dim(theirs, seq_rank % plane, 1, 1)[:, 0]
    theirs = theirs[near_z].astype(jnp.int32)
    their_slots = slots_of(theirs, near_z)
    all_slots = jnp.arange(devices_all * per, dtype=jnp.int32)
    pick = (all_slots[:, None] == their_slots[None, :]).astype(BF16)
    carried = carried[:, :share].reshape(head_local, head_dim, head_dim)

    own = across(rates, lengths, key_vectors, carried, intra)
    mine = [own[0]]
    for turn in range(1, len(TURNS)):
        mine.append(lax.ppermute(own[turn], "head", shift(n_head, TURNS[turn])))
    place = (head_rank - turns) % n_head

    def spread(rows, flip):
        below = lax.ppermute(rows, "z", shift(n_z, 1))
        above = lax.ppermute(rows, "z", shift(n_z, -1))
        relay = lax.ppermute(above if flip else below, "z", shift(n_z, -1 if flip else 1))
        return rows, below, above, relay

    groups = [spread(mine[0], False)]
    mine[1], mine[2], *_ = lax.optimization_barrier((mine[1], mine[2]) + groups[0][1:3])
    groups.append(spread(mine[1], False))
    groups.append(spread(mine[2], False))
    mine[3], *_ = lax.optimization_barrier((mine[3], groups[0][3]))
    groups.append(spread(mine[3], True))
    pieces = [
        [
            pltpu.with_memory_space_constraint(q, pltpu.VMEM if turn < 2 else pltpu.HBM)
            for q in group
        ]
        for turn, group in enumerate(groups)
    ]

    send = project(place, pick, pieces, weight, 512)
    send = send.reshape(devices_all, per, -1)
    got = lax.all_to_all(send, ALL, split_axis=0, concat_axis=0, tiled=True)
    got = got.reshape(n_z, plane * n_head, per, -1)
    return merge(column, row, got, 2)


def solution(mesh):
    planes = mesh.shape["head"]
    devices = mesh.devices.reshape(planes, -1, 2, planes)
    return jax.shard_map(
        per_device,
        mesh=Mesh(devices, ALL),
        in_specs=(
            P(SEQ, "head"),
            P(SEQ, "head"),
            P(SEQ, "head"),
            P(SEQ, "head"),
            P("head"),
            P(),
            P(SEQ, None),
            P(SEQ),
        ),
        out_specs=P(ALL, None, None, None),
        check_vma=False,
    )
```
